32 devices in a mesh: fsdp: 4 (over x, core), seq: 8 (over z, y).
Axes of the slice: x: 2, y: 2, z: 4, core: 2. Of those that a mesh axis runs over, the one named last changes fastest.
Arguments:
- tokens: bfloat16 [8, 2048, 1024], P('fsdp', 'seq'), may hold values from -6 to 6
- cotangent: bfloat16 [8, 2048, 1024], P('fsdp', 'seq'), may hold values from -6 to 6
- w_query: bfloat16 [1024, 1024], P(('fsdp', 'seq')), may hold values from -0.25 to 0.25
- w_key: bfloat16 [1024, 1024], P(('fsdp', 'seq')), may hold values from -0.25 to 0.25
- w_value: bfloat16 [1024, 1024], P(('fsdp', 'seq')), may hold values from -0.1875 to 0.1875
- w_output: bfloat16 [1024, 1024], P(('fsdp', 'seq')), may hold values from -0.1875 to 0.1875
- w_up: bfloat16 [1024, 4096], P(('fsdp', 'seq')), may hold values from -0.1875 to 0.1875
- w_down: bfloat16 [4096, 1024], P(('fsdp', 'seq')), may hold values from -0.09375 to 0.09375
- attn_in_gain: bfloat16 [1024], P(('fsdp', 'seq')), may hold values from 0.5 to 1.5
- attn_in_bias: bfloat16 [1024], P(('fsdp', 'seq')), may hold values from -2 to 2
- attn_out_gain: bfloat16 [1024], P(('fsdp', 'seq')), may hold values from 0.5 to 1.5
- attn_out_bias: bfloat16 [1024], P(('fsdp', 'seq')), may hold values from -2 to 2
- mlp_in_gain: bfloat16 [1024], P(('fsdp', 'seq')), may hold values from 0.5 to 1.5
- mlp_in_bias: bfloat16 [1024], P(('fsdp', 'seq')), may hold values from -2 to 2
- mlp_out_gain: bfloat16 [1024], P(('fsdp', 'seq')), may hold values from 0.5 to 1.5
- mlp_out_bias: bfloat16 [1024], P(('fsdp', 'seq')), may hold values from -2 to 2
Outputs:
- block_out: bfloat16 [8, 2048, 1024], P('fsdp', 'seq')
- grad_tokens: bfloat16 [8, 2048, 1024], P('fsdp', 'seq')
- grad_query: float32 [1024, 1024], P(('fsdp', 'seq'))
- grad_key: float32 [1024, 1024], P(('fsdp', 'seq'))
- grad_value: float32 [1024, 1024], P(('fsdp', 'seq'))
- grad_output: float32 [1024, 1024], P(('fsdp', 'seq'))
- grad_up: float32 [1024, 4096], P(('fsdp', 'seq'))
- grad_down: float32 [4096, 1024], P(('fsdp', 'seq'))
- grad_attn_in_gain: float32 [1024], P(('fsdp', 'seq'))
- grad_attn_in_bias: float32 [1024], P(('fsdp', 'seq'))
- grad_attn_out_gain: float32 [1024], P(('fsdp', 'seq'))
- grad_attn_out_bias: float32 [1024], P(('fsdp', 'seq'))
- grad_mlp_in_gain: float32 [1024], P(('fsdp', 'seq'))
- grad_mlp_in_bias: float32 [1024], P(('fsdp', 'seq'))
- grad_mlp_out_gain: float32 [1024], P(('fsdp', 'seq'))
- grad_mlp_out_bias: float32 [1024], P(('fsdp', 'seq'))
The draws below stay inside these ranges and needn't reach their ends.
All inputs are finite; a program needn't handle non-finite values.
Results may differ from the reference program's by a relative error of at most 0.015.
Values may be sent and summed in bfloat16 or wider, within the bound.
No kernel may reach another device: no remote copies, remote signals or barrier semaphores. Data moves between devices by JAX's collectives and lax.ppermute only.
A program may use at most 192 MiB of HBM per device.

```python
import math
import jax
import jax.numpy as jnp
from jax import lax

D = 1024
FF = 4096
HEADS = 16
HEAD_DIM = 64
LEN = 2048
SEQUENCES = 8


def level_of(rng, extent, pieces, low, top_value):
    level, own = 1.0, jax.random.fold_in(rng, 6)
    for position, blocks in pieces:
        draws = jnp.exp(jax.random.uniform(jax.random.fold_in(own, position), (blocks,), jnp.float32, low / len(pieces), top_value / len(pieces)))
        level = level * jnp.repeat(draws, extent[position] // blocks).reshape([-1 if axis == position else 1 for axis in range(len(extent))])
    return level


def noise(stream_key, extent, scale, bound, pieces=(), kind=jnp.bfloat16):
    values = scale * jax.random.normal(stream_key, extent, jnp.float32)
    if pieces:
        values = values * level_of(stream_key, extent, pieces, -0.22, 0.18)
    return jnp.clip(values, -bound, bound).astype(kind)


def setup_inputs(seed: int = 0) -> dict:
    splits = jax.random.split(jax.random.key(seed), 17)
    return {
        "tokens": noise(splits[0], (SEQUENCES, LEN, D), 1.0, 6.0, ((0, 4), (1, 8))),
        "cotangent": noise(splits[1], (SEQUENCES, LEN, D), 1.0, 6.0, ((0, 4), (1, 8))),
        "w_query": noise(splits[2], (D, D), (D // 2) ** -0.5, 0.25, ((0, 32),)),
        "w_key": noise(splits[3], (D, D), (D // 2) ** -0.5, 0.25, ((0, 32),)),
        "w_value": noise(splits[4], (D, D), D ** -0.5, 0.1875, ((0, 32),)),
        "w_output": noise(splits[5], (D, D), D ** -0.5, 0.1875, ((0, 32),)),
        "w_up": noise(splits[6], (D, FF), D ** -0.5, 0.1875, ((0, 32),)),
        "w_down": noise(splits[7], (FF, D), FF ** -0.5, 0.09375, ((0, 32),)),
        "attn_in_gain": jnp.clip(1.0 + 0.1 * jax.random.normal(splits[8], (D,), jnp.float32), 0.5, 1.5).astype(jnp.bfloat16),
        "attn_in_bias": noise(splits[9], (D,), 0.3, 2.0, ((0, 32),)),
        "attn_out_gain": jnp.clip(1.0 + 0.1 * jax.random.normal(splits[10], (D,), jnp.float32), 0.5, 1.5).astype(jnp.bfloat16),
        "attn_out_bias": noise(splits[11], (D,), 0.3, 2.0, ((0, 32),)),
        "mlp_in_gain": jnp.clip(1.0 + 0.1 * jax.random.normal(splits[12], (D,), jnp.float32), 0.5, 1.5).astype(jnp.bfloat16),
        "mlp_in_bias": noise(splits[13], (D,), 0.3, 2.0, ((0, 32),)),
        "mlp_out_gain": jnp.clip(1.0 + 0.1 * jax.random.normal(splits[14], (D,), jnp.float32), 0.5, 1.5).astype(jnp.bfloat16),
        "mlp_out_bias": noise(splits[15], (D,), 0.3, 2.0, ((0, 32),)),
    }


EPSILON = 1e-05
NEGATIVE = -1e+30
HIGHEST = lax.Precision.HIGHEST

@jax.custom_vjp
def low(v):
    return lax.optimization_barrier(v.astype(jnp.bfloat16)).astype(jnp.float32)

@jax.custom_vjp
def low_back(v):
    return v

def low_keep(v):
    return (low(v), None)

def low_pass(kept, grad):
    return (grad,)

def back_keep(v):
    return (v, None)

def back_low(kept, grad):
    return (low(grad),)
low.defvjp(low_keep, low_pass)
low_back.defvjp(back_keep, back_low)

def layer_norm(values, gain_vec, shift_vec):
    center = values - lax.optimization_barrier(jnp.mean(values, axis=-1, keepdims=True))
    spread = lax.optimization_barrier(jnp.mean(center * center, axis=-1, keepdims=True))
    return center * lax.rsqrt(spread + EPSILON) * gain_vec + shift_vec

def rotary_tables(positions, head_size):
    frequency = jnp.exp(jnp.arange(head_size // 2, dtype=jnp.float32) * (-2.0 * math.log(10000.0) / head_size))
    angles = positions.astype(jnp.float32)[:, None] * frequency[None, :]
    return (jnp.cos(angles)[:, None, :], jnp.sin(angles)[:, None, :])

def rotary(tensor, cosine, sine_tab):
    middle = tensor.shape[-1] // 2
    leading = tensor[..., :middle]
    trailing = tensor[..., middle:]
    return jnp.concatenate([leading * cosine - trailing * sine_tab, trailing * cosine + leading * sine_tab], axis=-1)

def forward(inputs, w_query, w_key, w_value, w_output, w_up, w_down, gain_ai, bias_ai, gain_ao, bias_ao, gain_mi, bias_mi, gain_mo, bias_mo):
    normed = low(layer_norm(inputs, gain_ai, bias_ai))
    cosine, sine_tab = rotary_tables(jnp.arange(LEN, dtype=jnp.int32), HEAD_DIM)

    def project(weight):
        return low_back(jnp.dot(normed, weight, precision=HIGHEST)).reshape(LEN, HEADS, HEAD_DIM)
    queries = low(rotary(project(w_query), cosine, sine_tab))
    key_rows = low(rotary(project(w_key), cosine, sine_tab))
    value_rows = low(project(w_value))
    span_rows = min(512, LEN)
    key_pos = jnp.arange(LEN, dtype=jnp.int32)
    factor = HEAD_DIM ** (-0.5)

    def attend(block_id):
        offset = block_id * span_rows
        q_blk = lax.dynamic_slice_in_dim(queries, offset, span_rows, 0)
        scores = low_back(jnp.einsum('qhd,khd->hqk', q_blk, key_rows, precision=HIGHEST)) * factor
        allowed = key_pos[None, :] <= (offset + jnp.arange(span_rows, dtype=jnp.int32))[:, None]
        scores = jnp.where(allowed[None], scores, NEGATIVE)
        maxima = lax.optimization_barrier(jnp.max(scores, axis=-1, keepdims=True))
        exponent = jnp.exp(scores - maxima)
        attn_prob = low(exponent / lax.optimization_barrier(jnp.sum(exponent, axis=-1, keepdims=True)))
        return jnp.einsum('hqk,khd->qhd', attn_prob, value_rows, precision=HIGHEST)
    attended = lax.map(jax.checkpoint(attend), jnp.arange(LEN // span_rows, dtype=jnp.int32))
    attended = low(low_back(attended.reshape(LEN, D)))
    projected = low_back(jnp.dot(attended, w_output, precision=HIGHEST))
    residual = inputs + layer_norm(projected, gain_ao, bias_ao)
    mlp_normed = low(layer_norm(residual, gain_mi, bias_mi))
    pre_act = low_back(jnp.dot(mlp_normed, w_up, precision=HIGHEST))
    activated = low(jax.nn.gelu(pre_act))
    branch = low_back(jnp.dot(activated, w_down, precision=HIGHEST))
    return residual + layer_norm(branch, gain_mo, bias_mo)

def reference(tokens, cotangent, w_query, w_key, w_value, w_output, w_up, w_down, attn_in_gain, attn_in_bias, attn_out_gain, attn_out_bias, mlp_in_gain, mlp_in_bias, mlp_out_gain, mlp_out_bias):
    parameters = tuple((weight.astype(jnp.float32) for weight in (w_query, w_key, w_value, w_output, w_up, w_down, attn_in_gain, attn_in_bias, attn_out_gain, attn_out_bias, mlp_in_gain, mlp_in_bias, mlp_out_gain, mlp_out_bias)))

    def one_sequence(running, pair_in):
        seq_in, seq_cot = pair_in
        result, backward = jax.vjp(forward, seq_in.astype(jnp.float32), *parameters)
        gradients = backward(seq_cot.astype(jnp.float32))
        running = tuple((summed + added for summed, added in zip(running, gradients[1:])))
        return (running, (result.astype(jnp.bfloat16), gradients[0].astype(jnp.bfloat16)))
    zero_sums = tuple((jnp.zeros(weight.shape, jnp.float32) for weight in parameters))
    totals, (outputs, grad_x) = lax.scan(one_sequence, zero_sums, (tokens, cotangent))
    return (outputs, grad_x, totals[0], totals[1], totals[2], totals[3], totals[4], totals[5], totals[6], totals[7], totals[8], totals[9], totals[10], totals[11], totals[12], totals[13])
```

```python
import functools
import math

import jax
import jax.numpy as jnp
from jax import lax
from jax.experimental import pallas as pl
from jax.experimental.pallas import tpu as pltpu
from jax.sharding import Mesh
from jax.sharding import PartitionSpec as P

HEADS = 16
HEAD_DIM = 64
EPSILON = 1e-05
NEGATIVE = -1e30
LOG2E = math.log2(math.e)
AXES = ("j", "h", "c", "a", "b")
BF = jnp.bfloat16
F32 = jnp.float32
NT = (((1,), (1,)), ((), ()))
NN = (((1,), (0,)), ((), ()))
TN = (((0,), (0,)), ((), ()))


def cost(us):
    return pl.CostEstimate(flops=int(us * 1e6), bytes_accessed=1 << 10, transcendentals=0)


def dot(left, right, dims=NN):
    return lax.dot_general(left, right, dims, preferred_element_type=F32)


def qkv_kernel(table, *refs, pieces):
    x_refs = refs[:pieces]
    w_ref, vec_ref, cos_ref, sin_ref, n_ref, q_ref, k_ref, v_ref, held = refs[pieces:]
    step = pl.program_id(0)
    for n in range(pieces):

        @pl.when(step == n)
        def _(n=n):
            held[...] = x_refs[n][...]

    x = held[...].astype(F32)
    center = x - jnp.mean(x, axis=1, keepdims=True)
    rstd = lax.rsqrt(jnp.mean(center * center, axis=1, keepdims=True) + EPSILON)
    normed = (center * rstd * vec_ref[0:1] + vec_ref[1:2]).astype(BF)
    n_ref[...] = normed
    full = dot(normed, w_ref[...])
    lane = lax.broadcasted_iota(jnp.int32, (1, 128), 1)
    first = (lane % HEAD_DIM) < HEAD_DIM // 2
    cosine, sine = cos_ref[...], sin_ref[...]
    for pair in range(q_ref.shape[1] // 128):
        at = slice(pair * 128, (pair + 1) * 128)
        for which, out, scale in ((0, q_ref, LOG2E * HEAD_DIM**-0.5), (1, k_ref, 1.0)):
            t = full[:, (3 * pair + which) * 128 : (3 * pair + which + 1) * 128]
            other = jnp.where(first, pltpu.roll(t, 96, 1), pltpu.roll(t, 32, 1))
            out[:, at] = ((t * cosine + other * sine) * scale).astype(BF)
        v_ref[:, at] = full[:, (3 * pair + 2) * 128 : (3 * pair + 3) * 128].astype(BF)


def qkv_call(table, pieces, w, vec, cosine, sine):
    blocks = len(pieces)
    rows, model = pieces[0].shape
    width = w.shape[1] // 3
    length = blocks * rows
    at = lambda i, t: (t[i], 0)
    fixed = lambda i, t: (0, 0)
    return pl.pallas_call(
        functools.partial(qkv_kernel, pieces=blocks),
        out_shape=[jax.ShapeDtypeStruct((length, model), BF)]
        + [jax.ShapeDtypeStruct((length, width), BF)] * 3,
        grid_spec=pltpu.PrefetchScalarGridSpec(
            num_scalar_prefetch=1,
            grid=(blocks,),
            in_specs=[pl.BlockSpec((rows, model), fixed)] * blocks
            + [
                pl.BlockSpec(w.shape, fixed),
                pl.BlockSpec(vec.shape, fixed),
                pl.BlockSpec((rows, 128), at),
                pl.BlockSpec((rows, 128), at),
            ],
            out_specs=[pl.BlockSpec((rows, model), at)] + [pl.BlockSpec((rows, width), at)] * 3,
            scratch_shapes=[pltpu.VMEM((rows, model), BF)],
        ),
        compiler_params=pltpu.CompilerParams(
            dimension_semantics=("arbitrary",), vmem_limit_bytes=48 << 20
        ),
        cost_estimate=cost(11),
        name="qkv",
    )(table, *pieces, w, vec, cosine, sine)


def forward_kernel(table, q_ref, k_ref, v_ref, o_ref, lse_ref, vaug, *, bq, bk, rows):
    i = pl.program_id(1)
    lane = lax.broadcasted_iota(jnp.int32, (1, 128), 1)
    low = lane < HEAD_DIM

    @pl.when(i == 0)
    def _():
        v = v_ref[...]
        one = jnp.ones_like(v)
        vaug[0] = jnp.where(low, v, one)
        vaug[1] = jnp.where(low, one, v)

    q = q_ref[...]
    zero = jnp.zeros_like(q)
    heads = (jnp.where(low, q, zero), jnp.where(low, zero, q))

    def step(kb, carry, masked):
        start = pl.multiple_of(kb * bk, bk)
        k_blk = k_ref[pl.ds(start, bk), :]
        out = []
        for h in range(2):
            top, acc = carry[h]
            s = dot(heads[h], k_blk, NT)
            if masked:
                row = lax.broadcasted_iota(jnp.int32, s.shape, 0) + i * bq
                col = lax.broadcasted_iota(jnp.int32, s.shape, 1) + start
                s = jnp.where(col <= row, s, NEGATIVE)
            new = jnp.maximum(top, jnp.max(s, axis=1, keepdims=True))
            p = jnp.exp2(s - new)
            acc = acc * jnp.exp2(top - new) + dot(p.astype(BF), vaug[h, pl.ds(start, bk), :])
            out.append((new, acc))
        return tuple(out)

    init = tuple(
        (jnp.full((bq, 1), NEGATIVE, F32), jnp.zeros((bq, 128), F32)) for _ in range(2)
    )
    full = (i * bq) // bk
    carry = lax.fori_loop(0, full, lambda kb, c: step(kb, c, False), init)
    for d in range(bq // bk):
        carry = step(full + d, carry, True)
    (top0, acc0), (top1, acc1) = carry
    total = pltpu.roll(jnp.where(low, acc1, acc0), HEAD_DIM, 1)
    o = (jnp.where(low, acc0, acc1) / total).astype(BF)
    for d in range(bq // rows):
        o_ref[table[i * (bq // rows) + d]] = o[d * rows : (d + 1) * rows]
    lse_ref[...] = jnp.where(low, top0, top1) + jnp.log2(total)


def attention_forward(table, q, k, v, rows):
    length, width = q.shape
    bq, bk = min(1024, length), min(512, length)
    blocks = length // rows
    return pl.pallas_call(
        functools.partial(forward_kernel, bq=bq, bk=bk, rows=rows),
        out_shape=[
            jax.ShapeDtypeStruct((blocks, rows, width), BF),
            jax.ShapeDtypeStruct((length, width), F32),
        ],
        grid_spec=pltpu.PrefetchScalarGridSpec(
            num_scalar_prefetch=1,
            grid=(width // 128, length // bq),
            in_specs=[
                pl.BlockSpec((bq, 128), lambda p, i, t: (i, p)),
                pl.BlockSpec((length, 128), lambda p, i, t: (0, p)),
                pl.BlockSpec((length, 128), lambda p, i, t: (0, p)),
            ],
            out_specs=[
                pl.BlockSpec((blocks, rows, 128), lambda p, i, t: (0, 0, p)),
                pl.BlockSpec((bq, 128), lambda p, i, t: (i, p)),
            ],
            scratch_shapes=[pltpu.VMEM((2, length, 128), BF)],
        ),
        compiler_params=pltpu.CompilerParams(
            dimension_semantics=("arbitrary", "arbitrary"), vmem_limit_bytes=48 << 20
        ),
        cost_estimate=cost(23),
        name="attention_forward",
    )(table, q, k, v)


def split3(x):
    high = x.astype(BF)
    rest = x - high.astype(F32)
    mid = rest.astype(BF)
    return high, mid, (rest - mid.astype(F32)).astype(BF)


def backward_kernel(
    table, q_ref, k_ref, v_ref, o_ref, do_ref, lse_ref, cos_ref, sin_ref, ck_ref, sk_ref,
    d_ref, qa, da, dqt, *, bq, bk, rows
):
    j = pl.program_id(0)
    length = q_ref.shape[0]
    lane = lax.broadcasted_iota(jnp.int32, (1, 128), 1)
    low = lane < HEAD_DIM
    first = (lane % HEAD_DIM) < HEAD_DIM // 2

    def unturn(t, cosine, sine):
        other = jnp.where(first, pltpu.roll(t, 96, 1), pltpu.roll(t, 32, 1))
        return t * cosine - other * sine

    @pl.when(j == 0)
    def _():
        dqt[...] = jnp.zeros_like(dqt)

        def prep(b, _):
            r = pl.ds(pl.multiple_of(b * rows, rows), rows)
            q, do = q_ref[r, :], do_ref[table[b]]
            product = o_ref[table[b]].astype(F32) * do.astype(F32)
            for h in range(2):
                mine = low if h == 0 else jnp.logical_not(low)
                base = HEAD_DIM if h == 0 else 0
                delta = -jnp.sum(jnp.where(mine, product, 0.0), axis=1, keepdims=True)
                lse = -lse_ref[r, HEAD_DIM * h : HEAD_DIM * h + 1]
                for source, value, target in ((q, lse, qa), (do, delta, da)):
                    x = jnp.where(mine, source, jnp.zeros_like(source))
                    for n, part in enumerate(split3(value)):
                        x = jnp.where(lane == base + n, part, x)
                    target[h, r, :] = x
            return 0

        lax.fori_loop(0, length // rows, prep, 0)

    k, v = k_ref[...], v_ref[...]
    one, zero = jnp.ones_like(k), jnp.zeros_like(k)
    ka, va, kt = [], [], []
    for h in range(2):
        mine = low if h == 0 else jnp.logical_not(low)
        base = HEAD_DIM if h == 0 else 0
        extra = jnp.where(jnp.logical_and(lane >= base, lane < base + 3), one, zero)
        ka.append(jnp.where(mine, k, extra))
        va.append(jnp.where(mine, v, extra))
        kt.append(jnp.where(mine, k, zero).T)

    def step(qb, carry, masked):
        start = pl.multiple_of(qb * bq, bq)
        r = pl.ds(start, bq)
        out, low_scores = [], []
        for h in range(2):
            dk, dv = carry[h]
            qh, dh = qa[h, r, :], da[h, r, :]
            st = dot(ka[h], qh, NT)
            if masked:
                key = lax.broadcasted_iota(jnp.int32, st.shape, 0) + j * bk
                query = lax.broadcasted_iota(jnp.int32, st.shape, 1) + start
                st = jnp.where(key <= query, st, NEGATIVE)
            p = jnp.exp2(st)
            ds = (p * dot(va[h], dh, NT)).astype(BF)
            out.append((dk + dot(ds, qh), dv + dot(p.astype(BF), dh)))
            low_scores.append(ds)
        dqt[:, r] += dot(kt[0], low_scores[0]) + dot(kt[1], low_scores[1])
        return tuple(out)

    z = jnp.zeros((bk, 128), F32)
    carry = ((z, z), (z, z))
    begin, diagonal = (j * bk) // bq, max(bk // bq, 1)
    for d in range(diagonal):
        carry = step(begin + d, carry, True)
    carry = lax.fori_loop(
        begin + diagonal, length // bq, lambda qb, c: step(qb, c, False), carry
    )
    (dk0, dv0), (dk1, dv1) = carry
    dk = unturn(jnp.where(low, dk0, dk1) * (1.0 / LOG2E), ck_ref[...], sk_ref[...])
    mine = pl.ds(pl.multiple_of(j * bk, bk), bk)
    d_ref[mine, 128:256] = dk.astype(BF)
    d_ref[mine, 256:384] = jnp.where(low, dv0, dv1).astype(BF)

    @pl.when(j == pl.num_programs(0) - 1)
    def _():
        dq = dqt[...].T * HEAD_DIM**-0.5
        d_ref[:, 0:128] = unturn(dq, cos_ref[...], sin_ref[...]).astype(BF)


def attention_backward(table, pair, q, k, v, o, do, lse, cosine, sine):
    length = q.shape[0]
    blocks, rows, _ = o.shape
    bq, bk = min(512, length), min(512, length)
    full = pl.BlockSpec((length, 128), lambda j, t: (0, pair))
    block = pl.BlockSpec((bk, 128), lambda j, t: (j, pair))
    loose = pl.BlockSpec((blocks, rows, 128), lambda j, t: (0, 0, pair))
    return pl.pallas_call(
        functools.partial(backward_kernel, bq=bq, bk=bk, rows=rows),
        out_shape=jax.ShapeDtypeStruct((length, 384), BF),
        grid_spec=pltpu.PrefetchScalarGridSpec(
            num_scalar_prefetch=1,
            grid=(length // bk,),
            in_specs=[
                full, block, block, loose, loose, full,
                pl.BlockSpec((length, 128), lambda j, t: (0, 0)),
                pl.BlockSpec((length, 128), lambda j, t: (0, 0)),
                pl.BlockSpec((bk, 128), lambda j, t: (j, 0)),
                pl.BlockSpec((bk, 128), lambda j, t: (j, 0)),
            ],
            out_specs=pl.BlockSpec((length, 384), lambda j, t: (0, 0)),
            scratch_shapes=[
                pltpu.VMEM((2, length, 128), BF),
                pltpu.VMEM((2, length, 128), BF),
                pltpu.VMEM((128, length), F32),
            ],
        ),
        compiler_params=pltpu.CompilerParams(
            dimension_semantics=("arbitrary",), vmem_limit_bytes=56 << 20
        ),
        cost_estimate=cost(44),
        name="attention_backward",
    )(table, q, k, v, o, do, lse, cosine, sine, cosine, sine)


def gelu(v):
    return 0.5 * v * (1.0 + jnp.tanh(0.7978845608 * (v + 0.044715 * v * v * v)))


def gelu_slope(v):
    square = v * v
    t = jnp.tanh(0.7978845608 * v * (1.0 + 0.044715 * square))
    inner = 0.7978845608 * (1.0 + 3.0 * 0.044715 * square)
    return 0.5 * (1.0 + t) + 0.5 * v * (1.0 - t * t) * inner


def load_weights(order, weight_refs, up, down):
    if order is None:
        up[...], down[...] = weight_refs[0][...], weight_refs[1][...]
        return
    half = pl.program_id(0)
    ups, downs = weight_refs[:2], weight_refs[2:]
    sources, rows, _ = ups[0].shape
    part, cut = rows // 2, downs[0].shape[1]
    per = down.shape[0] // (2 * cut)
    for which in range(2):

        @pl.when(half == which)
        def _(which=which):
            for n in range(sources):
                source = order[which, n]
                base = (source // per) * 2 * per + source % per
                for c in range(2):
                    start = pl.multiple_of((base + c * per) * part, part)
                    up[pl.ds(start, part), :] = ups[which][n, c * part : (c + 1) * part, :]

        for n in range(sources):
            source = order[which, n]

            @pl.when(source // per == half)
            def _(n=n, source=source, which=which):
                start = pl.multiple_of(((source % per) * 2 + which) * cut, cut)
                down[pl.ds(start, cut), :] = downs[which][n]


def mlp_forward_kernel(*refs):
    order = refs[0] if len(refs) == 11 else None
    pre_ref, act_ref, sum_ref, up, down = refs[-5:]
    x_ref, *weight_refs = refs[order is not None : -5]
    half, tile = pl.program_id(0), pl.program_id(1)

    @pl.when(tile == 0)
    def _():
        load_weights(order, weight_refs, up, down)

    tm = pre_ref.shape[0]
    rows = pl.ds(pl.multiple_of(tile * tm, tm), tm)
    pre = dot(x_ref[...], up[...])
    act = gelu(pre).astype(BF)
    pre_ref[...] = pre.astype(BF)
    act_ref[...] = act
    term = dot(act, down[...])

    @pl.when(half == 0)
    def _():
        sum_ref[rows, :] = term

    @pl.when(half != 0)
    def _():
        sum_ref[rows, :] += term


def mlp_backward_kernel(*refs):
    order = refs[0] if len(refs) == 11 else None
    low_ref, sum_ref, up, down = refs[-4:]
    g_ref, pre_ref, *weight_refs = refs[order is not None : -4]
    half, tile = pl.program_id(0), pl.program_id(1)

    @pl.when(tile == 0)
    def _():
        load_weights(order, weight_refs, up, down)

    tm = pre_ref.shape[0]
    rows = pl.ds(pl.multiple_of(tile * tm, tm), tm)
    slope = gelu_slope(pre_ref[...].astype(F32))
    low = (slope * dot(g_ref[...], down[...], NT)).astype(BF)
    low_ref[...] = low
    term = dot(low, up[...], NT)

    @pl.when(half == 0)
    def _():
        sum_ref[rows, :] = term

    @pl.when(half != 0)
    def _():
        sum_ref[rows, :] += term


def mlp_call(kernel, name, us, acts, weights, halves, wide_outs):
    count, model = acts[0].shape
    tables = weights[4:]
    if tables:
        sources, rows, _ = weights[0].shape
        unit = model
        fixed = pl.BlockSpec((sources, rows, model), lambda f, m, *t: (0, 0, 0))
        specs = [fixed] * 4
    else:
        unit = weights[1].shape[0] // halves
        specs = [
            pl.BlockSpec((model, unit), lambda f, m, *t: (0, f)),
            pl.BlockSpec((unit, model), lambda f, m, *t: (f, 0)),
        ]
    tm = min(256, count)
    narrow = pl.BlockSpec((tm, model), lambda f, m, *t: (m, 0))
    wide = pl.BlockSpec((tm, unit), lambda f, m, *t: (m, f))
    return pl.pallas_call(
        kernel,
        out_shape=[jax.ShapeDtypeStruct((count, halves * unit), BF)] * wide_outs
        + [jax.ShapeDtypeStruct((count, model), F32)],
        grid_spec=pltpu.PrefetchScalarGridSpec(
            num_scalar_prefetch=len(tables),
            grid=(halves, count // tm),
            in_specs=[narrow] + [wide] * (len(acts) - 1) + specs,
            out_specs=[wide] * wide_outs
            + [pl.BlockSpec((count, model), lambda f, m, *t: (0, 0))],
            scratch_shapes=[pltpu.VMEM((model, unit), BF), pltpu.VMEM((unit, model), BF)],
        ),
        compiler_params=pltpu.CompilerParams(
            dimension_semantics=("arbitrary", "arbitrary"), vmem_limit_bytes=56 << 20
        ),
        cost_estimate=cost(us),
        name=name,
    )(*tables, *acts, *weights[: 4 if tables else 2])


def mlp_forward(x, weights, halves):
    return mlp_call(mlp_forward_kernel, "mlp_forward", 18, [x], weights, halves, 2)


def mlp_backward(grad, pre, weights, halves):
    return mlp_call(mlp_backward_kernel, "mlp_backward", 20, [grad, pre], weights, halves, 1)


def input_grad_kernel(table, *refs):
    w_ref, out_ref = refs[-2:]
    total = None
    for n, ref in enumerate(refs[:-2]):
        term = dot(ref[...], w_ref[:, n * 384 : (n + 1) * 384], NT)
        total = term if total is None else total + term
    out_ref[0] = total.astype(BF)


def input_grad(table, grads, w, rows):
    model = w.shape[0]
    blocks = grads[0].shape[0] // rows
    return pl.pallas_call(
        input_grad_kernel,
        out_shape=jax.ShapeDtypeStruct((blocks, rows, model), BF),
        grid_spec=pltpu.PrefetchScalarGridSpec(
            num_scalar_prefetch=1,
            grid=(blocks,),
            in_specs=[pl.BlockSpec((rows, 384), lambda i, t: (t[i], 0))] * len(grads)
            + [pl.BlockSpec(w.shape, lambda i, t: (0, 0))],
            out_specs=pl.BlockSpec((1, rows, model), lambda i, t: (i, 0, 0)),
        ),
        compiler_params=pltpu.CompilerParams(
            dimension_semantics=("arbitrary",), vmem_limit_bytes=40 << 20
        ),
        cost_estimate=cost(6),
        name="input_grad",
    )(table, *grads, w)


def head_sum_kernel(*refs, group, spread):
    x_refs, outs = refs[:-3], refs[-3:]
    width = outs[0].shape[1] // group
    for m in range(group):
        for pair, ref in enumerate(x_refs):
            total = None
            for n in spread(m):
                term = ref[n].astype(F32)
                total = term if total is None else total + term
            at = slice(m * width + pair * 128, m * width + (pair + 1) * 128)
            for which, out in enumerate(outs):
                out[:, at] = total[:, which * 128 : (which + 1) * 128]


def head_sum(parts, group, spread):
    _, rows, wide = parts[0].shape
    return pl.pallas_call(
        functools.partial(head_sum_kernel, group=group, spread=spread),
        out_shape=[jax.ShapeDtypeStruct((rows, group * len(parts) * wide // 3), F32)] * 3,
        cost_estimate=cost(2),
        name="head_sum",
    )(*parts)


def standardize(values):
    center = values - jnp.mean(values, axis=-1, keepdims=True)
    rstd = lax.rsqrt(jnp.mean(center * center, axis=-1, keepdims=True) + EPSILON)
    return center * rstd, rstd


def norm_backward(xhat, rstd, gain, grad):
    scaled = grad * gain
    inner = scaled - jnp.mean(scaled, axis=-1, keepdims=True)
    inner = inner - xhat * jnp.mean(scaled * xhat, axis=-1, keepdims=True)
    return rstd * inner, jnp.sum(grad * xhat, axis=0), jnp.sum(grad, axis=0)


def flip(x, axis, bit):
    size = lax.axis_size(axis)
    return lax.ppermute(x, axis, [(i, i ^ bit) for i in range(size)])


def scatter_sends(x, axis, dim, bit):
    here = (lax.axis_index(axis) // bit) % 2
    shape = x.shape
    x = x.reshape(shape[:dim] + (shape[dim] // 2, 2) + shape[dim + 1 :])
    mine = lax.dynamic_index_in_dim(x, here, dim + 1, keepdims=False)
    return mine, lax.dynamic_index_in_dim(x, 1 - here, dim + 1, keepdims=False)


def join(mine, came):
    return (mine.astype(F32) + came.astype(F32)).astype(BF)


def scatter_axis(x, axis, dim, bit=1):
    size = lax.axis_size(axis)
    while bit < size:
        mine, theirs = scatter_sends(x, axis, dim, bit)
        x = join(mine, flip(theirs, axis, bit))
        bit *= 2
    return x.reshape(x.shape[:dim] + x.shape[dim + 1 :])


def together(*groups):
    flat, tree = jax.tree.flatten(groups)
    return jax.tree.unflatten(tree, lax.optimization_barrier(tuple(flat)))


def place_in(order):
    index = jnp.arange(order.shape[0], dtype=jnp.int32)
    return jnp.sum(jnp.where(order[:, None] == index[None, :], index[:, None], 0), axis=0)


def gather_order(axes):
    masks = {axis: [0] for axis in AXES}
    for axis in axes:
        bit = lax.axis_size(axis) // 2
        while bit:
            for name in AXES:
                step = bit if name == axis else 0
                masks[name] = masks[name] + [m ^ step for m in masks[name]]
            bit //= 2
    return {axis: jnp.array(masks[axis], jnp.int32) for axis in AXES}


def source_of(axes):
    masks, total = gather_order(axes), 0
    for axis in ("j", "h", "a", "b"):
        total = total * lax.axis_size(axis) + (lax.axis_index(axis) ^ masks[axis])
    return total


def stages_of(axes):
    stages = []
    for axis in axes:
        bit = lax.axis_size(axis) // 2
        while bit:
            stages.append((axis, bit))
            bit //= 2
    return stages


def after(x, *others):
    return lax.optimization_barrier((x,) + others)[0]


def body(
    tokens, cotangent, w_query, w_key, w_value, w_output, w_up, w_down,
    attn_in_gain, attn_in_bias, attn_out_gain, attn_out_bias,
    mlp_in_gain, mlp_in_bias, mlp_out_gain, mlp_out_bias,
):
    _, rows, model = tokens.shape
    nh, na, nb = lax.axis_size("h"), lax.axis_size("a"), lax.axis_size("b")
    jh = 2 * nh
    devices = 4 * nh * na * nb
    group = 2 * nh * nb
    half = na // 2
    length = rows * na * nb
    width = model // group
    pairs = width // 128
    part = w_query.shape[0]
    ij, ih, ic, ia, ib = (lax.axis_index(axis) for axis in AXES)
    slot, parity = ia // half, ia % 2
    member = (ih * 2 + ic) * nb + ib

    def place(j, h, c, a, b):
        return (((j * nh + h) * 2 + c) * na + a) * nb + b

    everyone = [
        (j, h, c, a, b)
        for j in range(2)
        for h in range(nh)
        for c in range(2)
        for a in range(na)
        for b in range(nb)
    ]
    moves = ([], [])
    for turn in range(2):
        for j, h, c, a, b in everyone:
            to_h, to_c = divmod(a % half, 2)
            plane = (h * 2 + c) * 2 + (turn + a // half) % 2
            target = place(j, to_h, to_c, plane, b)
            moves[turn].append((place(j, h, c, a, b), target))

    def regroup(x, turn):
        x = lax.dynamic_index_in_dim(x, (turn + slot) % 2, 0, keepdims=False)
        return lax.ppermute(x, AXES, moves[turn])

    def restore(x, turn):
        return lax.ppermute(x, AXES, [(there, here) for here, there in moves[turn]])

    def ordered(first, second):
        swap = slot == 1
        return jnp.stack([jnp.where(swap, second, first), jnp.where(swap, first, second)])

    def by_offset(x, offset):
        sends = []
        for j, h, c, a, b in everyone:
            to_hc, to_b = divmod(((h * 2 + c) * nb + b) ^ offset, nb)
            sends.append((place(j, h, c, a, b), place(j, to_hc // 2, to_hc % 2, a, to_b)))
        return lax.ppermute(x, AXES, sends)

    core_bit = nb
    far_bits = [1 << n for n in range(group.bit_length() - 1) if (1 << n) != core_bit]

    packed = jnp.stack(
        [attn_in_gain, attn_in_bias, attn_out_gain, attn_out_bias,
         mlp_in_gain, mlp_in_bias, mlp_out_gain, mlp_out_bias]
    )
    vectors = lax.all_to_all(
        jnp.broadcast_to(packed[None], (devices,) + packed.shape), AXES, 0, 0, tiled=True
    )
    vectors = vectors.transpose(1, 0, 2).reshape(8, model).astype(F32)
    gain_ai, bias_ai, gain_ao, bias_ao, gain_mi, bias_mi, gain_mo, bias_mo = [
        vectors[n] for n in range(8)
    ]

    ff = w_up.shape[1]
    unit = ff // (2 * jh)
    up_split = w_up.reshape(part, jh, 2, unit)
    up_mine = lax.dynamic_index_in_dim(up_split, ic, 2, keepdims=False)
    up_other = flip(lax.dynamic_index_in_dim(up_split, 1 - ic, 2, keepdims=False), "c", 1)
    up_rows = jnp.stack(
        [jnp.where(ic == 0, up_mine, up_other), jnp.where(ic == 0, up_other, up_mine)]
    )
    n_up, n_down = 2 * part * jh * unit // model, w_down.shape[0]
    views = unit == model and part % 32 == 0 and n_up == n_down
    up_rows = up_rows.transpose(2, 0, 1, 3).reshape(n_up, model)
    cut, cut_up, cut_out = n_down // 2, n_up // 2, part // 2

    line_stages = stages_of(("a",))
    low_axes, high_axes = ("b", "h", "j"), ("h", "j", "b")

    def grow(x, came):
        return jnp.concatenate([x, came])

    def grow_all(x, stages):
        for axis, bit in stages:
            x = grow(x, flip(x, axis, bit))
        return x

    first = jnp.concatenate([w_down[:cut], w_output[:cut_out], w_down[cut:], w_output[cut_out:]])
    first, second = first[None], up_rows[None]

    own = [regroup(tokens, turn) for turn in range(2)]
    came = flip(first, *line_stages[0])
    own, came, second = together(own, came, second)
    first = grow_all(grow(first, came), line_stages[1:-1])

    columns = jnp.stack(
        [w.reshape(part, group, pairs, 128) for w in (w_query, w_key, w_value)], axis=3
    ).reshape(part, group, 3 * width)
    columns = columns.transpose(1, 0, 2).reshape(1, nh, 2, 1, nb, part, 3 * width)
    columns = jnp.broadcast_to(columns, (2, nh, 2, na, nb, part, 3 * width))
    columns = after(columns.reshape(devices, part, 3 * width), *own)
    w_heads = lax.all_to_all(columns, AXES, 0, 0, tiled=True).reshape(model, 3 * width)

    pieces = {0: own}
    for bit in far_bits:
        for offset in list(pieces):
            pieces[offset ^ bit] = [by_offset(x, bit) for x in pieces[offset]]
    first_came, second_came = flip(first, *line_stages[-1]), flip(second, *line_stages[0])
    pieces, first_came, second_came = together(pieces, first_came, second_came)
    first = grow(first, first_came)
    second = grow_all(grow(second, second_came), line_stages[1:-1])

    wide = cut + cut_out
    low_stages, high_stages = stages_of(low_axes), stages_of(high_axes)
    first_low, first_high = first[:, :wide], first[:, wide:]
    low_came, high_came = flip(first_low, *low_stages[0]), flip(first_high, *high_stages[0])
    for offset in list(pieces):
        pieces[offset ^ core_bit] = [by_offset(x, core_bit) for x in pieces[offset]]
    pieces, w_heads, low_came, high_came, second = together(
        pieces, w_heads, low_came, high_came, second
    )
    first_low = grow_all(grow(first_low, low_came), low_stages[1:-1])
    first_high = grow_all(grow(first_high, high_came), high_stages[1:-1])
    pieces = [pieces[d][r] for d in range(group) for r in range(2)]

    blocks = 2 * group
    index = jnp.arange(blocks, dtype=jnp.int32)
    table = (member ^ (index % group)) * 2 + (parity ^ (index // group))
    positions_of = (parity ^ (index % 2)) * group + (member ^ (index // 2))
    frequency = jnp.exp(
        jnp.arange(HEAD_DIM // 2, dtype=F32) * (-2.0 * math.log(10000.0) / HEAD_DIM)
    )
    angles = jnp.arange(length, dtype=jnp.int32).astype(F32)[:, None] * frequency[None, :]
    cosine = jnp.tile(jnp.cos(angles), (1, 4))
    sine = jnp.tile(jnp.concatenate([-jnp.sin(angles), jnp.sin(angles)], axis=1), (1, 2))

    pieces, first_low, first_high = together(pieces, first_low, first_high)
    second_came = flip(second, *line_stages[-1])
    low_came, high_came = flip(first_low, *low_stages[-1]), flip(first_high, *high_stages[-1])
    normed, queries, keys, values = qkv_call(
        positions_of, pieces, w_heads, vectors, cosine, sine
    )
    queries, second_came = together(queries, second_came)
    second = grow(second, second_came)
    second_low, second_high = second[:, :cut_up], second[:, cut_up:]
    queries, second_low, second_high, cotangent = together(
        queries, second_low, second_high, cotangent
    )
    up_low_came = flip(second_low, *low_stages[0])
    up_high_came = flip(second_high, *high_stages[0])
    grad_in = [regroup(cotangent, turn) for turn in range(2)]
    attended, lse = attention_forward(table, queries, keys, values, rows)
    attended, lse, low_came, high_came, up_low_came, up_high_came, grad_in = together(
        attended, lse, low_came, high_came, up_low_came, up_high_came, grad_in
    )
    first_low, first_high = grow(first_low, low_came), grow(first_high, high_came)
    second_low = grow_all(grow(second_low, up_low_came), low_stages[1:])
    second_high = grow_all(grow(second_high, up_high_came), high_stages[1:])
    low_from, high_from = (source_of(("a",) + axes) for axes in (low_axes, high_axes))

    def exchange(x):
        return [x[0]] + [by_offset(x[d], d) for d in range(1, group)]

    low_at, high_at = place_in(low_from), place_in(high_from)
    out_mine = jnp.concatenate([first_low[:, cut:][low_at], first_high[:, cut:][high_at]], axis=1)
    out_mine = out_mine.reshape(jh, na * nb * part, model)
    out_other = flip(out_mine, "c", 1)
    if group == 2 * jh:
        w_out = jnp.concatenate([out_mine, out_other])
    else:
        w_out = jnp.where(
            ic == 0,
            jnp.stack([out_mine, out_other], axis=1),
            jnp.stack([out_other, out_mine], axis=1),
        ).reshape(group, width, model)
    mixed = exchange(attended.reshape(group, 2 * rows, width))

    def w_out_of(d):
        block = member ^ d
        if group == 2 * jh:
            block = ((block % 2) ^ ic) * jh + block // 2
        return lax.dynamic_index_in_dim(w_out, block, 0, keepdims=False)

    projected = sum(dot(mixed[d], w_out_of(d)) for d in range(group))
    inputs = jnp.concatenate(own).astype(F32)
    hat_ao, rstd_ao = standardize(projected)
    residual = inputs + hat_ao * gain_ao + bias_ao
    hat_mi, rstd_mi = standardize(residual)
    mlp_mine = (hat_mi * gain_mi + bias_mi).astype(BF)
    mlp_normed = jnp.concatenate([mlp_mine, flip(mlp_mine, "c", 1)])
    mlp_normed, second_low, second_high = together(mlp_normed, second_low, second_high)
    if views:
        weights = [second_low, second_high, first_low, first_high]
        weights.append(jnp.stack([low_from, high_from]))
    else:
        up = jnp.concatenate([second_low[low_at], second_high[high_at]], axis=1)
        up = up.reshape(jh, na, nb, jh, 2, part, unit)
        up = up.transpose(0, 4, 1, 2, 5, 3, 6).reshape(model, jh * unit)
        down = [first_low[:, :cut][low_at], first_high[:, :cut][high_at]]
        weights = [up, jnp.concatenate(down, axis=1).reshape(jh * unit, model)]
    pre_act, activated, branch = mlp_forward(mlp_normed, weights, jh)
    count = 2 * rows

    def core_sum(x):
        return x[:count] + flip(x[count:].astype(BF), "c", 1).astype(F32)

    branch = core_sum(branch)
    hat_mo, rstd_mo = standardize(branch)
    block_loose = (residual + hat_mo * gain_mo + bias_mo).astype(BF)

    grad_in = jnp.concatenate(grad_in).astype(F32)
    grad_branch, g_mo_gain, g_mo_bias = norm_backward(hat_mo, rstd_mo, gain_mo, grad_in)
    branch_mine = grad_branch.astype(BF)
    branch_low = jnp.concatenate([branch_mine, flip(branch_mine, "c", 1)])

    down_part = dot(activated, branch_low, TN).astype(BF)
    down_part = down_part.reshape(2, nh, na, nb, n_down, model)
    down_sends = [
        scatter_sends(x, "b", 3, 1) if nb > 1 else None
        for x in (down_part[..., :cut, :], down_part[..., cut:, :])
    ]
    branch_low, down_sends = together(branch_low, down_sends)

    def meet(pair, axis):
        return join(pair[0], flip(pair[1], axis, 1))

    if nb > 1:
        down_came = [flip(down_sends[n][1], "b", 1) for n in range(2)]
    pre_low, grad_mlp = mlp_backward(branch_low, pre_act, weights, jh)
    if nb > 1:
        pre_low, grad_mlp, down_came[0] = together(pre_low, grad_mlp, down_came[0])
    up_part = dot(mlp_normed, pre_low, TN).astype(BF).reshape(2, nh, 2, na, nb, part, jh * unit)
    up_sends = [scatter_sends(up_part[:, :, c], "j", 0, 1) for c in range(2)]
    grad_mlp, up_sends = together(grad_mlp, up_sends)
    up_came = [flip(x[1], "j", 1) for x in up_sends]
    grad_mlp = core_sum(grad_mlp)

    from_mlp, g_mi_gain, g_mi_bias = norm_backward(hat_mi, rstd_mi, gain_mi, grad_mlp)
    grad_residual = grad_in + from_mlp
    grad_projected, g_ao_gain, g_ao_bias = norm_backward(hat_ao, rstd_ao, gain_ao, grad_residual)
    projected_low = grad_projected.astype(BF)
    attended_low = [dot(projected_low, w_out_of(d), NT).astype(BF) for d in range(group)]
    grad_heads = jnp.stack(exchange(attended_low)).reshape(blocks, rows, width)
    grad_out = jnp.stack([dot(mixed[d], projected_low, TN).astype(BF) for d in range(group)])
    grad_out = jnp.stack(
        [lax.dynamic_index_in_dim(grad_out, member ^ m, 0, keepdims=False) for m in range(group)]
    ).reshape(2, nh, 2, na, nb, part, model)
    grad_out = scatter_axis(grad_out, "c", 2)

    if nb > 1:
        down_part = jnp.concatenate(
            [join(mine[0], came) for mine, came in zip(down_sends, down_came)], axis=-2
        )
    down_part = down_part.reshape(2, nh, na, n_down, model)
    up_parts = [
        scatter_axis(join(mine[0], came).reshape(nh, na, nb, part, -1), "h", 0)
        for mine, came in zip(up_sends, up_came)
    ]
    down_sends = scatter_sends(down_part, "j", 0, 1)
    up_sends = [scatter_sends(x, "b", 1, 1) if nb > 1 else None for x in up_parts]
    out_sends = scatter_sends(grad_out, "b", 3, 1) if nb > 1 else None
    grad_heads, down_sends, up_sends, out_sends = together(
        grad_heads, down_sends, up_sends, out_sends
    )

    def backward(pair, grads):
        return attention_backward(
            table, pair, queries, keys, values, attended, grads, lse, cosine, sine
        )

    down_came = flip(down_sends[1], "j", 1)
    if nb > 1:
        up_came = [flip(x[1], "b", 1) for x in up_sends]
        out_came = flip(out_sends[1], "b", 1)
    grad_pairs = [backward(0, grad_heads)]
    if nb > 1:
        grad_pairs, down_came, up_came, out_came = together(
            grad_pairs, down_came, up_came, out_came
        )
        up_parts = [join(mine[0], came) for mine, came in zip(up_sends, up_came)]
        grad_out = join(out_sends[0], out_came)
    else:
        grad_pairs, down_came = together(grad_pairs, down_came)
    down_part = scatter_axis(join(down_sends[0], down_came).reshape(nh, na, n_down, model), "h", 0)
    up_parts = [x.reshape(na, part, -1) for x in up_parts]
    down_sends = scatter_sends(down_part, "a", 0, 1)
    up_sends = [scatter_sends(x, "a", 0, 1) for x in up_parts]
    out_sends = scatter_sends(grad_out.reshape(2, nh, na, part, model), "j", 0, 1)
    weight_pairs = [dot(normed, grad_pairs[0], TN).astype(BF)]
    heads_in = [
        lax.all_to_all(weight_pairs[0].reshape(devices, part, 384), AXES, 0, 0, tiled=True)
    ]
    if pairs > 1:
        grad_heads, down_sends, up_sends, out_sends, weight_pairs = together(
            grad_heads, down_sends, up_sends, out_sends, weight_pairs
        )
    down_came = flip(down_sends[1], "a", 1)
    up_came = [flip(x[1], "a", 1) for x in up_sends]
    out_came = flip(out_sends[1], "j", 1)
    if pairs > 1:
        grad_pairs.append(backward(1, grad_heads))
        grad_pairs, down_came, up_came, out_came = together(
            grad_pairs, down_came, up_came, out_came
        )
        weight_pairs.append(dot(normed, grad_pairs[1], TN).astype(BF))
    grad_pairs, weight_pairs, heads_in = together(grad_pairs, weight_pairs, heads_in)
    for x in weight_pairs[1:]:
        heads_in.append(lax.all_to_all(x.reshape(devices, part, 384), AXES, 0, 0, tiled=True))
    grad_blocks = input_grad(positions_of, grad_pairs, w_heads, rows)
    grad_out = join(out_sends[0], out_came).reshape(nh, na, part, model)
    grad_out = scatter_axis(grad_out, "h", 0)
    grad_out = scatter_axis(grad_out, "a", 0)
    down_part = scatter_axis(join(down_sends[0], down_came), "a", 0, 2)
    up_low, up_high = (
        scatter_axis(join(mine[0], came), "a", 0, 2) for mine, came in zip(up_sends, up_came)
    )
    block_out = ordered(restore(block_loose[:rows], 0), restore(block_loose[rows:], 1))

    sums = {d: [grad_blocks[2 * d + r] for r in range(2)] for d in range(group)}
    for bit in [core_bit] + far_bits:
        kind = BF if far_bits and bit != far_bits[-1] else F32
        for d in [d for d in sums if d & bit]:
            gone = sums.pop(d)
            for r in range(2):
                came = by_offset(gone[r], bit).astype(F32)
                sums[d ^ bit][r] = (sums[d ^ bit][r].astype(F32) + came).astype(kind)
    g_ai_gain, g_ai_bias, grad_tokens = 0.0, 0.0, []
    for r in range(2):
        hat, rstd = standardize(own[r].astype(F32))
        grad_input, gain_term, bias_term = norm_backward(hat, rstd, gain_ai, sums[0][r])
        g_ai_gain, g_ai_bias = g_ai_gain + gain_term, g_ai_bias + bias_term
        total = grad_residual[r * rows : (r + 1) * rows] + grad_input
        if r == 1:
            total, heads_in = together(total, heads_in)
        grad_tokens.append(restore(total.astype(BF), r))
    grad_tokens = ordered(*grad_tokens)

    def spread(m):
        hc, b = divmod(m, nb)
        return [place(j, hc // 2, hc % 2, a, b) for j in range(2) for a in range(na)]

    g_query, g_key, g_value = head_sum(heads_in, group, spread)
    g_down, g_out = down_part.astype(F32), grad_out.astype(F32)
    up_keep = jnp.where(ic == 0, up_low, up_high).reshape(part, jh, unit)
    up_give = jnp.where(ic == 0, up_high, up_low)
    up_come = flip(up_give, "c", 1).reshape(part, jh, unit)
    g_up = jnp.where(
        ic == 0, jnp.stack([up_keep, up_come], axis=2), jnp.stack([up_come, up_keep], axis=2)
    ).reshape(part, ff).astype(F32)

    small = jnp.stack(
        [g_ai_gain, g_ai_bias, g_ao_gain, g_ao_bias, g_mi_gain, g_mi_bias, g_mo_gain, g_mo_bias]
    )
    small = small.reshape(8, devices, part).transpose(1, 0, 2)
    small = jnp.sum(lax.all_to_all(small, AXES, 0, 0, tiled=True), axis=0)
    return (
        block_out, grad_tokens, g_query, g_key, g_value, g_out, g_up, g_down,
        small[0], small[1], small[2], small[3], small[4], small[5], small[6], small[7],
    )


def solution(mesh):
    fsdp, seq = mesh.shape["fsdp"], mesh.shape["seq"]
    inner = Mesh(mesh.devices.reshape(2, fsdp // 4, 2, fsdp, seq // fsdp), AXES)
    lead, line = ("j", "h", "c"), ("a", "b")
    acts = P(lead, line, None)
    weights = P(lead + line, None)
    vector = P(lead + line)
    return jax.shard_map(
        body,
        mesh=inner,
        in_specs=(acts,) * 2 + (weights,) * 6 + (vector,) * 8,
        out_specs=(acts,) * 2 + (weights,) * 6 + (vector,) * 8,
        check_vma=False,
    )
```

```python
import functools
import math

import jax
import jax.numpy as jnp
from jax import lax
from jax.experimental import pallas as pl
from jax.experimental.pallas import tpu as pltpu
from jax.sharding import Mesh
from jax.sharding import PartitionSpec as P

HEADS = 16
HEAD_DIM = 64
EPSILON = 1e-05
NEGATIVE = -1e30
LOG2E = math.log2(math.e)
AXES = ("j", "h", "c", "a", "b")
BF = jnp.bfloat16
F32 = jnp.float32
NT = (((1,), (1,)), ((), ()))
NN = (((1,), (0,)), ((), ()))
TN = (((0,), (0,)), ((), ()))


def cost(us):
    return pl.CostEstimate(flops=int(us * 1e6), bytes_accessed=1 << 10, transcendentals=0)


def dot(left, right, dims=NN):
    return lax.dot_general(left, right, dims, preferred_element_type=F32)


def qkv_kernel(table, order, *refs, group, shape):
    x_refs = refs[:group]
    w_in_ref, vec_ref, cos_ref, sin_ref, n_ref, q_ref, k_ref, v_ref, w_ref, held = refs[group:]
    step = pl.program_id(0)

    @pl.when(step == 0)
    def _():
        if shape is None:
            w_ref[...] = w_in_ref[...]
            return
        na, nb, part = shape
        for n in range(w_in_ref.shape[0]):
            j, a = order[n] // na, order[n] % na
            for m in range(group):
                row = ((j * (group // nb) + m // nb) * na + a) * nb + m % nb
                start = pl.multiple_of(row * part, part)
                w_ref[pl.ds(start, part), :] = w_in_ref[n, m * part : (m + 1) * part, :]

    for n in range(group):

        @pl.when(step // 2 == n)
        def _(n=n):
            held[...] = x_refs[n][step % 2]

    x = held[...].astype(F32)
    center = x - jnp.mean(x, axis=1, keepdims=True)
    rstd = lax.rsqrt(jnp.mean(center * center, axis=1, keepdims=True) + EPSILON)
    normed = (center * rstd * vec_ref[0:1] + vec_ref[1:2]).astype(BF)
    n_ref[...] = normed
    full = dot(normed, w_ref[...])
    lane = lax.broadcasted_iota(jnp.int32, (1, 128), 1)
    first = (lane % HEAD_DIM) < HEAD_DIM // 2
    cosine, sine = cos_ref[...], sin_ref[...]
    for pair in range(q_ref.shape[1] // 128):
        at = slice(pair * 128, (pair + 1) * 128)
        for which, out, scale in ((0, q_ref, LOG2E * HEAD_DIM**-0.5), (1, k_ref, 1.0)):
            t = full[:, (3 * pair + which) * 128 : (3 * pair + which + 1) * 128]
            other = jnp.where(first, pltpu.roll(t, 96, 1), pltpu.roll(t, 32, 1))
            out[:, at] = ((t * cosine + other * sine) * scale).astype(BF)
        v_ref[:, at] = full[:, (3 * pair + 2) * 128 : (3 * pair + 3) * 128].astype(BF)


def qkv_call(table, order, pieces, w, vec, cosine, sine, shape):
    group = len(pieces)
    _, rows, model = pieces[0].shape
    width = model // group
    length = 2 * group * rows
    at = lambda i, *t: (t[0][i], 0)
    fixed = lambda shape: pl.BlockSpec(
        shape, lambda i, *t: (0,) * len(shape), pipeline_mode=pl.Buffered(1)
    )
    return pl.pallas_call(
        functools.partial(qkv_kernel, group=group, shape=shape),
        out_shape=[jax.ShapeDtypeStruct((length, model), BF)]
        + [jax.ShapeDtypeStruct((length, width), BF)] * 3
        + [jax.ShapeDtypeStruct((model, 3 * width), BF)],
        grid_spec=pltpu.PrefetchScalarGridSpec(
            num_scalar_prefetch=2,
            grid=(2 * group,),
            in_specs=[fixed((2, rows, model))] * group
            + [fixed(w.shape), fixed(vec.shape)]
            + [pl.BlockSpec((rows, 128), at)] * 2,
            out_specs=[pl.BlockSpec((rows, model), at)]
            + [pl.BlockSpec((rows, width), at)] * 3
            + [fixed((model, 3 * width))],
            scratch_shapes=[pltpu.VMEM((rows, model), BF)],
        ),
        compiler_params=pltpu.CompilerParams(
            dimension_semantics=("arbitrary",), vmem_limit_bytes=60 << 20
        ),
        cost_estimate=cost(11),
        name="qkv",
    )(table, order, *pieces, w, vec, cosine, sine)


def forward_kernel(table, q_ref, k_ref, v_ref, o_ref, lse_ref, vaug, *, bq, bk, rows):
    i = pl.program_id(1)
    lane = lax.broadcasted_iota(jnp.int32, (1, 128), 1)
    low = lane < HEAD_DIM

    @pl.when(i == 0)
    def _():
        v = v_ref[...]
        one = jnp.ones_like(v)
        vaug[0] = jnp.where(low, v, one)
        vaug[1] = jnp.where(low, one, v)

    parts = bq // bk
    heads = []
    for n in range(parts):
        q = q_ref[n * bk : (n + 1) * bk, :]
        zero = jnp.zeros_like(q)
        heads.append((jnp.where(low, q, zero), jnp.where(low, zero, q)))

    def step(kb, carry, first, masked):
        start = pl.multiple_of(kb * bk, bk)
        k_blk = k_ref[pl.ds(start, bk), :]
        out = list(carry)
        for n in range(first, parts):
            for h in range(2):
                top, acc = carry[2 * n + h]
                s = dot(heads[n][h], k_blk, NT)
                if masked and n == first:
                    row = lax.broadcasted_iota(jnp.int32, s.shape, 0)
                    col = lax.broadcasted_iota(jnp.int32, s.shape, 1)
                    s = jnp.where(col <= row, s, NEGATIVE)
                new = jnp.maximum(top, jnp.max(s, axis=1, keepdims=True))
                p = jnp.exp2(s - new)
                acc = acc * jnp.exp2(top - new) + dot(p.astype(BF), vaug[h, pl.ds(start, bk), :])
                out[2 * n + h] = (new, acc)
        return tuple(out)

    carry = tuple(
        (jnp.full((bk, 1), NEGATIVE, F32), jnp.zeros((bk, 128), F32)) for _ in range(2 * parts)
    )
    full = i * parts
    carry = lax.fori_loop(0, full, lambda kb, c: step(kb, c, 0, False), carry)
    for d in range(parts):
        carry = step(full + d, carry, d, True)
    for n in range(parts):
        (top0, acc0), (top1, acc1) = carry[2 * n : 2 * n + 2]
        total = pltpu.roll(jnp.where(low, acc1, acc0), HEAD_DIM, 1)
        o = (jnp.where(low, acc0, acc1) / total).astype(BF)
        for d in range(bk // rows):
            o_ref[table[(full + n) * (bk // rows) + d]] = o[d * rows : (d + 1) * rows]
        lse_ref[n * bk : (n + 1) * bk, :] = jnp.where(low, top0, top1) + jnp.log2(total)


def attention_forward(table, q, k, v, rows):
    length, width = q.shape
    bq, bk = min(2048, length), min(512, length)
    blocks = length // rows
    return pl.pallas_call(
        functools.partial(forward_kernel, bq=bq, bk=bk, rows=rows),
        out_shape=[
            jax.ShapeDtypeStruct((blocks, rows, width), BF),
            jax.ShapeDtypeStruct((length, width), F32),
        ],
        grid_spec=pltpu.PrefetchScalarGridSpec(
            num_scalar_prefetch=1,
            grid=(width // 128, length // bq),
            in_specs=[
                pl.BlockSpec((bq, 128), lambda p, i, t: (i, p)),
                pl.BlockSpec((length, 128), lambda p, i, t: (0, p)),
                pl.BlockSpec((length, 128), lambda p, i, t: (0, p)),
            ],
            out_specs=[
                pl.BlockSpec((blocks, rows, 128), lambda p, i, t: (0, 0, p)),
                pl.BlockSpec((bq, 128), lambda p, i, t: (i, p)),
            ],
            scratch_shapes=[pltpu.VMEM((2, length, 128), BF)],
        ),
        compiler_params=pltpu.CompilerParams(
            dimension_semantics=("arbitrary", "arbitrary"), vmem_limit_bytes=60 << 20
        ),
        cost_estimate=cost(23),
        name="attention_forward",
    )(table, q, k, v)


def split3(x):
    high = x.astype(BF)
    rest = x - high.astype(F32)
    mid = rest.astype(BF)
    return high, mid, (rest - mid.astype(F32)).astype(BF)


def backward_kernel(
    table, q_ref, k_ref, v_ref, o_ref, do_ref, lse_ref, cos_ref, sin_ref, ck_ref, sk_ref,
    d_ref, qa, da, dqt, *, bk, rows
):
    j = pl.program_id(0)
    length = q_ref.shape[0]
    lane = lax.broadcasted_iota(jnp.int32, (1, 128), 1)
    low = lane < HEAD_DIM
    first = (lane % HEAD_DIM) < HEAD_DIM // 2

    def unturn(t, cosine, sine):
        other = jnp.where(first, pltpu.roll(t, 96, 1), pltpu.roll(t, 32, 1))
        return t * cosine - other * sine

    @pl.when(j == 0)
    def _():
        dqt[...] = jnp.zeros_like(dqt)

        def prep(b, _):
            r = pl.ds(pl.multiple_of(b * rows, rows), rows)
            q, do = q_ref[r, :], do_ref[table[b]]
            product = o_ref[table[b]].astype(F32) * do.astype(F32)
            for h in range(2):
                mine = low if h == 0 else jnp.logical_not(low)
                base = HEAD_DIM if h == 0 else 0
                delta = -jnp.sum(jnp.where(mine, product, 0.0), axis=1, keepdims=True)
                lse = -lse_ref[r, HEAD_DIM * h : HEAD_DIM * h + 1]
                for source, value, target in ((q, lse, qa), (do, delta, da)):
                    x = jnp.where(mine, source, jnp.zeros_like(source))
                    for n, part in enumerate(split3(value)):
                        x = jnp.where(lane == base + n, part, x)
                    target[h, r, :] = x
            return 0

        lax.fori_loop(0, length // rows, prep, 0)

    k, v = k_ref[...], v_ref[...]
    one, zero = jnp.ones_like(k), jnp.zeros_like(k)
    ka, va, kt = [], [], []
    for h in range(2):
        mine = low if h == 0 else jnp.logical_not(low)
        base = HEAD_DIM if h == 0 else 0
        extra = jnp.where(jnp.logical_and(lane >= base, lane < base + 3), one, zero)
        ka.append(jnp.where(mine, k, extra))
        va.append(jnp.where(mine, v, extra))
        kt.append(jnp.where(mine, k, zero).T)

    def products(h, keys, r, masked):
        qh, dh = qa[h, r, :], da[h, r, :]
        st = dot(ka[h][keys], qh, NT)
        if masked:
            key = lax.broadcasted_iota(jnp.int32, st.shape, 0)
            query = lax.broadcasted_iota(jnp.int32, st.shape, 1)
            st = jnp.where(key <= query, st, NEGATIVE)
        p = jnp.exp2(st)
        ds = (p * dot(va[h][keys], dh, NT)).astype(BF)
        return dot(ds, qh), dot(p.astype(BF), dh), ds

    def step(qb, carry):
        r = pl.ds(pl.multiple_of(qb * bk, bk), bk)
        out, low_scores = [], []
        for h in range(2):
            dk, dv, ds = products(h, slice(None), r, False)
            out.append((carry[h][0] + dk, carry[h][1] + dv))
            low_scores.append(ds)
        dqt[:, r] += dot(kt[0], low_scores[0]) + dot(kt[1], low_scores[1])
        return tuple(out)

    half = bk // 2
    carry = []
    upper = pl.ds(pl.multiple_of(j * bk, bk), bk)
    lower = pl.ds(pl.multiple_of(j * bk + half, half), half)
    firsts = [products(h, slice(0, half), upper, True) for h in range(2)]
    seconds = [products(h, slice(half, bk), lower, True) for h in range(2)]
    for h in range(2):
        carry.append(
            tuple(jnp.concatenate([firsts[h][n], seconds[h][n]], axis=0) for n in range(2))
        )
    dqt[:, upper] += dot(kt[0][:, :half], firsts[0][2]) + dot(kt[1][:, :half], firsts[1][2])
    dqt[:, lower] += dot(kt[0][:, half:], seconds[0][2]) + dot(kt[1][:, half:], seconds[1][2])
    carry = lax.fori_loop(j + 1, length // bk, step, tuple(carry))
    (dk0, dv0), (dk1, dv1) = carry
    dk = unturn(jnp.where(low, dk0, dk1) * (1.0 / LOG2E), ck_ref[...], sk_ref[...])
    mine = pl.ds(pl.multiple_of(j * bk, bk), bk)
    d_ref[mine, 128:256] = dk.astype(BF)
    d_ref[mine, 256:384] = jnp.where(low, dv0, dv1).astype(BF)

    @pl.when(j == pl.num_programs(0) - 1)
    def _():
        dq = dqt[...].T * HEAD_DIM**-0.5
        d_ref[:, 0:128] = unturn(dq, cos_ref[...], sin_ref[...]).astype(BF)


def attention_backward(table, pair, q, k, v, o, do, lse, cosine, sine):
    length = q.shape[0]
    blocks, rows, _ = o.shape
    bk = min(512, length)
    full = pl.BlockSpec((length, 128), lambda j, t: (0, pair))
    block = pl.BlockSpec((bk, 128), lambda j, t: (j, pair))
    loose = pl.BlockSpec((blocks, rows, 128), lambda j, t: (0, 0, pair))
    return pl.pallas_call(
        functools.partial(backward_kernel, bk=bk, rows=rows),
        out_shape=jax.ShapeDtypeStruct((length, 384), BF),
        grid_spec=pltpu.PrefetchScalarGridSpec(
            num_scalar_prefetch=1,
            grid=(length // bk,),
            in_specs=[
                full, block, block, loose, loose, full,
                pl.BlockSpec((length, 128), lambda j, t: (0, 0)),
                pl.BlockSpec((length, 128), lambda j, t: (0, 0)),
                pl.BlockSpec((bk, 128), lambda j, t: (j, 0)),
                pl.BlockSpec((bk, 128), lambda j, t: (j, 0)),
            ],
            out_specs=pl.BlockSpec((length, 384), lambda j, t: (0, 0)),
            scratch_shapes=[
                pltpu.VMEM((2, length, 128), BF),
                pltpu.VMEM((2, length, 128), BF),
                pltpu.VMEM((128, length), F32),
            ],
        ),
        compiler_params=pltpu.CompilerParams(
            dimension_semantics=("arbitrary",), vmem_limit_bytes=56 << 20
        ),
        cost_estimate=cost(44),
        name="attention_backward",
    )(table, q, k, v, o, do, lse, cosine, sine, cosine, sine)


def gelu(v):
    return 0.5 * v * (1.0 + jnp.tanh(0.7978845608 * (v + 0.044715 * v * v * v)))


def gelu_slope(v):
    square = v * v
    t = jnp.tanh(0.7978845608 * v * (1.0 + 0.044715 * square))
    inner = 0.7978845608 * (1.0 + 3.0 * 0.044715 * square)
    return 0.5 * (1.0 + t) + 0.5 * v * (1.0 - t * t) * inner


def load_weights(order, weight_refs, up, down):
    if order is None:
        up[...], down[...] = weight_refs[0][...], weight_refs[1][...]
        return
    half = pl.program_id(0)
    ups, downs = weight_refs[:2], weight_refs[2:]
    sources, rows, _ = ups[0].shape
    part, cut = rows // 2, downs[0].shape[1]
    per = down.shape[0] // (2 * cut)
    for which in range(2):

        @pl.when(half == which)
        def _(which=which):
            for n in range(sources):
                source = order[which, n]
                base = (source // per) * 2 * per + source % per
                for c in range(2):
                    start = pl.multiple_of((base + c * per) * part, part)
                    up[pl.ds(start, part), :] = ups[which][n, c * part : (c + 1) * part, :]

        for n in range(sources):
            source = order[which, n]

            @pl.when(source // per == half)
            def _(n=n, source=source, which=which):
                start = pl.multiple_of(((source % per) * 2 + which) * cut, cut)
                down[pl.ds(start, cut), :] = downs[which][n]


def take(step, refs, held):
    for n, ref in enumerate(refs):

        @pl.when(step == n)
        def _(ref=ref):
            held[...] = ref[...].reshape(held.shape)

    return held[...]


def add_halves(term, own_ref, other_ref, total):
    half, tile = pl.program_id(0), pl.program_id(1)

    @pl.when(half == 0)
    def _():
        total[tile] = term

    @pl.when(half != 0)
    def _():
        total[tile] += term

    @pl.when(jnp.logical_and(half == pl.num_programs(0) - 1, tile == 0))
    def _():
        own_ref[...] = total[0]

    @pl.when(jnp.logical_and(half == pl.num_programs(0) - 1, tile == 1))
    def _():
        other_ref[...] = total[1].astype(BF)


def mlp_forward_kernel(*refs, tables):
    order = refs[0] if tables else None
    pre_ref, act_ref, own_ref, other_ref, up, down, held, total = refs[-8:]
    x_refs, weight_refs = refs[tables : tables + 2], refs[tables + 2 : -8]

    @pl.when(pl.program_id(1) == 0)
    def _():
        load_weights(order, weight_refs, up, down)

    pre = dot(take(pl.program_id(1), x_refs, held), up[...])
    act = gelu(pre).astype(BF)
    pre_ref[...] = pre.astype(BF)
    act_ref[...] = act
    add_halves(dot(act, down[...]), own_ref, other_ref, total)


def mlp_backward_kernel(*refs, tables):
    order = refs[0] if tables else None
    low_ref, own_ref, other_ref, up, down, held, total = refs[-7:]
    g_refs, pre_ref, weight_refs = refs[tables : tables + 2], refs[tables + 2], refs[tables + 3 : -7]

    @pl.when(pl.program_id(1) == 0)
    def _():
        load_weights(order, weight_refs, up, down)

    grad = dot(take(pl.program_id(1), g_refs, held), down[...], NT)
    low = (grad * gelu_slope(pre_ref[...].astype(F32))).astype(BF)
    low_ref[...] = low
    add_halves(dot(low, up[...], NT), own_ref, other_ref, total)


def mlp_call(kernel, name, us, narrow, wide, weights, halves, wide_outs):
    count, model = narrow[0].shape
    tables = weights[4:]
    fixed = lambda shape: pl.BlockSpec(
        shape, lambda f, m, *t: (0,) * len(shape), pipeline_mode=pl.Buffered(1)
    )
    if tables:
        sources, rows, _ = weights[0].shape
        unit = model
        specs = [fixed((sources, rows, model))] * 4
    else:
        unit = weights[1].shape[0] // halves
        specs = [
            pl.BlockSpec((model, unit), lambda f, m, *t: (0, f)),
            pl.BlockSpec((unit, model), lambda f, m, *t: (f, 0)),
        ]
    wide_spec = pl.BlockSpec((count, unit), lambda f, m, *t: (m, f))
    return pl.pallas_call(
        functools.partial(kernel, tables=len(tables)),
        out_shape=[jax.ShapeDtypeStruct((2 * count, halves * unit), BF)] * wide_outs
        + [jax.ShapeDtypeStruct((count, model), F32), jax.ShapeDtypeStruct((count, model), BF)],
        grid_spec=pltpu.PrefetchScalarGridSpec(
            num_scalar_prefetch=len(tables),
            grid=(halves, 2),
            in_specs=[fixed((count, model))] * 2 + [wide_spec] * len(wide) + specs,
            out_specs=[wide_spec] * wide_outs + [fixed((count, model))] * 2,
            scratch_shapes=[
                pltpu.VMEM((model, unit), BF),
                pltpu.VMEM((unit, model), BF),
                pltpu.VMEM((count, model), BF),
                pltpu.VMEM((2, count, model), F32),
            ],
        ),
        compiler_params=pltpu.CompilerParams(
            dimension_semantics=("arbitrary", "arbitrary"), vmem_limit_bytes=56 << 20
        ),
        cost_estimate=cost(us),
        name=name,
    )(*tables, *narrow, *wide, *weights[: 4 if tables else 2])


def mlp_forward(narrow, weights, halves):
    return mlp_call(mlp_forward_kernel, "mlp_forward", 18, narrow, [], weights, halves, 2)


def mlp_backward(narrow, pre, weights, halves):
    return mlp_call(mlp_backward_kernel, "mlp_backward", 20, narrow, [pre], weights, halves, 1)


def spread_of(values):
    center = values - jnp.mean(values, axis=1, keepdims=True)
    rstd = lax.rsqrt(jnp.mean(center * center, axis=1, keepdims=True) + EPSILON)
    return center * rstd, rstd


def norm_slope(hat, rstd, gain, grad, sums_ref, at):
    scaled = grad * gain
    inner = scaled - jnp.mean(scaled, axis=1, keepdims=True)
    sums_ref[at : at + 1] += jnp.sum(grad * hat, axis=0, keepdims=True)
    sums_ref[at + 1 : at + 2] += jnp.sum(grad, axis=0, keepdims=True)
    return rstd * (inner - hat * jnp.mean(scaled * hat, axis=1, keepdims=True))


def clear_at_start(ref):
    @pl.when(pl.program_id(0) == 0)
    def _():
        ref[...] = jnp.zeros_like(ref)


def out_kernel(order, places, *refs, group, views):
    projected_ref, residual_ref, normed_ref, w_ref, held = refs[-5:]
    mixed, tokens, vec_ref, weights = refs[:group], refs[group : group + 2], refs[group + 2], refs[group + 3 : -5]
    step = pl.program_id(0)

    @pl.when(step == 0)
    def _():
        if not views:
            w_ref[...] = weights[0][...]
            return
        sources, cut = weights[0].shape[0], weights[0].shape[1] // 2
        halves = places.shape[0] // 2
        per = sources // halves
        for which in range(2):
            for n in range(sources):
                source = order[which, n]
                start = pl.multiple_of((source % per) * 2 * cut + which * cut, cut)
                for core in range(2):
                    block = places[core * halves + source // per]
                    w_ref[block, pl.ds(start, cut), :] = weights[core][n, which * cut : (which + 1) * cut]

    projected = dot(mixed[0][...], w_ref[0])
    for d in range(1, group):
        projected = projected + dot(mixed[d][...], w_ref[d])
    projected_ref[...] = projected
    hat, _ = spread_of(projected)
    x = take(step, tokens, held).astype(F32)
    residual = x + hat * vec_ref[2:3] + vec_ref[3:4]
    residual_ref[...] = residual
    hat, _ = spread_of(residual)
    normed_ref[...] = (hat * vec_ref[4:5] + vec_ref[5:6]).astype(BF)


def out_projection(order, places, mixed, tokens, vec, weights, views):
    group = len(mixed)
    count, width = mixed[0].shape
    rows, model = tokens[0].shape
    fixed = lambda shape: pl.BlockSpec(shape, lambda i, *t: (0,) * len(shape))
    tall = pl.BlockSpec((rows, model), lambda i, *t: (i, 0))
    specs = [fixed(x.shape) for x in weights]
    return pl.pallas_call(
        functools.partial(out_kernel, group=group, views=views),
        out_shape=[
            jax.ShapeDtypeStruct((count, model), F32),
            jax.ShapeDtypeStruct((count, model), F32),
            jax.ShapeDtypeStruct((count, model), BF),
            jax.ShapeDtypeStruct((group, width, model), BF),
        ],
        grid_spec=pltpu.PrefetchScalarGridSpec(
            num_scalar_prefetch=2,
            grid=(count // rows,),
            in_specs=[pl.BlockSpec((rows, width), lambda i, *t: (i, 0))] * group
            + [fixed((rows, model))] * 2
            + [fixed(vec.shape)]
            + specs,
            out_specs=[tall, tall, tall, fixed((group, width, model))],
            scratch_shapes=[pltpu.VMEM((rows, model), BF)],
        ),
        compiler_params=pltpu.CompilerParams(
            dimension_semantics=("arbitrary",), vmem_limit_bytes=40 << 20
        ),
        cost_estimate=cost(5),
        name="out_projection",
    )(order, places, *mixed, *tokens, vec, *weights)


def middle_kernel(own_ref, came_ref, residual_ref, g0_ref, g1_ref, vec_ref, out_ref, low_ref, sums_ref, held):
    clear_at_start(sums_ref)
    hat, rstd = spread_of(own_ref[...] + came_ref[...].astype(F32))
    out_ref[...] = (residual_ref[...] + hat * vec_ref[6:7] + vec_ref[7:8]).astype(BF)
    grad = take(pl.program_id(0), (g0_ref, g1_ref), held).astype(F32)
    low_ref[...] = norm_slope(hat, rstd, vec_ref[6:7], grad, sums_ref, 6).astype(BF)


def turn_kernel(own_ref, came_ref, residual_ref, projected_ref, g0_ref, g1_ref, vec_ref, w_ref, *refs, group):
    grad_ref, low_ref, *heads, sums_ref, held = refs
    clear_at_start(sums_ref)
    hat, rstd = spread_of(residual_ref[...])
    grad = own_ref[...] + came_ref[...].astype(F32)
    passed = take(pl.program_id(0), (g0_ref, g1_ref), held).astype(F32)
    grad = passed + norm_slope(hat, rstd, vec_ref[4:5], grad, sums_ref, 4)
    grad_ref[...] = grad
    hat, rstd = spread_of(projected_ref[...])
    low = norm_slope(hat, rstd, vec_ref[2:3], grad, sums_ref, 2).astype(BF)
    low_ref[...] = low
    for d in range(group):
        heads[d][...] = dot(low, w_ref[d], NT).astype(BF)


def last_kernel(x_ref, grad_ref, *refs):
    *parts, vec_ref, out_ref, sums_ref = refs
    clear_at_start(sums_ref)
    hat, rstd = spread_of(x_ref[...].astype(F32))
    grad = parts[0][...].astype(F32)
    for part in parts[1:]:
        grad = grad + part[...].astype(F32)
    grad = norm_slope(hat, rstd, vec_ref[0:1], grad, sums_ref, 0)
    out_ref[...] = (grad_ref[...] + grad).astype(BF)


def row_call(kernel, name, us, rows, tall, halves, fixed, outs):
    model = tall[0].shape[1]
    count = tall[0].shape[0]
    whole = lambda x: pl.BlockSpec(x.shape, lambda i, n=x.ndim: (0,) * n)
    block = lambda width: pl.BlockSpec((rows, width), lambda i: (i, 0))
    return pl.pallas_call(
        kernel,
        out_shape=[jax.ShapeDtypeStruct((count, width), kind) for width, kind in outs]
        + [jax.ShapeDtypeStruct((8, model), F32)],
        grid=(count // rows,),
        in_specs=[block(model)] * len(tall) + [whole(x) for x in (*halves, *fixed)],
        out_specs=[block(width) for width, _ in outs] + [pl.BlockSpec((8, model), lambda i: (0, 0))],
        scratch_shapes=[pltpu.VMEM((rows, model), BF)] if halves else [],
        compiler_params=pltpu.CompilerParams(
            dimension_semantics=("arbitrary",), vmem_limit_bytes=40 << 20
        ),
        cost_estimate=cost(us),
        name=name,
    )(*tall, *halves, *fixed)


def input_grad_kernel(table, *refs):
    w_ref, give_ref, keep_ref = refs[-3:]
    total = None
    for n, ref in enumerate(refs[:-3]):
        term = dot(ref[...], w_ref[:, n * 384 : (n + 1) * 384], NT)
        total = term if total is None else total + term
    giving = pl.program_id(0) < pl.num_programs(0) // 2

    @pl.when(giving)
    def _():
        give_ref[0] = total.astype(BF)

    @pl.when(jnp.logical_not(giving))
    def _():
        keep_ref[0] = total.astype(BF)


def input_grad(table, grads, w, rows):
    model = w.shape[0]
    blocks = grads[0].shape[0] // rows
    half = blocks // 2
    return pl.pallas_call(
        input_grad_kernel,
        out_shape=[jax.ShapeDtypeStruct((half, rows, model), BF)] * 2,
        grid_spec=pltpu.PrefetchScalarGridSpec(
            num_scalar_prefetch=1,
            grid=(blocks,),
            in_specs=[pl.BlockSpec((rows, 384), lambda i, t: (t[i], 0))] * len(grads)
            + [pl.BlockSpec(w.shape, lambda i, t: (0, 0))],
            out_specs=[
                pl.BlockSpec((1, rows, model), lambda i, t: (jnp.minimum(i, half - 1), 0, 0)),
                pl.BlockSpec((1, rows, model), lambda i, t: (jnp.maximum(i - half, 0), 0, 0)),
            ],
        ),
        compiler_params=pltpu.CompilerParams(
            dimension_semantics=("arbitrary",), vmem_limit_bytes=40 << 20
        ),
        cost_estimate=cost(6),
        name="input_grad",
    )(table, *grads, w)


def head_sum_kernel(*refs, group, spread):
    x_refs, outs = refs[:-3], refs[-3:]
    width = outs[0].shape[1] // group
    for m in range(group):
        for pair, ref in enumerate(x_refs):
            total = None
            for n in spread(m):
                term = ref[n].astype(F32)
                total = term if total is None else total + term
            at = slice(m * width + pair * 128, m * width + (pair + 1) * 128)
            for which, out in enumerate(outs):
                out[:, at] = total[:, which * 128 : (which + 1) * 128]


def head_sum(parts, group, spread):
    _, rows, wide = parts[0].shape
    return pl.pallas_call(
        functools.partial(head_sum_kernel, group=group, spread=spread),
        out_shape=[jax.ShapeDtypeStruct((rows, group * len(parts) * wide // 3), F32)] * 3,
        cost_estimate=cost(2),
        name="head_sum",
    )(*parts)


def flip(x, axis, bit):
    size = lax.axis_size(axis)
    return lax.ppermute(x, axis, [(i, i ^ bit) for i in range(size)])


def scatter_sends(x, axis, dim, bit):
    here = (lax.axis_index(axis) // bit) % 2
    shape = x.shape
    x = x.reshape(shape[:dim] + (shape[dim] // 2, 2) + shape[dim + 1 :])
    mine = lax.dynamic_index_in_dim(x, here, dim + 1, keepdims=False)
    return mine, lax.dynamic_index_in_dim(x, 1 - here, dim + 1, keepdims=False)


def join(mine, came, kind=BF):
    return (mine.astype(F32) + came.astype(F32)).astype(kind)


def scatter_axis(x, axis, dim, bit=1, kind=BF):
    size = lax.axis_size(axis)
    while bit < size:
        mine, theirs = scatter_sends(x, axis, dim, bit)
        x = join(mine, flip(theirs, axis, bit), kind)
        bit *= 2
    return x.reshape(x.shape[:dim] + x.shape[dim + 1 :])


def together(*groups):
    flat, tree = jax.tree.flatten(groups)
    return jax.tree.unflatten(tree, lax.optimization_barrier(tuple(flat)))


def place_in(order):
    index = jnp.arange(order.shape[0], dtype=jnp.int32)
    return jnp.sum(jnp.where(order[:, None] == index[None, :], index[:, None], 0), axis=0)


def gather_order(axes):
    masks = {axis: [0] for axis in AXES}
    for axis in axes:
        bit = lax.axis_size(axis) // 2
        while bit:
            for name in AXES:
                step = bit if name == axis else 0
                masks[name] = masks[name] + [m ^ step for m in masks[name]]
            bit //= 2
    return {axis: jnp.array(masks[axis], jnp.int32) for axis in AXES}


def source_of(axes, along=("j", "h", "a", "b")):
    masks, total = gather_order(axes), 0
    for axis in along:
        total = total * lax.axis_size(axis) + (lax.axis_index(axis) ^ masks[axis])
    return total


def stages_of(axes):
    stages = []
    for axis in axes:
        bit = lax.axis_size(axis) // 2
        while bit:
            stages.append((axis, bit))
            bit //= 2
    return stages


def after(x, *others):
    return lax.optimization_barrier((x,) + others)[0]


def body(
    tokens, cotangent, w_query, w_key, w_value, w_output, w_up, w_down,
    attn_in_gain, attn_in_bias, attn_out_gain, attn_out_bias,
    mlp_in_gain, mlp_in_bias, mlp_out_gain, mlp_out_bias,
):
    _, rows, model = tokens.shape
    nh, na, nb = lax.axis_size("h"), lax.axis_size("a"), lax.axis_size("b")
    jh = 2 * nh
    devices = 4 * nh * na * nb
    group = 2 * nh * nb
    half = na // 2
    length = rows * na * nb
    width = model // group
    pairs = width // 128
    part = w_query.shape[0]
    ij, ih, ic, ia, ib = (lax.axis_index(axis) for axis in AXES)
    slot, parity = ia // half, ia % 2
    member = (ih * 2 + ic) * nb + ib

    def place(j, h, c, a, b):
        return (((j * nh + h) * 2 + c) * na + a) * nb + b

    everyone = [
        (j, h, c, a, b)
        for j in range(2)
        for h in range(nh)
        for c in range(2)
        for a in range(na)
        for b in range(nb)
    ]
    moves = ([], [])
    for turn in range(2):
        for j, h, c, a, b in everyone:
            to_h, to_c = divmod(a % half, 2)
            plane = (h * 2 + c) * 2 + (turn + a // half) % 2
            target = place(j, to_h, to_c, plane, b)
            moves[turn].append((place(j, h, c, a, b), target))

    def regroup(x, turn):
        x = lax.dynamic_index_in_dim(x, (turn + slot) % 2, 0, keepdims=False)
        return lax.ppermute(x, AXES, moves[turn])

    def restore(x, turn):
        return lax.ppermute(x, AXES, [(there, here) for here, there in moves[turn]])

    def ordered(first, second):
        swap = slot == 1
        return jnp.stack([jnp.where(swap, second, first), jnp.where(swap, first, second)])

    def by_offset(x, offset):
        sends = []
        for j, h, c, a, b in everyone:
            to_hc, to_b = divmod(((h * 2 + c) * nb + b) ^ offset, nb)
            sends.append((place(j, h, c, a, b), place(j, to_hc // 2, to_hc % 2, a, to_b)))
        return lax.ppermute(x, AXES, sends)

    core_bit = nb
    far_bits = [1 << n for n in range(group.bit_length() - 1) if (1 << n) != core_bit]

    ff = w_up.shape[1]
    unit = ff // (2 * jh)
    up_split = w_up.reshape(part, jh, 2, unit)
    up_mine = lax.dynamic_index_in_dim(up_split, ic, 2, keepdims=False)
    up_other = flip(lax.dynamic_index_in_dim(up_split, 1 - ic, 2, keepdims=False), "c", 1)
    up_rows = jnp.stack(
        [jnp.where(ic == 0, up_mine, up_other), jnp.where(ic == 0, up_other, up_mine)]
    )
    n_up, n_down = 2 * part * jh * unit // model, w_down.shape[0]
    views = unit == model and part % 32 == 0 and n_up == n_down
    up_rows = up_rows.transpose(2, 0, 1, 3).reshape(n_up, model)
    cut, cut_up, cut_out = n_down // 2, n_up // 2, part // 2

    line_stages = stages_of(("a",))
    low_axes, high_axes = ("b", "h", "j"), ("h", "j", "b")

    def grow(x, came):
        return jnp.concatenate([x, came])

    def grow_all(x, stages):
        for axis, bit in stages:
            x = grow(x, flip(x, axis, bit))
        return x

    first = jnp.concatenate([w_down[:cut], w_output[:cut_out], w_down[cut:], w_output[cut_out:]])
    first, second = first[None], up_rows[None]

    columns = jnp.stack(
        [w.reshape(part, group, pairs, 128) for w in (w_query, w_key, w_value)], axis=3
    ).reshape(part, group, 3 * width)
    columns = columns.transpose(1, 0, 2)
    columns = lax.all_to_all(columns, ("h", "c", "b"), 0, 0, tiled=True)
    columns = columns.reshape(1, group * part, 3 * width)

    blocks = 2 * group
    index = jnp.arange(blocks, dtype=jnp.int32)
    table = (member ^ (index % group)) * 2 + (parity ^ (index // group))
    positions_of = (parity ^ (index % 2)) * group + (member ^ (index // 2))
    lane = jnp.arange(128, dtype=jnp.int32)
    frequency = jnp.exp(
        (lane % (HEAD_DIM // 2)).astype(F32) * (-2.0 * math.log(10000.0) / HEAD_DIM)
    )
    angles = jnp.arange(length, dtype=jnp.int32).astype(F32)[:, None] * frequency[None, :]
    cosine = jnp.cos(angles)
    sine = jnp.sin(angles) * jnp.where((lane // (HEAD_DIM // 2)) % 2 == 0, -1.0, 1.0)[None, :]

    vectors = grow_all(
        jnp.stack(
            [attn_in_gain, attn_in_bias, attn_out_gain, attn_out_bias,
             mlp_in_gain, mlp_in_bias, mlp_out_gain, mlp_out_bias]
        )[None],
        stages_of(("c", "b", "h", "j", "a")),
    )
    vectors = vectors[place_in(source_of(("c", "b", "h", "j", "a"), AXES))]
    vectors = vectors.transpose(1, 0, 2).reshape(8, model).astype(F32)

    def columns_in_order(x):
        x = x[place_in(w_from)].reshape(2, na, nh, 2, nb, part, 3 * width)
        return x.transpose(0, 2, 3, 1, 4, 5, 6).reshape(model, 3 * width)

    own = [regroup(tokens, turn) for turn in range(2)]
    first_came = flip(first, *line_stages[0])
    w_came = flip(columns, *line_stages[0])
    first = grow_all(grow(first, first_came), line_stages[1:])
    wide = cut + cut_out
    low_stages, high_stages = stages_of(low_axes), stages_of(high_axes)
    first_low, first_high = first[:, :wide], first[:, wide:]
    own, first_low, first_high, w_came, second, cosine, sine, vectors = together(
        own, first_low, first_high, w_came, second, cosine, sine, vectors
    )
    columns = grow_all(grow(columns, w_came), line_stages[1:-1])
    second_came, w_came = flip(second, *line_stages[0]), flip(columns, *line_stages[-1])
    high_came = flip(first_high, *high_stages[0])
    pieces = {0: jnp.stack(own)}
    for bit in far_bits:
        for offset in list(pieces):
            pieces[offset ^ bit] = by_offset(pieces[offset], bit)
    pieces[core_bit] = by_offset(pieces[0], core_bit)
    pieces, high_came, second_came, w_came = together(pieces, high_came, second_came, w_came)
    second = grow_all(grow(second, second_came), line_stages[1:-1])
    columns = grow(columns, w_came)

    w_came = flip(columns, "j", 1)
    w_from = source_of(("a", "j"), ("j", "a"))
    low_came, second_came = flip(first_low, *low_stages[0]), flip(second, *line_stages[-1])
    for offset in range(1, group):
        if not offset & core_bit:
            pieces[offset ^ core_bit] = by_offset(pieces[offset], core_bit)
    pieces, w_came, low_came, second_came = together(pieces, w_came, low_came, second_came)
    columns = grow(columns, w_came)
    if views:
        w_heads, w_shape = columns, (na, nb, part)
    else:
        w_heads, w_shape = columns_in_order(columns), None
    first_low = grow_all(grow(first_low, low_came), low_stages[1:-1])
    first_high = grow_all(grow(first_high, high_came), high_stages[1:-1])
    second = grow(second, second_came)
    second_low, second_high = second[:, :cut_up], second[:, cut_up:]
    pieces, first_low, first_high, second_low, second_high = together(
        pieces, first_low, first_high, second_low, second_high
    )
    low_came, high_came = flip(first_low, *low_stages[-1]), flip(first_high, *high_stages[-1])
    up_low_came = flip(second_low, *low_stages[0])
    up_high_came = flip(second_high, *high_stages[0])
    normed, queries, keys, values, w_heads = qkv_call(
        positions_of, w_from, [pieces[d] for d in range(group)], w_heads, vectors,
        cosine, sine, w_shape,
    )
    attended, lse = attention_forward(table, queries, keys, values, rows)
    attended, lse, low_came, high_came, up_low_came, up_high_came, cotangent = together(
        attended, lse, low_came, high_came, up_low_came, up_high_came, cotangent
    )
    first_low, first_high = grow(first_low, low_came), grow(first_high, high_came)
    second_low = grow_all(grow(second_low, up_low_came), low_stages[1:])
    second_high = grow_all(grow(second_high, up_high_came), high_stages[1:])
    low_from, high_from = (source_of(("a",) + axes) for axes in (low_axes, high_axes))

    def exchange(x):
        return [x[0]] + [by_offset(x[d], d) for d in range(1, group)]

    order = jnp.stack([low_from, high_from])
    low_at, high_at = place_in(low_from), place_in(high_from)
    core_block = jnp.arange(2 * jh, dtype=jnp.int32)
    if views:
        mine = jnp.concatenate([first_low[:, cut:], first_high[:, cut:]], axis=1)
        out_weights = [mine, flip(mine, "c", 1)]
    else:
        mine = jnp.concatenate(
            [first_low[:, cut:][low_at], first_high[:, cut:][high_at]], axis=1
        ).reshape(jh, na * nb * part, model)
        other = flip(mine, "c", 1)
        w_out = jnp.where(
            ic == 0, jnp.stack([mine, other], axis=1), jnp.stack([other, mine], axis=1)
        ).reshape(group, width, model)
        out_weights = [w_out[member ^ jnp.arange(group)]]
    places = member ^ ((core_block % jh) * 2 + (ic ^ (core_block // jh)))
    mixed = exchange(attended.reshape(group, 2 * rows, width))
    projected, residual, mlp_mine, w_out = out_projection(
        order, places, mixed, own, vectors, out_weights, views
    )
    mlp_rows = [mlp_mine, flip(mlp_mine, "c", 1)]
    mlp_rows, second_low, second_high, cotangent = together(
        mlp_rows, second_low, second_high, cotangent
    )
    if views:
        weights = [second_low, second_high, first_low, first_high, order]
    else:
        up = jnp.concatenate([second_low[low_at], second_high[high_at]], axis=1)
        up = up.reshape(jh, na, nb, jh, 2, part, unit)
        up = up.transpose(0, 4, 1, 2, 5, 3, 6).reshape(model, jh * unit)
        down = [first_low[:, :cut][low_at], first_high[:, :cut][high_at]]
        weights = [up, jnp.concatenate(down, axis=1).reshape(jh * unit, model)]
    grad_in = [regroup(cotangent, turn) for turn in range(2)]
    pre_act, activated, branch, branch_other = mlp_forward(mlp_rows, weights, jh)
    branch, branch_other, grad_in = together(branch, branch_other, grad_in)
    block_loose, branch_mine, mo_sums = row_call(
        middle_kernel, "middle", 3, rows,
        [branch, flip(branch_other, "c", 1), residual], grad_in, [vectors],
        [(model, BF), (model, BF)],
    )
    branch_rows = [branch_mine, flip(branch_mine, "c", 1)]

    def sends(x, axis, dim):
        return scatter_sends(x, axis, dim, 1) if lax.axis_size(axis) > 1 else (x, None)

    def send(pair, axis):
        return None if pair[1] is None else flip(pair[1], axis, 1)

    def added(pair, came, shape):
        return (pair[0] if came is None else join(pair[0], came)).reshape(shape)

    down_part = dot(activated, jnp.concatenate(branch_rows), TN).astype(BF)
    down_part = down_part.reshape(2, nh, na, nb, n_down, model)
    low_sends = sends(down_part[..., :cut, :], "b", 3)
    high_sends = sends(down_part[..., cut:, :], "j", 0)
    branch_rows, low_sends, high_sends, block_loose = together(
        branch_rows, low_sends, high_sends, block_loose
    )
    low_came, high_came = send(low_sends, "b"), send(high_sends, "j")
    block_came = [restore(block_loose[:rows], 0), restore(block_loose[rows:], 1)]
    pre_low, grad_mlp, grad_other = mlp_backward(branch_rows, pre_act, weights, jh)
    pre_low, grad_mlp, grad_other, low_came, high_came = together(
        pre_low, grad_mlp, grad_other, low_came, high_came
    )
    grad_other = flip(grad_other, "c", 1)
    low_sends = sends(added(low_sends, low_came, (2, nh, na, cut, model)), "j", 0)
    high_sends = sends(added(high_sends, high_came, (nh, na, nb, cut, model)), "b", 2)
    grad_mlp, grad_other, low_sends, high_sends = together(
        grad_mlp, grad_other, low_sends, high_sends
    )
    low_came, high_came = send(low_sends, "j"), send(high_sends, "b")
    grad_residual, projected_low, *attended_low, turn_sums = row_call(
        functools.partial(turn_kernel, group=group), "turn", 6, rows,
        [grad_mlp, grad_other, residual, projected], grad_in, [vectors, w_out],
        [(model, F32), (model, BF)] + [(width, BF)] * group,
    )
    attended_low, pre_low, low_came, high_came, block_came = together(
        attended_low, pre_low, low_came, high_came, block_came
    )
    grad_heads = jnp.stack(exchange(attended_low)).reshape(blocks, rows, width)
    down_part = jnp.concatenate(
        [
            added(low_sends, low_came, (nh, na, cut, model)),
            added(high_sends, high_came, (nh, na, cut, model)),
        ],
        axis=2,
    )
    down_sends = sends(scatter_axis(down_part, "h", 0), "a", 0)
    up_part = dot(jnp.concatenate(mlp_rows), pre_low, TN).astype(BF)
    up_part = up_part.reshape(2, nh, 2, na, nb, part, jh * unit)
    low_sends = sends(up_part[:, :, 0], "j", 0)
    high_sends = sends(up_part[:, :, 1], "b", 3)
    grad_out = jnp.stack([dot(mixed[d], projected_low, TN).astype(BF) for d in range(group)])
    grad_out = jnp.stack(
        [lax.dynamic_index_in_dim(grad_out, member ^ m, 0, keepdims=False) for m in range(group)]
    ).reshape(2, nh, 2, na, nb, part, model)
    out_sends = sends(scatter_axis(grad_out, "c", 2), "j", 0)
    grad_heads, down_sends, low_sends, high_sends, out_sends = together(
        grad_heads, down_sends, low_sends, high_sends, out_sends
    )

    def backward(pair, grads):
        return attention_backward(
            table, pair, queries, keys, values, attended, grads, lse, cosine, sine
        )

    low_came, high_came = send(low_sends, "j"), send(high_sends, "b")
    down_came, out_came = send(down_sends, "a"), send(out_sends, "j")
    grad_pairs = [backward(0, grad_heads)]
    grad_pairs, down_came, low_came, high_came, out_came = together(
        grad_pairs, down_came, low_came, high_came, out_came
    )
    down_part = added(down_sends, down_came, (na // 2, n_down, model))
    down_sends = scatter_sends(down_part, "a", 0, 2)
    low_part = scatter_axis(added(low_sends, low_came, (nh, na, nb, part, jh * unit)), "h", 0)
    low_sends = sends(low_part, "b", 1)
    high_sends = sends(added(high_sends, high_came, (2, nh, na, part, jh * unit)), "j", 0)
    out_part = scatter_axis(added(out_sends, out_came, (nh, na, nb, part, model)), "h", 0)
    out_sends = sends(out_part, "b", 1)
    weight_pairs = [dot(normed, grad_pairs[0], TN).astype(BF)]
    heads_in = [
        lax.all_to_all(weight_pairs[0].reshape(devices, part, 384), AXES, 0, 0, tiled=True)
    ]
    if pairs > 1:
        grad_heads, down_sends, low_sends, high_sends, out_sends, weight_pairs = together(
            grad_heads, down_sends, low_sends, high_sends, out_sends, weight_pairs
        )
    down_came, low_came = flip(down_sends[1], "a", 2), send(low_sends, "b")
    high_came, out_came = send(high_sends, "j"), send(out_sends, "b")
    if pairs > 1:
        grad_pairs.append(backward(1, grad_heads))
    grads_give = [d for d in range(group) if d & core_bit]
    block_order = [2 * d + r for d in grads_give for r in range(2)]
    block_order += [2 * (d ^ core_bit) + r for d in grads_give for r in range(2)]
    grad_pairs, down_came, low_came, high_came, out_came, heads_in = together(
        grad_pairs, down_came, low_came, high_came, out_came, heads_in
    )
    grad_give, grad_keep = input_grad(
        positions_of[jnp.array(block_order, jnp.int32)], grad_pairs, w_heads, rows
    )
    grad_give, grad_keep, down_came, low_came, high_came, out_came, grad_pairs = together(
        grad_give, grad_keep, down_came, low_came, high_came, out_came, grad_pairs
    )
    give_came = by_offset(grad_give, core_bit)
    rest_part = jnp.concatenate(
        [
            added(low_sends, low_came, (na, part, jh * unit)),
            scatter_axis(added(high_sends, high_came, (nh, na, part, jh * unit)), "h", 0),
            added(out_sends, out_came, (na, part, model)),
        ],
        axis=2,
    )
    rest_sends = sends(rest_part, "a", 0)
    give_came, rest_sends, grad_keep = together(give_came, rest_sends, grad_keep)
    rest_came = send(rest_sends, "a")

    grad_keep = join(grad_keep, give_came)
    sums = {
        d ^ core_bit: [grad_keep[2 * n + r] for r in range(2)] for n, d in enumerate(grads_give)
    }
    for bit in far_bits[:-1]:
        for d in [d for d in sums if d & bit]:
            gone = sums.pop(d)
            for r in range(2):
                sums[d ^ bit][r] = join(sums[d ^ bit][r], by_offset(gone[r], bit))
    sums, grad_pairs = together(sums, grad_pairs)
    if far_bits:
        final = [by_offset(x, far_bits[-1]) for x in sums[far_bits[-1]]]
    weight_pairs = [dot(normed, x, TN).astype(BF) for x in grad_pairs[1:]]
    if far_bits:
        final[0], rest_came, down_came, block_came = together(
            final[0], rest_came, down_came, block_came
        )
    for x in weight_pairs:
        heads_in.append(lax.all_to_all(x.reshape(devices, part, 384), AXES, 0, 0, tiled=True))
    rest_part = added(rest_sends, rest_came, (na // 2, part, -1))
    rest_part = scatter_axis(rest_part, "a", 0, 2)
    down_part = join(down_sends[0], down_came).reshape(na // 4, n_down, model)
    down_part = scatter_axis(down_part, "a", 0, 4)
    block_out = ordered(*block_came)

    small, grad_tokens = mo_sums + turn_sums, []
    for r in range(2):
        parts = [sums[0][r]] + ([final[r]] if far_bits else [])
        total, sums_in = row_call(
            last_kernel, "last", 2, rows,
            [own[r], grad_residual[r * rows : (r + 1) * rows]] + parts, [], [vectors],
            [(model, BF)],
        )
        small = small + sums_in
        if r == 0 and far_bits:
            total, final[1] = together(total, final[1])
        grad_tokens.append(restore(total, r))
    grad_tokens = ordered(*grad_tokens)

    def spread(m):
        hc, b = divmod(m, nb)
        return [place(j, hc // 2, hc % 2, a, b) for j in range(2) for a in range(na)]

    g_query, g_key, g_value = head_sum(heads_in, group, spread)
    g_down, g_out = down_part.astype(F32), rest_part[:, 2 * jh * unit :].astype(F32)
    up_part = jnp.stack([rest_part[:, n * jh * unit : (n + 1) * jh * unit] for n in range(2)])
    up_keep = lax.dynamic_index_in_dim(up_part, ic, 0, keepdims=False).reshape(part, jh, unit)
    up_give = lax.dynamic_index_in_dim(up_part, 1 - ic, 0, keepdims=False)
    up_come = flip(up_give, "c", 1).reshape(part, jh, unit)
    g_up = jnp.where(
        ic == 0, jnp.stack([up_keep, up_come], axis=2), jnp.stack([up_come, up_keep], axis=2)
    ).reshape(part, ff).astype(F32)

    small = small.reshape(8, 2, nh, 2, na, nb, part).transpose(3, 5, 1, 2, 4, 0, 6)
    for axis in ("c", "b", "j", "h", "a"):
        small = scatter_axis(small, axis, 0, kind=F32)
    return (
        block_out, grad_tokens, g_query, g_key, g_value, g_out, g_up, g_down,
        small[0], small[1], small[2], small[3], small[4], small[5], small[6], small[7],
    )


def solution(mesh):
    fsdp, seq = mesh.shape["fsdp"], mesh.shape["seq"]
    inner = Mesh(mesh.devices.reshape(2, fsdp // 4, 2, fsdp, seq // fsdp), AXES)
    lead, line = ("j", "h", "c"), ("a", "b")
    acts = P(lead, line, None)
    weights = P(lead + line, None)
    vector = P(lead + line)
    return jax.shard_map(
        body,
        mesh=inner,
        in_specs=(acts,) * 2 + (weights,) * 6 + (vector,) * 8,
        out_specs=(acts,) * 2 + (weights,) * 6 + (vector,) * 8,
        check_vma=False,
    )
```

```python
import functools
import math

import jax
import jax.numpy as jnp
from jax import lax
from jax.experimental import pallas as pl
from jax.experimental.pallas import tpu as pltpu
from jax.sharding import Mesh
from jax.sharding import PartitionSpec as P

HEADS = 16
HEAD_DIM = 64
EPSILON = 1e-05
NEGATIVE = -1e30
LOG2E = math.log2(math.e)
AXES = ("j", "h", "c", "a", "b")
BF = jnp.bfloat16
F32 = jnp.float32
NT = (((1,), (1,)), ((), ()))
NN = (((1,), (0,)), ((), ()))
TN = (((0,), (0,)), ((), ()))


def cost(us):
    return pl.CostEstimate(flops=int(us * 1e6), bytes_accessed=1 << 10, transcendentals=0)


def dot(left, right, dims=NN):
    return lax.dot_general(left, right, dims, preferred_element_type=F32)


def qkv_kernel(table, order, *refs, group, shape):
    x_refs, w_refs = refs[:group], refs[group:-9]
    vec_ref, cos_ref, sin_ref, n_ref, q_ref, k_ref, v_ref, w_ref, held = refs[-9:]
    step = pl.program_id(0)

    @pl.when(step == 0)
    def _():
        if shape is None:
            w_ref[...] = w_refs[0][...]
            return
        na, nb, part = shape
        sources = w_refs[0].shape[0]
        for n in range(len(w_refs) * sources):
            j, a = order[n] // na, order[n] % na
            for m in range(group):
                row = ((j * (group // nb) + m // nb) * na + a) * nb + m % nb
                start = pl.multiple_of(row * part, part)
                block = w_refs[n // sources][n % sources, m * part : (m + 1) * part, :]
                w_ref[pl.ds(start, part), :] = block

    for n in range(group):

        @pl.when(step // 2 == n)
        def _(n=n):
            held[...] = x_refs[n][step % 2]

    x = held[...].astype(F32)
    center = x - jnp.mean(x, axis=1, keepdims=True)
    rstd = lax.rsqrt(jnp.mean(center * center, axis=1, keepdims=True) + EPSILON)
    normed = (center * rstd * vec_ref[0:1] + vec_ref[1:2]).astype(BF)
    n_ref[...] = normed
    full = dot(normed, w_ref[...])
    lane = lax.broadcasted_iota(jnp.int32, (1, 128), 1)
    first = (lane % HEAD_DIM) < HEAD_DIM // 2
    cosine, sine = cos_ref[...], sin_ref[...]
    for pair in range(q_ref.shape[1] // 128):
        at = slice(pair * 128, (pair + 1) * 128)
        for which, out, scale in ((0, q_ref, LOG2E * HEAD_DIM**-0.5), (1, k_ref, 1.0)):
            t = full[:, (3 * pair + which) * 128 : (3 * pair + which + 1) * 128]
            other = jnp.where(first, pltpu.roll(t, 96, 1), pltpu.roll(t, 32, 1))
            out[:, at] = ((t * cosine + other * sine) * scale).astype(BF)
        v_ref[:, at] = full[:, (3 * pair + 2) * 128 : (3 * pair + 3) * 128].astype(BF)


def qkv_call(table, order, pieces, w, vec, cosine, sine, shape):
    group = len(pieces)
    _, rows, model = pieces[0].shape
    width = model // group
    length = 2 * group * rows
    at = lambda i, *t: (t[0][i], 0)
    fixed = lambda shape: pl.BlockSpec(
        shape, lambda i, *t: (0,) * len(shape), pipeline_mode=pl.Buffered(1)
    )
    return pl.pallas_call(
        functools.partial(qkv_kernel, group=group, shape=shape),
        out_shape=[jax.ShapeDtypeStruct((length, model), BF)]
        + [jax.ShapeDtypeStruct((length, width), BF)] * 3
        + [jax.ShapeDtypeStruct((model, 3 * width), BF)],
        grid_spec=pltpu.PrefetchScalarGridSpec(
            num_scalar_prefetch=2,
            grid=(2 * group,),
            in_specs=[fixed((2, rows, model))] * group
            + [fixed(x.shape) for x in (*w, vec)]
            + [pl.BlockSpec((rows, 128), at)] * 2,
            out_specs=[pl.BlockSpec((rows, model), at)]
            + [pl.BlockSpec((rows, width), at)] * 3
            + [fixed((model, 3 * width))],
            scratch_shapes=[pltpu.VMEM((rows, model), BF)],
        ),
        compiler_params=pltpu.CompilerParams(
            dimension_semantics=("arbitrary",), vmem_limit_bytes=60 << 20
        ),
        cost_estimate=cost(11),
        name="qkv",
    )(table, order, *pieces, *w, vec, cosine, sine)


def forward_kernel(table, q_ref, k_ref, v_ref, o_ref, lse_ref, vaug, *, bq, bk, rows):
    i = pl.program_id(1)
    lane = lax.broadcasted_iota(jnp.int32, (1, 128), 1)
    low = lane < HEAD_DIM

    @pl.when(i == 0)
    def _():
        v = v_ref[...]
        one = jnp.ones_like(v)
        vaug[0] = jnp.where(low, v, one)
        vaug[1] = jnp.where(low, one, v)

    parts = bq // bk
    heads = []
    for n in range(parts):
        q = q_ref[n * bk : (n + 1) * bk, :]
        zero = jnp.zeros_like(q)
        heads.append((jnp.where(low, q, zero), jnp.where(low, zero, q)))

    def step(kb, carry, first, masked):
        start = pl.multiple_of(kb * bk, bk)
        k_blk = k_ref[pl.ds(start, bk), :]
        out = list(carry)
        for n in range(first, parts):
            for h in range(2):
                top, acc = carry[2 * n + h]
                s = dot(heads[n][h], k_blk, NT)
                if masked and n == first:
                    row = lax.broadcasted_iota(jnp.int32, s.shape, 0)
                    col = lax.broadcasted_iota(jnp.int32, s.shape, 1)
                    s = jnp.where(col <= row, s, NEGATIVE)
                new = jnp.maximum(top, jnp.max(s, axis=1, keepdims=True))
                p = jnp.exp2(s - new)
                acc = acc * jnp.exp2(top - new) + dot(p.astype(BF), vaug[h, pl.ds(start, bk), :])
                out[2 * n + h] = (new, acc)
        return tuple(out)

    carry = tuple(
        (jnp.full((bk, 1), NEGATIVE, F32), jnp.zeros((bk, 128), F32)) for _ in range(2 * parts)
    )
    full = i * parts
    carry = lax.fori_loop(0, full, lambda kb, c: step(kb, c, 0, False), carry)
    for d in range(parts):
        carry = step(full + d, carry, d, True)
    for n in range(parts):
        (top0, acc0), (top1, acc1) = carry[2 * n : 2 * n + 2]
        total = pltpu.roll(jnp.where(low, acc1, acc0), HEAD_DIM, 1)
        o = (jnp.where(low, acc0, acc1) / total).astype(BF)
        for d in range(bk // rows):
            o_ref[table[(full + n) * (bk // rows) + d]] = o[d * rows : (d + 1) * rows]
        lse_ref[n * bk : (n + 1) * bk, :] = jnp.where(low, top0, top1) + jnp.log2(total)


def attention_forward(table, q, k, v, rows):
    length, width = q.shape
    bq, bk = min(2048, length), min(512, length)
    blocks = length // rows
    return pl.pallas_call(
        functools.partial(forward_kernel, bq=bq, bk=bk, rows=rows),
        out_shape=[
            jax.ShapeDtypeStruct((blocks, rows, width), BF),
            jax.ShapeDtypeStruct((length, width), F32),
        ],
        grid_spec=pltpu.PrefetchScalarGridSpec(
            num_scalar_prefetch=1,
            grid=(width // 128, length // bq),
            in_specs=[
                pl.BlockSpec((bq, 128), lambda p, i, t: (i, p)),
                pl.BlockSpec((length, 128), lambda p, i, t: (0, p)),
                pl.BlockSpec((length, 128), lambda p, i, t: (0, p)),
            ],
            out_specs=[
                pl.BlockSpec((blocks, rows, 128), lambda p, i, t: (0, 0, p)),
                pl.BlockSpec((bq, 128), lambda p, i, t: (i, p)),
            ],
            scratch_shapes=[pltpu.VMEM((2, length, 128), BF)],
        ),
        compiler_params=pltpu.CompilerParams(
            dimension_semantics=("arbitrary", "arbitrary"), vmem_limit_bytes=60 << 20
        ),
        cost_estimate=cost(23),
        name="attention_forward",
    )(table, q, k, v)


def split3(x):
    high = x.astype(BF)
    rest = x - high.astype(F32)
    mid = rest.astype(BF)
    return high, mid, (rest - mid.astype(F32)).astype(BF)


def backward_kernel(
    table, q_ref, k_ref, v_ref, o_ref, do_ref, lse_ref, cos_ref, sin_ref, ck_ref, sk_ref,
    d_ref, qa, da, dqt, *, bk, rows
):
    j = pl.program_id(0)
    length = q_ref.shape[0]
    lane = lax.broadcasted_iota(jnp.int32, (1, 128), 1)
    low = lane < HEAD_DIM
    first = (lane % HEAD_DIM) < HEAD_DIM // 2

    def unturn(t, cosine, sine):
        other = jnp.where(first, pltpu.roll(t, 96, 1), pltpu.roll(t, 32, 1))
        return t * cosine - other * sine

    @pl.when(j == 0)
    def _():
        dqt[...] = jnp.zeros_like(dqt)

        def prep(b, _):
            r = pl.ds(pl.multiple_of(b * rows, rows), rows)
            q, do = q_ref[r, :], do_ref[table[b]]
            product = o_ref[table[b]].astype(F32) * do.astype(F32)
            for h in range(2):
                mine = low if h == 0 else jnp.logical_not(low)
                base = HEAD_DIM if h == 0 else 0
                delta = -jnp.sum(jnp.where(mine, product, 0.0), axis=1, keepdims=True)
                lse = -lse_ref[r, HEAD_DIM * h : HEAD_DIM * h + 1]
                for source, value, target in ((q, lse, qa), (do, delta, da)):
                    x = jnp.where(mine, source, jnp.zeros_like(source))
                    for n, part in enumerate(split3(value)):
                        x = jnp.where(lane == base + n, part, x)
                    target[h, r, :] = x
            return 0

        lax.fori_loop(0, length // rows, prep, 0)

    k, v = k_ref[...], v_ref[...]
    one, zero = jnp.ones_like(k), jnp.zeros_like(k)
    ka, va, kt = [], [], []
    for h in range(2):
        mine = low if h == 0 else jnp.logical_not(low)
        base = HEAD_DIM if h == 0 else 0
        extra = jnp.where(jnp.logical_and(lane >= base, lane < base + 3), one, zero)
        ka.append(jnp.where(mine, k, extra))
        va.append(jnp.where(mine, v, extra))
        kt.append(jnp.where(mine, k, zero).T)

    def products(h, keys, r, masked):
        qh, dh = qa[h, r, :], da[h, r, :]
        st = dot(ka[h][keys], qh, NT)
        if masked:
            key = lax.broadcasted_iota(jnp.int32, st.shape, 0)
            query = lax.broadcasted_iota(jnp.int32, st.shape, 1)
            st = jnp.where(key <= query, st, NEGATIVE)
        p = jnp.exp2(st)
        ds = (p * dot(va[h][keys], dh, NT)).astype(BF)
        return dot(ds, qh), dot(p.astype(BF), dh), ds

    def step(qb, carry):
        r = pl.ds(pl.multiple_of(qb * bk, bk), bk)
        out, low_scores = [], []
        for h in range(2):
            dk, dv, ds = products(h, slice(None), r, False)
            out.append((carry[h][0] + dk, carry[h][1] + dv))
            low_scores.append(ds)
        dqt[:, r] += dot(kt[0], low_scores[0]) + dot(kt[1], low_scores[1])
        return tuple(out)

    half = bk // 2
    carry = []
    upper = pl.ds(pl.multiple_of(j * bk, bk), bk)
    lower = pl.ds(pl.multiple_of(j * bk + half, half), half)
    firsts = [products(h, slice(0, half), upper, True) for h in range(2)]
    seconds = [products(h, slice(half, bk), lower, True) for h in range(2)]
    for h in range(2):
        carry.append(
            tuple(jnp.concatenate([firsts[h][n], seconds[h][n]], axis=0) for n in range(2))
        )
    dqt[:, upper] += dot(kt[0][:, :half], firsts[0][2]) + dot(kt[1][:, :half], firsts[1][2])
    dqt[:, lower] += dot(kt[0][:, half:], seconds[0][2]) + dot(kt[1][:, half:], seconds[1][2])
    carry = lax.fori_loop(j + 1, length // bk, step, tuple(carry))
    (dk0, dv0), (dk1, dv1) = carry
    dk = unturn(jnp.where(low, dk0, dk1) * (1.0 / LOG2E), ck_ref[...], sk_ref[...])
    mine = pl.ds(pl.multiple_of(j * bk, bk), bk)
    d_ref[mine, 128:256] = dk.astype(BF)
    d_ref[mine, 256:384] = jnp.where(low, dv0, dv1).astype(BF)

    @pl.when(j == pl.num_programs(0) - 1)
    def _():
        dq = dqt[...].T * HEAD_DIM**-0.5
        d_ref[:, 0:128] = unturn(dq, cos_ref[...], sin_ref[...]).astype(BF)


def attention_backward(table, pair, q, k, v, o, do, lse, cosine, sine):
    length = q.shape[0]
    blocks, rows, _ = o.shape
    bk = min(512, length)
    full = pl.BlockSpec((length, 128), lambda j, t: (0, pair))
    block = pl.BlockSpec((bk, 128), lambda j, t: (j, pair))
    loose = pl.BlockSpec((blocks, rows, 128), lambda j, t: (0, 0, pair))
    return pl.pallas_call(
        functools.partial(backward_kernel, bk=bk, rows=rows),
        out_shape=jax.ShapeDtypeStruct((length, 384), BF),
        grid_spec=pltpu.PrefetchScalarGridSpec(
            num_scalar_prefetch=1,
            grid=(length // bk,),
            in_specs=[
                full, block, block, loose, loose, full,
                pl.BlockSpec((length, 128), lambda j, t: (0, 0)),
                pl.BlockSpec((length, 128), lambda j, t: (0, 0)),
                pl.BlockSpec((bk, 128), lambda j, t: (j, 0)),
                pl.BlockSpec((bk, 128), lambda j, t: (j, 0)),
            ],
            out_specs=pl.BlockSpec((length, 384), lambda j, t: (0, 0)),
            scratch_shapes=[
                pltpu.VMEM((2, length, 128), BF),
                pltpu.VMEM((2, length, 128), BF),
                pltpu.VMEM((128, length), F32),
            ],
        ),
        compiler_params=pltpu.CompilerParams(
            dimension_semantics=("arbitrary",), vmem_limit_bytes=56 << 20
        ),
        cost_estimate=cost(44),
        name="attention_backward",
    )(table, q, k, v, o, do, lse, cosine, sine, cosine, sine)


def gelu(v):
    return 0.5 * v * (1.0 + jnp.tanh(0.7978845608 * (v + 0.044715 * v * v * v)))


def gelu_slope(v):
    square = v * v
    t = jnp.tanh(0.7978845608 * v * (1.0 + 0.044715 * square))
    inner = 0.7978845608 * (1.0 + 3.0 * 0.044715 * square)
    return 0.5 * (1.0 + t) + 0.5 * v * (1.0 - t * t) * inner


def take(step, refs, held):
    for n, ref in enumerate(refs):

        @pl.when(step == n)
        def _(ref=ref):
            held[...] = ref[...].reshape(held.shape)

    return held[...]


def load_up(order, refs, up):
    pieces, (sources, rows, unit) = len(refs) // 2, refs[0].shape
    part, total = rows // 2, pieces * sources
    per = total // (up.shape[1] // unit)
    for which in range(2):
        for n in range(total):
            source = order[which, n]
            ref = refs[which * pieces + n // sources]
            base = (source // per) * 2 * per + source % per
            for c in range(2):
                start = pl.multiple_of((base + c * per) * part, part)
                up[pl.ds(start, part), which * unit : (which + 1) * unit] = ref[
                    n % sources, c * part : (c + 1) * part, :
                ]


def load_down(order, refs, down):
    at = 0
    for ref in refs:
        deep = ref.shape[1]
        for n in range(ref.shape[0]):
            down[pl.ds(pl.multiple_of(order[2, at] * deep, deep), deep), :] = ref[n]
            at += 1


def mlp_up_kernel(*refs, tables):
    pre_ref, act_ref, held = refs[tables + 2 :][-(3 + tables) :][:3]
    x_refs, weights = refs[tables : tables + 2], refs[tables + 2 : -(3 + tables)]
    up = weights[0]
    if tables:
        up = refs[-1]

        @pl.when(pl.program_id(0) == 0)
        def _():
            load_up(refs[0], weights, up)

    x = take(pl.program_id(0), x_refs, held)
    for n in range(up.shape[1] // x.shape[1]):
        at = slice(n * x.shape[1], (n + 1) * x.shape[1])
        pre = dot(x, up[:, at])
        pre_ref[:, at] = pre.astype(BF)
        act_ref[:, at] = gelu(pre).astype(BF)


def leave(total, own_ref, other_ref):
    @pl.when(pl.program_id(0) == 0)
    def _():
        own_ref[...] = total

    @pl.when(pl.program_id(0) == 1)
    def _():
        other_ref[...] = total.astype(BF)


def mlp_down_kernel(*refs, tables):
    act_ref, weights = refs[tables], refs[tables + 1 : -(2 + tables)]
    own_ref, other_ref = refs[tables + 1 :][-(2 + tables) :][:2]
    down = weights[0]
    if tables:
        down = refs[-1]

        @pl.when(pl.program_id(0) == 0)
        def _():
            load_down(refs[0], weights, down)

    leave(dot(act_ref[...], down[...]), own_ref, other_ref)


def mlp_backward_kernel(*refs, tables):
    g_refs, pre_ref, weights = refs[tables : tables + 2], refs[tables + 2], refs[tables + 3 : -(4 + 2 * tables)]
    low_ref, own_ref, other_ref, held = refs[tables + 3 :][-(4 + 2 * tables) :][:4]
    up, down = weights[0], weights[-1]
    if tables:
        up, down = refs[-2:]

        @pl.when(pl.program_id(0) == 0)
        def _():
            load_up(refs[0], weights[:4], up)
            load_down(refs[0], weights[4:], down)

    g = take(pl.program_id(0), g_refs, held)
    total = None
    for n in range(up.shape[1] // g.shape[1]):
        at = slice(n * g.shape[1], (n + 1) * g.shape[1])
        grad = dot(g, down[at, :], NT)
        low = (grad * gelu_slope(pre_ref[:, at].astype(F32))).astype(BF)
        low_ref[:, at] = low
        term = dot(low, up[:, at], NT)
        total = term if total is None else total + term
    leave(total, own_ref, other_ref)


def mlp_call(kernel, name, us, narrow, wide, weights, tables, scratch, wide_outs, split):
    count = (narrow or wide)[0].shape[0] if narrow else wide[0].shape[0] // 2
    model = weights[0][0].shape[-1] if tables else min(weights[0][0].shape)
    units = 2 * model if tables else max(weights[0][0].shape)
    fixed = lambda shape: pl.BlockSpec(
        shape, lambda m, *t: (0,) * len(shape), pipeline_mode=pl.Buffered(1)
    )
    wide_spec = pl.BlockSpec((count, units), lambda m, *t: (m, 0))
    return pl.pallas_call(
        functools.partial(kernel, tables=len(tables)),
        out_shape=[jax.ShapeDtypeStruct((2 * count, units), BF)] * wide_outs
        + [jax.ShapeDtypeStruct((count, model), kind) for kind in (F32, BF) if split],
        grid_spec=pltpu.PrefetchScalarGridSpec(
            num_scalar_prefetch=len(tables),
            grid=(2,),
            in_specs=[fixed((count, model))] * len(narrow)
            + [wide_spec] * len(wide)
            + [fixed(x.shape[:-2] + (rows, x.shape[-1])) for x, rows in weights],
            out_specs=[wide_spec] * wide_outs + [fixed((count, model))] * (2 * split),
            scratch_shapes=[pltpu.VMEM((count, model), BF)] * bool(narrow)
            + [pltpu.VMEM(shape, BF) for shape in scratch if tables],
        ),
        compiler_params=pltpu.CompilerParams(
            dimension_semantics=("arbitrary",), vmem_limit_bytes=56 << 20
        ),
        cost_estimate=cost(us),
        name=name,
    )(*tables, *narrow, *wide, *[x for x, _ in weights])


def relay_kernel(here, *refs, layout, arrivals):
    count = sum(len(pieces) for _, pieces in layout)
    kept, came = refs[:count], refs[count : count + arrivals]
    outs, given = refs[count + arrivals : 2 * count + arrivals], refs[2 * count + arrivals :]
    at = 0
    for g, (n, pieces) in enumerate(layout):
        mine = here[g]
        for start, source, offset in pieces:
            width = kept[at].shape[3]
            for i in range(n):
                for keep in (True, False):
                    half = mine if keep else 1 - mine
                    x = kept[at][i, half].astype(F32)
                    x = x + came[source][i, half, :, offset : offset + width].astype(F32)
                    if keep:
                        outs[at][i] = x.astype(BF)
                    else:
                        given[g][i, :, start : start + width] = x.astype(BF)
            at += 1


def relay(groups, fused):
    if not fused:
        results = []
        for here, (n, halves, m), pieces in groups:
            kept, given = [], []
            for x, came, offset in pieces:
                width = x.shape[-1]
                x = x.reshape(-1, width)
                if came is not None:
                    x = join(x, came.reshape(-1, came.shape[-1])[:, offset : offset + width])
                if x.shape[0] != n * halves * m:
                    x = scatter_axis(x.reshape(lax.axis_size("h"), -1, width), "h", 0)
                x = x.reshape(n, halves, m, width)
                mine = 0 if here is None else here
                kept.append(lax.dynamic_index_in_dim(x, mine, 1, keepdims=False))
                if here is not None:
                    given.append(lax.dynamic_index_in_dim(x, 1 - here, 1, keepdims=False))
            results.append((kept, jnp.concatenate(given, axis=-1) if given else None))
        return results
    kept, came, layout, widths = [], [], [], []
    for _, (n, halves, m), pieces in groups:
        start, entries = 0, []
        for x, arrived, offset in pieces:
            kept.append(x.reshape(n, halves, m, x.shape[-1]))
            if not any(arrived is y for y, _ in came):
                came.append((arrived, (n, halves, m, arrived.shape[-1])))
            source = [arrived is y for y, _ in came].index(True)
            entries.append((start, source, offset))
            start += x.shape[-1]
        layout.append((n, tuple(entries)))
        widths.append((n, m, start))
    came = [y.reshape(shape) for y, shape in came]
    shapes = [(x.shape[0],) + x.shape[2:] for x in kept] + widths
    fixed = lambda shape: pl.BlockSpec(
        tuple(shape), lambda i, t: (0,) * len(shape), pipeline_mode=pl.Buffered(1)
    )
    outs = pl.pallas_call(
        functools.partial(relay_kernel, layout=tuple(layout), arrivals=len(came)),
        out_shape=[jax.ShapeDtypeStruct(shape, BF) for shape in shapes],
        grid_spec=pltpu.PrefetchScalarGridSpec(
            num_scalar_prefetch=1,
            grid=(1,),
            in_specs=[fixed(x.shape) for x in kept + came],
            out_specs=[fixed(shape) for shape in shapes],
        ),
        compiler_params=pltpu.CompilerParams(
            dimension_semantics=("arbitrary",), vmem_limit_bytes=60 << 20
        ),
        cost_estimate=cost(4),
        name="relay",
    )(jnp.stack([here for here, *_ in groups]), *kept, *came)
    results, at = [], 0
    for g, (_, entries) in enumerate(layout):
        results.append((list(outs[at : at + len(entries)]), outs[len(kept) + g]))
        at += len(entries)
    return results


def spread_of(values):
    center = values - jnp.mean(values, axis=1, keepdims=True)
    rstd = lax.rsqrt(jnp.mean(center * center, axis=1, keepdims=True) + EPSILON)
    return center * rstd, rstd


def norm_slope(hat, rstd, gain, grad, sums_ref, at):
    scaled = grad * gain
    inner = scaled - jnp.mean(scaled, axis=1, keepdims=True)
    sums_ref[at : at + 1] += jnp.sum(grad * hat, axis=0, keepdims=True)
    sums_ref[at + 1 : at + 2] += jnp.sum(grad, axis=0, keepdims=True)
    return rstd * (inner - hat * jnp.mean(scaled * hat, axis=1, keepdims=True))


def clear_at_start(ref):
    @pl.when(pl.program_id(0) == 0)
    def _():
        ref[...] = jnp.zeros_like(ref)


def pick_kernel(*refs):
    out = refs[-1]
    sources, cut, _ = refs[0].shape
    for n, ref in enumerate(refs[:-1]):
        which, piece = divmod(n, (len(refs) - 1) // 2)
        out[piece * sources : (piece + 1) * sources, which * cut : (which + 1) * cut] = ref[...]


def pick(arrays, cut):
    sources, wide, model = arrays[0].shape
    spec = pl.BlockSpec((sources, cut, model), lambda i: (0, wide // cut - 1, 0))
    shape = (sources * len(arrays) // 2, 2 * cut, model)
    return pl.pallas_call(
        pick_kernel,
        out_shape=jax.ShapeDtypeStruct(shape, BF),
        grid=(1,),
        in_specs=[spec] * len(arrays),
        out_specs=pl.BlockSpec(shape, lambda i: (0, 0, 0)),
        cost_estimate=cost(2),
        name="pick",
    )(*arrays)


def out_kernel(order, places, *refs, group, views):
    projected_ref, residual_ref, normed_ref, w_ref, held = refs[-5:]
    mixed, tokens, vec_ref, weights = refs[:group], refs[group : group + 2], refs[group + 2], refs[group + 3 : -5]
    step = pl.program_id(0)

    @pl.when(step == 0)
    def _():
        if not views:
            w_ref[...] = weights[0][...]
            return
        sources, cut = weights[0].shape[0], weights[0].shape[1] // 2
        halves = places.shape[0] // 2
        per = sources // halves
        for which in range(2):
            for n in range(sources):
                source = order[which, n]
                start = pl.multiple_of((source % per) * 2 * cut + which * cut, cut)
                for core in range(2):
                    block = places[core * halves + source // per]
                    w_ref[block, pl.ds(start, cut), :] = weights[core][n, which * cut : (which + 1) * cut]

    projected = dot(mixed[0][...], w_ref[0])
    for d in range(1, group):
        projected = projected + dot(mixed[d][...], w_ref[d])
    projected_ref[...] = projected
    hat, _ = spread_of(projected)
    x = take(step, tokens, held).astype(F32)
    residual = x + hat * vec_ref[2:3] + vec_ref[3:4]
    residual_ref[...] = residual
    hat, _ = spread_of(residual)
    normed_ref[...] = (hat * vec_ref[4:5] + vec_ref[5:6]).astype(BF)


def out_projection(order, places, mixed, tokens, vec, weights, views):
    group = len(mixed)
    count, width = mixed[0].shape
    rows, model = tokens[0].shape
    fixed = lambda shape: pl.BlockSpec(shape, lambda i, *t: (0,) * len(shape))
    tall = pl.BlockSpec((rows, model), lambda i, *t: (i, 0))
    specs = [fixed(x.shape) for x in weights]
    return pl.pallas_call(
        functools.partial(out_kernel, group=group, views=views),
        out_shape=[
            jax.ShapeDtypeStruct((count, model), F32),
            jax.ShapeDtypeStruct((count, model), F32),
            jax.ShapeDtypeStruct((count, model), BF),
            jax.ShapeDtypeStruct((group, width, model), BF),
        ],
        grid_spec=pltpu.PrefetchScalarGridSpec(
            num_scalar_prefetch=2,
            grid=(count // rows,),
            in_specs=[pl.BlockSpec((rows, width), lambda i, *t: (i, 0))] * group
            + [fixed((rows, model))] * 2
            + [fixed(vec.shape)]
            + specs,
            out_specs=[tall, tall, tall, fixed((group, width, model))],
            scratch_shapes=[pltpu.VMEM((rows, model), BF)],
        ),
        compiler_params=pltpu.CompilerParams(
            dimension_semantics=("arbitrary",), vmem_limit_bytes=40 << 20
        ),
        cost_estimate=cost(5),
        name="out_projection",
    )(order, places, *mixed, *tokens, vec, *weights)


def middle_kernel(own_ref, came_ref, residual_ref, g0_ref, g1_ref, vec_ref, out_ref, low_ref, sums_ref, held):
    clear_at_start(sums_ref)
    hat, rstd = spread_of(own_ref[...] + came_ref[...].astype(F32))
    out_ref[...] = (residual_ref[...] + hat * vec_ref[6:7] + vec_ref[7:8]).astype(BF)
    grad = take(pl.program_id(0), (g0_ref, g1_ref), held).astype(F32)
    low_ref[...] = norm_slope(hat, rstd, vec_ref[6:7], grad, sums_ref, 6).astype(BF)


def turn_kernel(own_ref, came_ref, residual_ref, projected_ref, g0_ref, g1_ref, vec_ref, w_ref, *refs, group):
    grad_ref, low_ref, *heads, sums_ref, held = refs
    clear_at_start(sums_ref)
    hat, rstd = spread_of(residual_ref[...])
    grad = own_ref[...] + came_ref[...].astype(F32)
    passed = take(pl.program_id(0), (g0_ref, g1_ref), held).astype(F32)
    grad = passed + norm_slope(hat, rstd, vec_ref[4:5], grad, sums_ref, 4)
    grad_ref[...] = grad
    hat, rstd = spread_of(projected_ref[...])
    low = norm_slope(hat, rstd, vec_ref[2:3], grad, sums_ref, 2).astype(BF)
    low_ref[...] = low
    for d in range(group):
        heads[d][...] = dot(low, w_ref[d], NT).astype(BF)


def last_kernel(x_ref, grad_ref, *refs):
    *parts, vec_ref, out_ref, sums_ref = refs
    clear_at_start(sums_ref)
    hat, rstd = spread_of(x_ref[...].astype(F32))
    grad = parts[0][...].astype(F32)
    for part in parts[1:]:
        grad = grad + part[...].astype(F32)
    grad = norm_slope(hat, rstd, vec_ref[0:1], grad, sums_ref, 0)
    out_ref[...] = (grad_ref[...] + grad).astype(BF)


def row_call(kernel, name, us, rows, tall, halves, fixed, outs, limit=40):
    model = tall[0].shape[1]
    count = tall[0].shape[0]
    starts = [at[1] if isinstance(at, tuple) else 0 for at in tall]
    tall = [at[0] if isinstance(at, tuple) else at for at in tall]
    whole = lambda x: pl.BlockSpec(x.shape, lambda i, n=x.ndim: (0,) * n)
    block = lambda width: pl.BlockSpec((rows, width), lambda i: (i, 0))
    return pl.pallas_call(
        kernel,
        out_shape=[jax.ShapeDtypeStruct((count, width), kind) for width, kind in outs]
        + [jax.ShapeDtypeStruct((8, model), F32)],
        grid=(count // rows,),
        in_specs=[
            pl.BlockSpec((rows, model), lambda i, start=start: (i + start, 0)) for start in starts
        ]
        + [whole(x) for x in (*halves, *fixed)],
        out_specs=[block(width) for width, _ in outs] + [pl.BlockSpec((8, model), lambda i: (0, 0))],
        scratch_shapes=[pltpu.VMEM((rows, model), BF)] if halves else [],
        compiler_params=pltpu.CompilerParams(
            dimension_semantics=("arbitrary",), vmem_limit_bytes=limit << 20
        ),
        cost_estimate=cost(us),
        name=name,
    )(*tall, *halves, *fixed)


def input_grad_kernel(table, *refs):
    w_ref, give_ref, keep_ref = refs[-3:]
    total = None
    for n, ref in enumerate(refs[:-3]):
        term = dot(ref[...], w_ref[:, n * 384 : (n + 1) * 384], NT)
        total = term if total is None else total + term
    giving = pl.program_id(0) < pl.num_programs(0) // 2

    @pl.when(giving)
    def _():
        give_ref[0] = total.astype(BF)

    @pl.when(jnp.logical_not(giving))
    def _():
        keep_ref[0] = total.astype(BF)


def input_grad(table, grads, w, rows):
    model = w.shape[0]
    blocks = grads[0].shape[0] // rows
    half = blocks // 2
    return pl.pallas_call(
        input_grad_kernel,
        out_shape=[jax.ShapeDtypeStruct((half, rows, model), BF)] * 2,
        grid_spec=pltpu.PrefetchScalarGridSpec(
            num_scalar_prefetch=1,
            grid=(blocks,),
            in_specs=[pl.BlockSpec((rows, 384), lambda i, t: (t[i], 0))] * len(grads)
            + [pl.BlockSpec(w.shape, lambda i, t: (0, 0))],
            out_specs=[
                pl.BlockSpec((1, rows, model), lambda i, t: (jnp.minimum(i, half - 1), 0, 0)),
                pl.BlockSpec((1, rows, model), lambda i, t: (jnp.maximum(i - half, 0), 0, 0)),
            ],
        ),
        compiler_params=pltpu.CompilerParams(
            dimension_semantics=("arbitrary",), vmem_limit_bytes=40 << 20
        ),
        cost_estimate=cost(6),
        name="input_grad",
    )(table, *grads, w)


def head_sum_kernel(*refs, group, spread):
    x_refs, outs = refs[:-3], refs[-3:]
    width = outs[0].shape[1] // group
    for m in range(group):
        for pair, ref in enumerate(x_refs):
            total = None
            for n in spread(m):
                term = ref[n].astype(F32)
                total = term if total is None else total + term
            at = slice(m * width + pair * 128, m * width + (pair + 1) * 128)
            for which, out in enumerate(outs):
                out[:, at] = total[:, which * 128 : (which + 1) * 128]


def head_sum(parts, group, spread):
    _, rows, wide = parts[0].shape
    return pl.pallas_call(
        functools.partial(head_sum_kernel, group=group, spread=spread),
        out_shape=[jax.ShapeDtypeStruct((rows, group * len(parts) * wide // 3), F32)] * 3,
        cost_estimate=cost(2),
        name="head_sum",
    )(*parts)


def flip(x, axis, bit):
    size = lax.axis_size(axis)
    return lax.ppermute(x, axis, [(i, i ^ bit) for i in range(size)])


def scatter_sends(x, axis, dim, bit):
    here = (lax.axis_index(axis) // bit) % 2
    shape = x.shape
    x = x.reshape(shape[:dim] + (shape[dim] // 2, 2) + shape[dim + 1 :])
    mine = lax.dynamic_index_in_dim(x, here, dim + 1, keepdims=False)
    return mine, lax.dynamic_index_in_dim(x, 1 - here, dim + 1, keepdims=False)


def join(mine, came, kind=BF):
    return (mine.astype(F32) + came.astype(F32)).astype(kind)


def scatter_axis(x, axis, dim, bit=1, kind=BF):
    size = lax.axis_size(axis)
    while bit < size:
        mine, theirs = scatter_sends(x, axis, dim, bit)
        x = join(mine, flip(theirs, axis, bit), kind)
        bit *= 2
    return x.reshape(x.shape[:dim] + x.shape[dim + 1 :])


def together(*groups):
    flat, tree = jax.tree.flatten(groups)
    return jax.tree.unflatten(tree, lax.optimization_barrier(tuple(flat)))


def place_in(order):
    index = jnp.arange(order.shape[0], dtype=jnp.int32)
    return jnp.sum(jnp.where(order[:, None] == index[None, :], index[:, None], 0), axis=0)


def gather_order(axes):
    masks = {axis: [0] for axis in AXES}
    for axis in axes:
        bit = lax.axis_size(axis) // 2
        while bit:
            for name in AXES:
                step = bit if name == axis else 0
                masks[name] = masks[name] + [m ^ step for m in masks[name]]
            bit //= 2
    return {axis: jnp.array(masks[axis], jnp.int32) for axis in AXES}


def source_of(axes, along=("j", "h", "a", "b")):
    masks, total = gather_order(axes), 0
    for axis in along:
        total = total * lax.axis_size(axis) + (lax.axis_index(axis) ^ masks[axis])
    return total


def stages_of(axes):
    stages = []
    for axis in axes:
        bit = lax.axis_size(axis) // 2
        while bit:
            stages.append((axis, bit))
            bit //= 2
    return stages


def after(x, *others):
    return lax.optimization_barrier((x,) + others)[0]


def body(
    tokens, cotangent, w_query, w_key, w_value, w_output, w_up, w_down,
    attn_in_gain, attn_in_bias, attn_out_gain, attn_out_bias,
    mlp_in_gain, mlp_in_bias, mlp_out_gain, mlp_out_bias,
):
    _, rows, model = tokens.shape
    nh, na, nb = lax.axis_size("h"), lax.axis_size("a"), lax.axis_size("b")
    jh = 2 * nh
    devices = 4 * nh * na * nb
    group = 2 * nh * nb
    half = na // 2
    length = rows * na * nb
    width = model // group
    pairs = width // 128
    part = w_query.shape[0]
    ij, ih, ic, ia, ib = (lax.axis_index(axis) for axis in AXES)
    slot, parity = ia // half, ia % 2
    member = (ih * 2 + ic) * nb + ib

    def place(j, h, c, a, b):
        return (((j * nh + h) * 2 + c) * na + a) * nb + b

    everyone = [
        (j, h, c, a, b)
        for j in range(2)
        for h in range(nh)
        for c in range(2)
        for a in range(na)
        for b in range(nb)
    ]
    moves = ([], [])
    for turn in range(2):
        for j, h, c, a, b in everyone:
            to_h, to_c = divmod(a % half, 2)
            plane = (h * 2 + c) * 2 + (turn + a // half) % 2
            target = place(j, to_h, to_c, plane, b)
            moves[turn].append((place(j, h, c, a, b), target))

    def regroup(x, turn):
        x = lax.dynamic_index_in_dim(x, (turn + slot) % 2, 0, keepdims=False)
        return lax.ppermute(x, AXES, moves[turn])

    def restore(x, turn):
        return lax.ppermute(x, AXES, [(there, here) for here, there in moves[turn]])

    def ordered(first, second):
        swap = slot == 1
        return jnp.stack([jnp.where(swap, second, first), jnp.where(swap, first, second)])

    def by_offset(x, offset):
        sends = []
        for j, h, c, a, b in everyone:
            to_hc, to_b = divmod(((h * 2 + c) * nb + b) ^ offset, nb)
            sends.append((place(j, h, c, a, b), place(j, to_hc // 2, to_hc % 2, a, to_b)))
        return lax.ppermute(x, AXES, sends)

    core_bit = nb
    far_bits = [1 << n for n in range(group.bit_length() - 1) if (1 << n) != core_bit]

    ff = w_up.shape[1]
    unit = ff // (2 * jh)
    up_split = w_up.reshape(part, jh, 2, unit)
    up_mine = lax.dynamic_index_in_dim(up_split, ic, 2, keepdims=False)
    up_other = flip(lax.dynamic_index_in_dim(up_split, 1 - ic, 2, keepdims=False), "c", 1)
    up_rows = jnp.stack(
        [jnp.where(ic == 0, up_mine, up_other), jnp.where(ic == 0, up_other, up_mine)]
    )
    n_up, n_down = 2 * part * jh * unit // model, w_down.shape[0]
    views = unit == model and part % 32 == 0 and n_up == n_down
    up_rows = up_rows.transpose(2, 0, 1, 3).reshape(n_up, model)
    cut, cut_up, cut_out = n_down // 2, n_up // 2, part // 2

    line_stages = stages_of(("a",))
    low_axes, high_axes = ("b", "h", "j"), ("h", "j", "b")

    def grow(x, came):
        return jnp.concatenate([x, came])

    def grow_all(x, stages):
        for axis, bit in stages:
            x = grow(x, flip(x, axis, bit))
        return x

    first = [up_rows[:cut_up], w_output[:cut_out], up_rows[cut_up:], w_output[cut_out:]]
    first, second = jnp.concatenate(first)[None], w_down[None]

    columns = jnp.stack(
        [w.reshape(part, group, pairs, 128) for w in (w_query, w_key, w_value)], axis=3
    ).reshape(part, group, 3 * width)
    columns = columns.transpose(1, 0, 2)
    columns = lax.all_to_all(columns, ("h", "c", "b"), 0, 0, tiled=True)
    columns = columns.reshape(1, group * part, 3 * width)

    blocks = 2 * group
    index = jnp.arange(blocks, dtype=jnp.int32)
    table = (member ^ (index % group)) * 2 + (parity ^ (index // group))
    positions_of = (parity ^ (index % 2)) * group + (member ^ (index // 2))
    lane, first = together(jnp.arange(128, dtype=jnp.int32), first)
    frequency = jnp.exp(
        (lane % (HEAD_DIM // 2)).astype(F32) * (-2.0 * math.log(10000.0) / HEAD_DIM)
    )
    angles = jnp.arange(length, dtype=jnp.int32).astype(F32)[:, None] * frequency[None, :]
    cosine = jnp.cos(angles)
    sine = jnp.sin(angles) * jnp.where((lane // (HEAD_DIM // 2)) % 2 == 0, -1.0, 1.0)[None, :]

    vectors, columns = together(
        jnp.stack(
            [attn_in_gain, attn_in_bias, attn_out_gain, attn_out_bias,
             mlp_in_gain, mlp_in_bias, mlp_out_gain, mlp_out_bias]
        ),
        columns,
    )
    vectors = jnp.broadcast_to(vectors[None], (devices,) + vectors.shape)
    vectors = lax.all_to_all(vectors, AXES, 0, 0, tiled=True)
    vectors = vectors.transpose(1, 0, 2).reshape(8, model).astype(F32)

    def columns_in_order(x):
        x = x[place_in(w_from)].reshape(2, na, nh, 2, nb, part, 3 * width)
        return x.transpose(0, 2, 3, 1, 4, 5, 6).reshape(model, 3 * width)

    own = [regroup(tokens, turn) for turn in range(2)]
    first_came = flip(first, *line_stages[0])
    w_came = flip(columns, *line_stages[0])
    own, first_came, w_came, second, cosine, sine, vectors = together(
        own, first_came, w_came, second, cosine, sine, vectors
    )
    first = grow_all(grow(first, first_came), line_stages[1:])
    wide = cut_up + cut_out
    low_stages, high_stages = stages_of(low_axes), stages_of(high_axes)
    first_low, first_high = first[:, :wide], first[:, wide:]
    columns = grow_all(grow(columns, w_came), line_stages[1:-1])
    second_came, w_came = flip(second, *line_stages[0]), flip(columns, *line_stages[-1])
    high_came = flip(first_high, *high_stages[0])
    pieces = {0: jnp.stack(own)}
    for bit in far_bits:
        for offset in list(pieces):
            pieces[offset ^ bit] = by_offset(pieces[offset], bit)
    pieces[core_bit] = by_offset(pieces[0], core_bit)
    pieces, high_came, second_came, w_came = together(pieces, high_came, second_came, w_came)
    second = grow_all(grow(second, second_came), line_stages[1:-1])
    columns = grow(columns, w_came)

    w_came = flip(columns, "j", 1)
    w_from = source_of(("a", "j"), ("j", "a"))
    low_came, second_came = flip(first_low, *low_stages[0]), flip(second, *line_stages[-1])
    for offset in range(1, group):
        if not offset & core_bit:
            pieces[offset ^ core_bit] = by_offset(pieces[offset], core_bit)
    pieces, w_came, low_came, second_came = together(pieces, w_came, low_came, second_came)
    if views:
        w_heads, w_shape = [columns, w_came], (na, nb, part)
    else:
        w_heads, w_shape = [columns_in_order(grow(columns, w_came))], None
    first_low = grow_all(grow(first_low, low_came), low_stages[1:-1])
    first_high = grow_all(grow(first_high, high_came), high_stages[1:-1])
    second = grow(second, second_came)
    pieces, first_low, first_high, second = together(pieces, first_low, first_high, second)
    low_came, high_came = flip(first_low, *low_stages[-1]), flip(first_high, *high_stages[-1])
    seconds = [second]
    if views:
        seconds += [flip(second, "b", 1), flip(second, "j", 1)]
    normed, queries, keys, values, w_heads = qkv_call(
        positions_of, w_from, [pieces[d] for d in range(group)], w_heads, vectors,
        cosine, sine, w_shape,
    )
    grad_in = [regroup(cotangent, 0)]
    attended, lse = attention_forward(table, queries, keys, values, rows)
    attended, lse, low_came, high_came, grad_in, cotangent = together(
        attended, lse, low_came, high_came, grad_in, cotangent
    )
    first_low, first_high = [first_low, low_came], [first_high, high_came]
    if views:
        near = source_of(("a",))
        over_b, over_j = (near // nb) * nb + (near % nb ^ 1), near ^ (na * nb)
        over_both = over_b ^ (na * nb)
        down_from = jnp.concatenate([near, over_b, over_j, over_both])
    else:
        seconds = [grow_all(second, stages_of(("h", "j", "b")))]
        down_from = source_of(("a", "h", "j", "b"))
    low_from, high_from = (source_of(("a",) + axes) for axes in (low_axes, high_axes))

    def exchange(x):
        return [x[0]] + [by_offset(x[d], d) for d in range(1, group)]

    order = jnp.stack([low_from, high_from, down_from])
    low_at, high_at = place_in(low_from), place_in(high_from)
    core_block = jnp.arange(2 * jh, dtype=jnp.int32)
    if views:
        mine = pick(first_low + first_high, cut_out)
        out_weights = [mine, flip(mine, "c", 1)]
    else:
        mine = jnp.concatenate(
            [jnp.concatenate([x[:, cut_up:] for x in pair]) for pair in (first_low, first_high)],
            axis=1,
        )
        mine = jnp.concatenate([mine[:, :cut_out][low_at], mine[:, cut_out:][high_at]], axis=1)
        mine = mine.reshape(jh, na * nb * part, model)
        other = flip(mine, "c", 1)
        w_out = jnp.where(
            ic == 0, jnp.stack([mine, other], axis=1), jnp.stack([other, mine], axis=1)
        ).reshape(group, width, model)
        out_weights = [w_out[member ^ jnp.arange(group)]]
    places = member ^ ((core_block % jh) * 2 + (ic ^ (core_block // jh)))
    mixed = exchange(attended.reshape(group, 2 * rows, width))
    projected, residual, mlp_mine, w_out = out_projection(
        order, places, mixed, own, vectors, out_weights, views
    )
    mlp_rows = [mlp_mine, flip(mlp_mine, "c", 1)]
    if views:
        mlp_rows, seconds = together(mlp_rows, seconds)
        seconds += [flip(seconds[1][: na // 2], "j", 1), flip(seconds[2][na // 2 :], "b", 1)]
    if views:
        tables = [order]
        up_weights = [(x, 2 * part) for x in first_low + first_high]
    else:
        tables = []
        up = [jnp.concatenate([x[:, :cut_up] for x in pair]) for pair in (first_low, first_high)]
        up = jnp.concatenate([up[0][low_at], up[1][high_at]], axis=1)
        up = up.reshape(jh, na, nb, jh, 2, part, unit)
        up_weights = [(up.transpose(0, 4, 1, 2, 5, 3, 6).reshape(model, jh * unit), model)]
    grad_in.append(regroup(cotangent, 1))
    pre_act, activated = mlp_call(
        mlp_up_kernel, "mlp_up", 11, mlp_rows, [], up_weights, tables,
        [(model, jh * unit)], 2, False,
    )
    activated, grad_in, seconds = together(activated, grad_in, seconds)
    if views:
        down_weights = [(x, n_down) for x in seconds]
    else:
        down = seconds[0][place_in(down_from)]
        down_weights = [(down.reshape(jh * unit, model), jh * unit)]
    branch, branch_other = mlp_call(
        mlp_down_kernel, "mlp_down", 9, [], [activated], down_weights, tables,
        [(jh * unit, model)], 0, True,
    )
    block_loose, branch_mine, mo_sums = row_call(
        middle_kernel, "middle", 3, rows,
        [branch, flip(branch_other, "c", 1), residual], grad_in, [vectors],
        [(model, BF), (model, BF)],
    )
    branch_rows = [branch_mine, flip(branch_mine, "c", 1)]

    def sends(x, axis, dim):
        return scatter_sends(x, axis, dim, 1) if lax.axis_size(axis) > 1 else (x, None)

    def send(pair, axis):
        return None if pair[1] is None else flip(pair[1], axis, 1)

    def added(pair, came, shape):
        return (pair[0] if came is None else join(pair[0], came)).reshape(shape)

    def sends_of(arrays, axis, dim):
        kept, given = zip(*[sends(x, axis, dim) for x in arrays])
        return list(kept), None if given[0] is None else jnp.concatenate(given, axis=-1)

    def added_of(kept, came, shape):
        out, start = [], 0
        for x in kept:
            width = x.shape[-1]
            if came is not None:
                x = join(x, came[..., start : start + width])
            out.append(x.reshape(shape + (width,)))
            start += width
        return out

    down_part = dot(activated, jnp.concatenate(branch_rows), TN).astype(BF)
    down_part = down_part.reshape(2, nh, na, nb, n_down, model)
    low_sends = sends(down_part[..., :cut, :], "b", 3)
    high_sends = sends(down_part[..., cut:, :], "j", 0)
    branch_rows, low_sends, high_sends, block_loose = together(
        branch_rows, low_sends, high_sends, block_loose
    )
    half_b, halves_b = (ib if nb > 1 else None), min(nb, 2)
    low_bit, next_bit = ia % 2, (ia // 2) % 2
    low_came, high_came = send(low_sends, "b"), send(high_sends, "j")
    block_came = [restore(block_loose[:rows], 0), restore(block_loose[rows:], 1)]
    pre_low, grad_mlp, grad_other = mlp_call(
        mlp_backward_kernel, "mlp_backward", 20, branch_rows, [pre_act],
        up_weights + down_weights, tables, [(model, jh * unit), (jh * unit, model)], 1, True,
    )
    pre_low, grad_mlp, grad_other, low_came, high_came, block_came = together(
        pre_low, grad_mlp, grad_other, low_came, high_came, block_came
    )
    grad_other = flip(grad_other, "c", 1)
    low_sends, high_sends = relay(
        [
            (ij, (1, 2, nh * na * cut), [(low_sends[0], low_came, 0)]),
            (half_b, (nh * na, halves_b, cut), [(high_sends[0], high_came, 0)]),
        ],
        views,
    )
    grad_mlp, grad_other, low_sends, high_sends = together(
        grad_mlp, grad_other, low_sends, high_sends
    )
    low_came, high_came = send(low_sends, "j"), send(high_sends, "b")
    grad_residual, projected_low, *attended_low, turn_sums = row_call(
        functools.partial(turn_kernel, group=group), "turn", 6, rows,
        [grad_mlp, grad_other, residual, projected], grad_in, [vectors, w_out],
        [(model, F32), (model, BF)] + [(width, BF)] * group, limit=60,
    )
    attended_low, projected_low, pre_low, low_came, high_came, block_came = together(
        attended_low, projected_low, pre_low, low_came, high_came, block_came
    )
    grad_heads = exchange(attended_low)
    grad_heads[1], pre_low = together(grad_heads[1], pre_low)
    grad_heads = jnp.stack(grad_heads).reshape(blocks, rows, width)
    down_pieces = [(low_sends[0][0], low_came, 0), (high_sends[0][0], high_came, 0)]
    (down_sends,) = relay([(low_bit, (na // 2, 2, cut), down_pieces)], views)
    up_part = dot(jnp.concatenate(mlp_rows), pre_low, TN).astype(BF)
    up_part = up_part.reshape(2, nh, 2, na, nb, part, jh * unit)
    grad_out = jnp.stack([dot(mixed[d], projected_low, TN).astype(BF) for d in range(group)])
    grad_out = jnp.stack(
        [lax.dynamic_index_in_dim(grad_out, member ^ m, 0, keepdims=False) for m in range(group)]
    ).reshape(2, nh, 2, na, nb, part, model)
    grad_out = scatter_axis(grad_out, "c", 2)
    low_sends = sends_of([up_part[:, :, 0], grad_out[..., : model // 2]], "j", 0)
    high_sends = sends_of([up_part[:, :, 1], grad_out[..., model // 2 :]], "b", 3)
    grad_heads, down_sends, low_sends, high_sends = together(
        grad_heads, down_sends, low_sends, high_sends
    )

    def backward(pair, grads):
        return attention_backward(
            table, pair, queries, keys, values, attended, grads, lse, cosine, sine
        )

    units = jh * unit
    low_came, high_came = send(low_sends, "j"), send(high_sends, "b")
    down_came = send(down_sends, "a")
    grad_pairs = [backward(0, grad_heads)]
    grad_pairs, down_came, low_came, high_came = together(
        grad_pairs, down_came, low_came, high_came
    )
    weight_pairs = [dot(normed, grad_pairs[0], TN).astype(BF)]
    low_pieces = [(low_sends[0][0], low_came, 0), (low_sends[0][1], low_came, units)]
    high_pieces = [(high_sends[0][0], high_came, 0), (high_sends[0][1], high_came, units)]
    down_pieces = [(down_sends[0][0], down_came, 0), (down_sends[0][1], down_came, model)]
    low_sends, high_sends, down_sends = relay(
        [
            (half_b, (na, halves_b, part), low_pieces),
            (ij, (1, 2, nh * na * part), high_pieces),
            (next_bit, (na // 4, 2, cut), down_pieces),
        ],
        views,
    )
    heads_in = [
        lax.all_to_all(weight_pairs[0].reshape(devices, part, 384), AXES, 0, 0, tiled=True)
    ]
    if pairs > 1:
        grad_heads, down_sends, low_sends, high_sends, weight_pairs = together(
            grad_heads, down_sends, low_sends, high_sends, weight_pairs
        )
    down_came, low_came = flip(down_sends[1], "a", 2), send(low_sends, "b")
    high_came = send(high_sends, "j")
    if pairs > 1:
        grad_pairs.append(backward(1, grad_heads))
    grads_give = [d for d in range(group) if d & core_bit]
    block_order = [2 * d + r for d in grads_give for r in range(2)]
    block_order += [2 * (d ^ core_bit) + r for d in grads_give for r in range(2)]
    grad_pairs, down_came, low_came, high_came, heads_in = together(
        grad_pairs, down_came, low_came, high_came, heads_in
    )
    grad_give, grad_keep = input_grad(
        positions_of[jnp.array(block_order, jnp.int32)], grad_pairs, w_heads, rows
    )
    grad_give, grad_keep, down_came, low_came, high_came, grad_pairs = together(
        grad_give, grad_keep, down_came, low_came, high_came, grad_pairs
    )
    give_came = by_offset(grad_give, core_bit)
    rest_pieces = [
        (x, came, at)
        for (kept, _), came in ((low_sends, low_came), (high_sends, high_came))
        for x, at in zip(kept, (0, units))
    ]
    (rest_sends,) = relay([(low_bit, (na // 2, 2, part), rest_pieces)], views)
    give_came, rest_sends, grad_keep = together(give_came, rest_sends, grad_keep)
    rest_came = send(rest_sends, "a")

    grad_keep = join(grad_keep, give_came)
    sums = {
        d ^ core_bit: [grad_keep[2 * n + r] for r in range(2)] for n, d in enumerate(grads_give)
    }
    for bit in far_bits[:-1]:
        for d in [d for d in sums if d & bit]:
            gone = sums.pop(d)
            for r in range(2):
                sums[d ^ bit][r] = join(sums[d ^ bit][r], by_offset(gone[r], bit))
    sums, grad_pairs = together(sums, grad_pairs)
    if far_bits:
        final = [by_offset(x, far_bits[-1]) for x in sums[far_bits[-1]]]
    weight_pairs = [dot(normed, x, TN).astype(BF) for x in grad_pairs[1:]]
    if far_bits:
        final[0], rest_came, down_came, block_came = together(
            final[0], rest_came, down_came, block_came
        )
    for x in weight_pairs:
        heads_in.append(lax.all_to_all(x.reshape(devices, part, 384), AXES, 0, 0, tiled=True))
    starts = (0, units, units + model // 2, 2 * units + model // 2)
    rest_pieces = [(x, rest_came, at) for x, at in zip(rest_sends[0], starts)]
    (rest_sends,) = relay([(next_bit, (na // 4, 2, part), rest_pieces)], views)
    rest_came = flip(rest_sends[1], "a", 2)
    if far_bits:
        final[1], rest_came = together(final[1], rest_came)
    down_parts = added_of(down_sends[0], down_came, (na // 4, cut))
    down_part = jnp.concatenate([scatter_axis(x, "a", 0, 4) for x in down_parts])
    block_out = ordered(*block_came)

    small, totals = mo_sums + turn_sums, []
    for r in range(2):
        parts = [sums[0][r]] + ([final[r]] if far_bits else [])
        total, sums_in = row_call(
            last_kernel, "last", 2, rows,
            [own[r], (grad_residual, r)] + parts, [], [vectors],
            [(model, BF)],
        )
        small = small + sums_in
        if r == 0 and far_bits:
            total, final[1] = together(total, final[1])
        totals.append(total)
    small = small.reshape(8, 2, nh, 2, na, nb, part).transpose(4, 3, 5, 1, 2, 0, 6)
    small = scatter_axis(small, "a", 0, kind=F32)
    small, totals = together(small, totals)
    grad_tokens = [restore(totals[0], 0)]
    grad_tokens.append(restore(totals[1], 1))
    rest_parts = added_of(rest_sends[0], rest_came, (na // 4, part))
    low_up, low_out, high_up, high_out = (scatter_axis(x, "a", 0, 4) for x in rest_parts)
    for axis in ("c", "b", "j", "h"):
        small = scatter_axis(small, axis, 0, kind=F32)
    grad_tokens = ordered(*grad_tokens)

    def spread(m):
        hc, b = divmod(m, nb)
        return [place(j, hc // 2, hc % 2, a, b) for j in range(2) for a in range(na)]

    g_query, g_key, g_value = head_sum(heads_in, group, spread)
    g_down, g_out = down_part.astype(F32), jnp.concatenate([low_out, high_out], axis=1).astype(F32)
    up_part = jnp.stack([low_up, high_up])
    up_keep = lax.dynamic_index_in_dim(up_part, ic, 0, keepdims=False).reshape(part, jh, unit)
    up_give = lax.dynamic_index_in_dim(up_part, 1 - ic, 0, keepdims=False)
    up_come = flip(up_give, "c", 1).reshape(part, jh, unit)
    g_up = jnp.where(
        ic == 0, jnp.stack([up_keep, up_come], axis=2), jnp.stack([up_come, up_keep], axis=2)
    ).reshape(part, ff).astype(F32)

    return (
        block_out, grad_tokens, g_query, g_key, g_value, g_out, g_up, g_down,
        small[0], small[1], small[2], small[3], small[4], small[5], small[6], small[7],
    )


def solution(mesh):
    fsdp, seq = mesh.shape["fsdp"], mesh.shape["seq"]
    inner = Mesh(mesh.devices.reshape(2, fsdp // 4, 2, fsdp, seq // fsdp), AXES)
    lead, line = ("j", "h", "c"), ("a", "b")
    acts = P(lead, line, None)
    weights = P(lead + line, None)
    vector = P(lead + line)
    return jax.shard_map(
        body,
        mesh=inner,
        in_specs=(acts,) * 2 + (weights,) * 6 + (vector,) * 8,
        out_specs=(acts,) * 2 + (weights,) * 6 + (vector,) * 8,
        check_vma=False,
    )
```

```python
import functools
import math

import jax
import jax.numpy as jnp
from jax import lax
from jax.experimental import pallas as pl
from jax.experimental.pallas import tpu as pltpu
from jax.sharding import Mesh
from jax.sharding import PartitionSpec as P

HEADS = 16
HEAD_DIM = 64
EPSILON = 1e-05
NEGATIVE = -1e30
LOG2E = math.log2(math.e)
AXES = ("j", "h", "c", "a", "b")
BF = jnp.bfloat16
F32 = jnp.float32
NT = (((1,), (1,)), ((), ()))
NN = (((1,), (0,)), ((), ()))
TN = (((0,), (0,)), ((), ()))


def cost(us):
    return pl.CostEstimate(flops=int(us * 1e6), bytes_accessed=1 << 10, transcendentals=0)


def dot(left, right, dims=NN):
    return lax.dot_general(left, right, dims, preferred_element_type=F32)


def qkv_kernel(table, order, *refs, group, shape):
    x_refs, w_refs = refs[:group], refs[group:-9]
    vec_ref, cos_ref, sin_ref, n_ref, q_ref, k_ref, v_ref, w_ref, held = refs[-9:]
    step = pl.program_id(0)

    @pl.when(step == 0)
    def _():
        if shape is None:
            w_ref[...] = w_refs[0][...]
            return
        na, nb, part = shape
        sources = w_refs[0].shape[0]
        for n in range(len(w_refs) * sources):
            j, a = order[n] // na, order[n] % na
            for m in range(group):
                row = ((j * (group // nb) + m // nb) * na + a) * nb + m % nb
                start = pl.multiple_of(row * part, part)
                block = w_refs[n // sources][n % sources, m * part : (m + 1) * part, :]
                w_ref[pl.ds(start, part), :] = block

    for n in range(group):

        @pl.when(step // 2 == n)
        def _(n=n):
            held[...] = x_refs[n][step % 2]

    x = held[...].astype(F32)
    center = x - jnp.mean(x, axis=1, keepdims=True)
    rstd = lax.rsqrt(jnp.mean(center * center, axis=1, keepdims=True) + EPSILON)
    normed = (center * rstd * vec_ref[0:1] + vec_ref[1:2]).astype(BF)
    n_ref[...] = normed
    full = dot(normed, w_ref[...])
    lane = lax.broadcasted_iota(jnp.int32, (1, 128), 1)
    first = (lane % HEAD_DIM) < HEAD_DIM // 2
    cosine, sine = cos_ref[...], sin_ref[...]
    for pair in range(q_ref.shape[1] // 128):
        at = slice(pair * 128, (pair + 1) * 128)
        for which, out, scale in ((0, q_ref, LOG2E * HEAD_DIM**-0.5), (1, k_ref, 1.0)):
            t = full[:, (3 * pair + which) * 128 : (3 * pair + which + 1) * 128]
            other = jnp.where(first, pltpu.roll(t, 96, 1), pltpu.roll(t, 32, 1))
            out[:, at] = ((t * cosine + other * sine) * scale).astype(BF)
        v_ref[:, at] = full[:, (3 * pair + 2) * 128 : (3 * pair + 3) * 128].astype(BF)


def qkv_call(table, order, pieces, w, vec, cosine, sine, shape):
    group = len(pieces)
    _, rows, model = pieces[0].shape
    width = model // group
    length = 2 * group * rows
    at = lambda i, *t: (t[0][i], 0)
    fixed = lambda shape: pl.BlockSpec(
        shape, lambda i, *t: (0,) * len(shape), pipeline_mode=pl.Buffered(1)
    )
    return pl.pallas_call(
        functools.partial(qkv_kernel, group=group, shape=shape),
        out_shape=[jax.ShapeDtypeStruct((length, model), BF)]
        + [jax.ShapeDtypeStruct((length, width), BF)] * 3
        + [jax.ShapeDtypeStruct((model, 3 * width), BF)],
        grid_spec=pltpu.PrefetchScalarGridSpec(
            num_scalar_prefetch=2,
            grid=(2 * group,),
            in_specs=[fixed((2, rows, model))] * group
            + [fixed(x.shape) for x in (*w, vec)]
            + [pl.BlockSpec((rows, 128), at)] * 2,
            out_specs=[pl.BlockSpec((rows, model), at)]
            + [pl.BlockSpec((rows, width), at)] * 3
            + [fixed((model, 3 * width))],
            scratch_shapes=[pltpu.VMEM((rows, model), BF)],
        ),
        compiler_params=pltpu.CompilerParams(
            dimension_semantics=("arbitrary",), vmem_limit_bytes=60 << 20
        ),
        cost_estimate=cost(11),
        name="qkv",
    )(table, order, *pieces, *w, vec, cosine, sine)


def forward_kernel(table, q_ref, k_ref, v_ref, o_ref, lse_ref, vaug, *, bq, bk, rows):
    i = pl.program_id(1)
    lane = lax.broadcasted_iota(jnp.int32, (1, 128), 1)
    low = lane < HEAD_DIM

    @pl.when(i == 0)
    def _():
        v = v_ref[...]
        one = jnp.ones_like(v)
        vaug[0] = jnp.where(low, v, one)
        vaug[1] = jnp.where(low, one, v)

    parts = bq // bk
    heads = []
    for n in range(parts):
        q = q_ref[n * bk : (n + 1) * bk, :]
        zero = jnp.zeros_like(q)
        heads.append((jnp.where(low, q, zero), jnp.where(low, zero, q)))

    def step(kb, carry, first, masked):
        start = pl.multiple_of(kb * bk, bk)
        k_blk = k_ref[pl.ds(start, bk), :]
        out = list(carry)
        for n in range(first, parts):
            for h in range(2):
                top, acc = carry[2 * n + h]
                s = dot(heads[n][h], k_blk, NT)
                if masked and n == first:
                    row = lax.broadcasted_iota(jnp.int32, s.shape, 0)
                    col = lax.broadcasted_iota(jnp.int32, s.shape, 1)
                    s = jnp.where(col <= row, s, NEGATIVE)
                new = jnp.maximum(top, jnp.max(s, axis=1, keepdims=True))
                p = jnp.exp2(s - new)
                acc = acc * jnp.exp2(top - new) + dot(p.astype(BF), vaug[h, pl.ds(start, bk), :])
                out[2 * n + h] = (new, acc)
        return tuple(out)

    carry = tuple(
        (jnp.full((bk, 1), NEGATIVE, F32), jnp.zeros((bk, 128), F32)) for _ in range(2 * parts)
    )
    full = i * parts
    carry = lax.fori_loop(0, full, lambda kb, c: step(kb, c, 0, False), carry)
    for d in range(parts):
        carry = step(full + d, carry, d, True)
    for n in range(parts):
        (top0, acc0), (top1, acc1) = carry[2 * n : 2 * n + 2]
        total = pltpu.roll(jnp.where(low, acc1, acc0), HEAD_DIM, 1)
        o = (jnp.where(low, acc0, acc1) / total).astype(BF)
        for d in range(bk // rows):
            o_ref[table[(full + n) * (bk // rows) + d]] = o[d * rows : (d + 1) * rows]
        lse_ref[n * bk : (n + 1) * bk, :] = jnp.where(low, top0, top1) + jnp.log2(total)


def attention_forward(table, q, k, v, rows):
    length, width = q.shape
    bq, bk = min(2048, length), min(512, length)
    blocks = length // rows
    return pl.pallas_call(
        functools.partial(forward_kernel, bq=bq, bk=bk, rows=rows),
        out_shape=[
            jax.ShapeDtypeStruct((blocks, rows, width), BF),
            jax.ShapeDtypeStruct((length, width), F32),
        ],
        grid_spec=pltpu.PrefetchScalarGridSpec(
            num_scalar_prefetch=1,
            grid=(width // 128, length // bq),
            in_specs=[
                pl.BlockSpec((bq, 128), lambda p, i, t: (i, p)),
                pl.BlockSpec((length, 128), lambda p, i, t: (0, p)),
                pl.BlockSpec((length, 128), lambda p, i, t: (0, p)),
            ],
            out_specs=[
                pl.BlockSpec((blocks, rows, 128), lambda p, i, t: (0, 0, p)),
                pl.BlockSpec((bq, 128), lambda p, i, t: (i, p)),
            ],
            scratch_shapes=[pltpu.VMEM((2, length, 128), BF)],
        ),
        compiler_params=pltpu.CompilerParams(
            dimension_semantics=("arbitrary", "arbitrary"), vmem_limit_bytes=60 << 20
        ),
        cost_estimate=cost(23),
        name="attention_forward",
    )(table, q, k, v)


def split3(x):
    high = x.astype(BF)
    rest = x - high.astype(F32)
    mid = rest.astype(BF)
    return high, mid, (rest - mid.astype(F32)).astype(BF)


def backward_kernel(
    table, q_ref, k_ref, v_ref, o_ref, do_ref, lse_ref, cos_ref, sin_ref, ck_ref, sk_ref,
    d_ref, qa, da, dqt, *, bk, rows
):
    j = pl.program_id(0)
    length = q_ref.shape[0]
    lane = lax.broadcasted_iota(jnp.int32, (1, 128), 1)
    low = lane < HEAD_DIM
    first = (lane % HEAD_DIM) < HEAD_DIM // 2

    def unturn(t, cosine, sine):
        other = jnp.where(first, pltpu.roll(t, 96, 1), pltpu.roll(t, 32, 1))
        return t * cosine - other * sine

    @pl.when(j == 0)
    def _():
        dqt[...] = jnp.zeros_like(dqt)

        def prep(b, _):
            r = pl.ds(pl.multiple_of(b * rows, rows), rows)
            q, do = q_ref[r, :], do_ref[table[b]]
            product = o_ref[table[b]].astype(F32) * do.astype(F32)
            for h in range(2):
                mine = low if h == 0 else jnp.logical_not(low)
                base = HEAD_DIM if h == 0 else 0
                delta = -jnp.sum(jnp.where(mine, product, 0.0), axis=1, keepdims=True)
                lse = -lse_ref[r, HEAD_DIM * h : HEAD_DIM * h + 1]
                for source, value, target in ((q, lse, qa), (do, delta, da)):
                    x = jnp.where(mine, source, jnp.zeros_like(source))
                    for n, part in enumerate(split3(value)):
                        x = jnp.where(lane == base + n, part, x)
                    target[h, r, :] = x
            return 0

        lax.fori_loop(0, length // rows, prep, 0)

    k, v = k_ref[...], v_ref[...]
    one, zero = jnp.ones_like(k), jnp.zeros_like(k)
    ka, va, kt = [], [], []
    for h in range(2):
        mine = low if h == 0 else jnp.logical_not(low)
        base = HEAD_DIM if h == 0 else 0
        extra = jnp.where(jnp.logical_and(lane >= base, lane < base + 3), one, zero)
        ka.append(jnp.where(mine, k, extra))
        va.append(jnp.where(mine, v, extra))
        kt.append(jnp.where(mine, k, zero).T)

    def products(h, keys, r, masked):
        qh, dh = qa[h, r, :], da[h, r, :]
        st = dot(ka[h][keys], qh, NT)
        if masked:
            key = lax.broadcasted_iota(jnp.int32, st.shape, 0)
            query = lax.broadcasted_iota(jnp.int32, st.shape, 1)
            st = jnp.where(key <= query, st, NEGATIVE)
        p = jnp.exp2(st)
        ds = (p * dot(va[h][keys], dh, NT)).astype(BF)
        return dot(ds, qh), dot(p.astype(BF), dh), ds

    def step(qb, carry):
        r = pl.ds(pl.multiple_of(qb * bk, bk), bk)
        out, low_scores = [], []
        for h in range(2):
            dk, dv, ds = products(h, slice(None), r, False)
            out.append((carry[h][0] + dk, carry[h][1] + dv))
            low_scores.append(ds)
        dqt[:, r] += dot(kt[0], low_scores[0]) + dot(kt[1], low_scores[1])
        return tuple(out)

    half = bk // 2
    carry = []
    upper = pl.ds(pl.multiple_of(j * bk, bk), bk)
    lower = pl.ds(pl.multiple_of(j * bk + half, half), half)
    firsts = [products(h, slice(0, half), upper, True) for h in range(2)]
    seconds = [products(h, slice(half, bk), lower, True) for h in range(2)]
    for h in range(2):
        carry.append(
            tuple(jnp.concatenate([firsts[h][n], seconds[h][n]], axis=0) for n in range(2))
        )
    dqt[:, upper] += dot(kt[0][:, :half], firsts[0][2]) + dot(kt[1][:, :half], firsts[1][2])
    dqt[:, lower] += dot(kt[0][:, half:], seconds[0][2]) + dot(kt[1][:, half:], seconds[1][2])
    carry = lax.fori_loop(j + 1, length // bk, step, tuple(carry))
    (dk0, dv0), (dk1, dv1) = carry
    dk = unturn(jnp.where(low, dk0, dk1) * (1.0 / LOG2E), ck_ref[...], sk_ref[...])
    mine = pl.ds(pl.multiple_of(j * bk, bk), bk)
    d_ref[mine, 128:256] = dk.astype(BF)
    d_ref[mine, 256:384] = jnp.where(low, dv0, dv1).astype(BF)

    @pl.when(j == pl.num_programs(0) - 1)
    def _():
        dq = dqt[...].T * HEAD_DIM**-0.5
        d_ref[:, 0:128] = unturn(dq, cos_ref[...], sin_ref[...]).astype(BF)


def attention_backward(table, pair, q, k, v, o, do, lse, cosine, sine):
    length = q.shape[0]
    blocks, rows, _ = o.shape
    bk = min(512, length)
    full = pl.BlockSpec((length, 128), lambda j, t: (0, pair))
    block = pl.BlockSpec((bk, 128), lambda j, t: (j, pair))
    loose = pl.BlockSpec((blocks, rows, 128), lambda j, t: (0, 0, pair))
    return pl.pallas_call(
        functools.partial(backward_kernel, bk=bk, rows=rows),
        out_shape=jax.ShapeDtypeStruct((length, 384), BF),
        grid_spec=pltpu.PrefetchScalarGridSpec(
            num_scalar_prefetch=1,
            grid=(length // bk,),
            in_specs=[
                full, block, block, loose, loose, full,
                pl.BlockSpec((length, 128), lambda j, t: (0, 0)),
                pl.BlockSpec((length, 128), lambda j, t: (0, 0)),
                pl.BlockSpec((bk, 128), lambda j, t: (j, 0)),
                pl.BlockSpec((bk, 128), lambda j, t: (j, 0)),
            ],
            out_specs=pl.BlockSpec((length, 384), lambda j, t: (0, 0)),
            scratch_shapes=[
                pltpu.VMEM((2, length, 128), BF),
                pltpu.VMEM((2, length, 128), BF),
                pltpu.VMEM((128, length), F32),
            ],
        ),
        compiler_params=pltpu.CompilerParams(
            dimension_semantics=("arbitrary",), vmem_limit_bytes=56 << 20
        ),
        cost_estimate=cost(44),
        name="attention_backward",
    )(table, q, k, v, o, do, lse, cosine, sine, cosine, sine)


def gelu(v):
    return 0.5 * v * (1.0 + jnp.tanh(0.7978845608 * (v + 0.044715 * v * v * v)))


def gelu_slope(v):
    square = v * v
    t = jnp.tanh(0.7978845608 * v * (1.0 + 0.044715 * square))
    inner = 0.7978845608 * (1.0 + 3.0 * 0.044715 * square)
    return 0.5 * (1.0 + t) + 0.5 * v * (1.0 - t * t) * inner


def take(step, refs, held):
    for n, ref in enumerate(refs):

        @pl.when(step == n)
        def _(ref=ref):
            held[...] = ref[...].reshape(held.shape)

    return held[...]


def load_up(order, refs, up):
    pieces, (sources, rows, unit) = len(refs) // 2, refs[0].shape
    part, total = rows // 2, pieces * sources
    per = total // (up.shape[1] // unit)
    for which in range(2):
        for n in range(total):
            source = order[which, n]
            ref = refs[which * pieces + n // sources]
            base = (source // per) * 2 * per + source % per
            for c in range(2):
                start = pl.multiple_of((base + c * per) * part, part)
                up[pl.ds(start, part), which * unit : (which + 1) * unit] = ref[
                    n % sources, c * part : (c + 1) * part, :
                ]


def load_down(order, refs, down):
    at = 0
    for ref in refs:
        deep = ref.shape[1]
        for n in range(ref.shape[0]):
            down[pl.ds(pl.multiple_of(order[2, at] * deep, deep), deep), :] = ref[n]
            at += 1


def mlp_up_kernel(*refs, tables):
    pre_ref, act_ref, held = refs[tables + 2 :][-(3 + tables) :][:3]
    x_refs, weights = refs[tables : tables + 2], refs[tables + 2 : -(3 + tables)]
    up = weights[0]
    if tables:
        up = refs[-1]

        @pl.when(pl.program_id(0) == 0)
        def _():
            load_up(refs[0], weights, up)

    x = take(pl.program_id(0), x_refs, held)
    for n in range(up.shape[1] // x.shape[1]):
        at = slice(n * x.shape[1], (n + 1) * x.shape[1])
        pre = dot(x, up[:, at])
        pre_ref[:, at] = pre.astype(BF)
        act_ref[:, at] = gelu(pre).astype(BF)


def leave(total, own_ref, other_ref):
    @pl.when(pl.program_id(0) == 0)
    def _():
        own_ref[...] = total

    @pl.when(pl.program_id(0) == 1)
    def _():
        other_ref[...] = total.astype(BF)


def mlp_down_kernel(*refs, tables):
    act_ref, weights = refs[tables], refs[tables + 1 : -(2 + tables)]
    own_ref, other_ref = refs[tables + 1 :][-(2 + tables) :][:2]
    down = weights[0]
    if tables:
        down = refs[-1]

        @pl.when(pl.program_id(0) == 0)
        def _():
            load_down(refs[0], weights, down)

    leave(dot(act_ref[...], down[...]), own_ref, other_ref)


def mlp_backward_kernel(*refs, tables):
    g_refs, pre_ref, weights = refs[tables : tables + 2], refs[tables + 2], refs[tables + 3 : -(4 + 2 * tables)]
    low_ref, own_ref, other_ref, held = refs[tables + 3 :][-(4 + 2 * tables) :][:4]
    up, down = weights[0], weights[-1]
    if tables:
        up, down = refs[-2:]

        @pl.when(pl.program_id(0) == 0)
        def _():
            load_up(refs[0], weights[:4], up)
            load_down(refs[0], weights[4:], down)

    g = take(pl.program_id(0), g_refs, held)
    total = None
    for n in range(up.shape[1] // g.shape[1]):
        at = slice(n * g.shape[1], (n + 1) * g.shape[1])
        grad = dot(g, down[at, :], NT)
        low = (grad * gelu_slope(pre_ref[:, at].astype(F32))).astype(BF)
        low_ref[:, at] = low
        term = dot(low, up[:, at], NT)
        total = term if total is None else total + term
    leave(total, own_ref, other_ref)


def mlp_call(kernel, name, us, narrow, wide, weights, tables, scratch, wide_outs, split):
    count = (narrow or wide)[0].shape[0] if narrow else wide[0].shape[0] // 2
    model = weights[0][0].shape[-1] if tables else min(weights[0][0].shape)
    units = 2 * model if tables else max(weights[0][0].shape)
    fixed = lambda shape: pl.BlockSpec(
        shape, lambda m, *t: (0,) * len(shape), pipeline_mode=pl.Buffered(1)
    )
    wide_spec = pl.BlockSpec((count, units), lambda m, *t: (m, 0))
    return pl.pallas_call(
        functools.partial(kernel, tables=len(tables)),
        out_shape=[jax.ShapeDtypeStruct((2 * count, units), BF)] * wide_outs
        + [jax.ShapeDtypeStruct((count, model), kind) for kind in (F32, BF) if split],
        grid_spec=pltpu.PrefetchScalarGridSpec(
            num_scalar_prefetch=len(tables),
            grid=(2,),
            in_specs=[fixed((count, model))] * len(narrow)
            + [wide_spec] * len(wide)
            + [fixed(x.shape[:-2] + (rows, x.shape[-1])) for x, rows in weights],
            out_specs=[wide_spec] * wide_outs + [fixed((count, model))] * (2 * split),
            scratch_shapes=[pltpu.VMEM((count, model), BF)] * bool(narrow)
            + [pltpu.VMEM(shape, BF) for shape in scratch if tables],
        ),
        compiler_params=pltpu.CompilerParams(
            dimension_semantics=("arbitrary",), vmem_limit_bytes=56 << 20
        ),
        cost_estimate=cost(us),
        name=name,
    )(*tables, *narrow, *wide, *[x for x, _ in weights])


def relay_kernel(here, *refs, layout, arrivals):
    count = sum(len(pieces) for _, pieces in layout)
    kept, came = refs[:count], refs[count : count + arrivals]
    outs, given = refs[count + arrivals : 2 * count + arrivals], refs[2 * count + arrivals :]
    at = 0
    for g, (n, pieces) in enumerate(layout):
        mine = here[g]
        for start, source, offset in pieces:
            width = kept[at].shape[3]
            for i in range(n):
                for keep in (True, False):
                    half = mine if keep else 1 - mine
                    x = kept[at][i, half].astype(F32)
                    x = x + came[source][i, half, :, offset : offset + width].astype(F32)
                    if keep:
                        outs[at][i] = x.astype(BF)
                    else:
                        given[g][i, :, start : start + width] = x.astype(BF)
            at += 1


def relay(groups, fused):
    if not fused:
        results = []
        for here, (n, halves, m), pieces in groups:
            kept, given = [], []
            for x, came, offset in pieces:
                width = x.shape[-1]
                x = x.reshape(-1, width)
                if came is not None:
                    x = join(x, came.reshape(-1, came.shape[-1])[:, offset : offset + width])
                if x.shape[0] != n * halves * m:
                    x = scatter_axis(x.reshape(lax.axis_size("h"), -1, width), "h", 0)
                x = x.reshape(n, halves, m, width)
                mine = 0 if here is None else here
                kept.append(lax.dynamic_index_in_dim(x, mine, 1, keepdims=False))
                if here is not None:
                    given.append(lax.dynamic_index_in_dim(x, 1 - here, 1, keepdims=False))
            results.append((kept, jnp.concatenate(given, axis=-1) if given else None))
        return results
    kept, came, layout, widths = [], [], [], []
    for _, (n, halves, m), pieces in groups:
        start, entries = 0, []
        for x, arrived, offset in pieces:
            kept.append(x.reshape(n, halves, m, x.shape[-1]))
            if not any(arrived is y for y, _ in came):
                came.append((arrived, (n, halves, m, arrived.shape[-1])))
            source = [arrived is y for y, _ in came].index(True)
            entries.append((start, source, offset))
            start += x.shape[-1]
        layout.append((n, tuple(entries)))
        widths.append((n, m, start))
    came = [y.reshape(shape) for y, shape in came]
    shapes = [(x.shape[0],) + x.shape[2:] for x in kept] + widths
    fixed = lambda shape: pl.BlockSpec(
        tuple(shape), lambda i, t: (0,) * len(shape), pipeline_mode=pl.Buffered(1)
    )
    outs = pl.pallas_call(
        functools.partial(relay_kernel, layout=tuple(layout), arrivals=len(came)),
        out_shape=[jax.ShapeDtypeStruct(shape, BF) for shape in shapes],
        grid_spec=pltpu.PrefetchScalarGridSpec(
            num_scalar_prefetch=1,
            grid=(1,),
            in_specs=[fixed(x.shape) for x in kept + came],
            out_specs=[fixed(shape) for shape in shapes],
        ),
        compiler_params=pltpu.CompilerParams(
            dimension_semantics=("arbitrary",), vmem_limit_bytes=60 << 20
        ),
        cost_estimate=cost(4),
        name="relay",
    )(jnp.stack([here for here, *_ in groups]), *kept, *came)
    results, at = [], 0
    for g, (_, entries) in enumerate(layout):
        results.append((list(outs[at : at + len(entries)]), outs[len(kept) + g]))
        at += len(entries)
    return results


def spread_of(values):
    center = values - jnp.mean(values, axis=1, keepdims=True)
    rstd = lax.rsqrt(jnp.mean(center * center, axis=1, keepdims=True) + EPSILON)
    return center * rstd, rstd


def norm_slope(hat, rstd, gain, grad, sums_ref, at):
    scaled = grad * gain
    inner = scaled - jnp.mean(scaled, axis=1, keepdims=True)
    sums_ref[at : at + 1] += jnp.sum(grad * hat, axis=0, keepdims=True)
    sums_ref[at + 1 : at + 2] += jnp.sum(grad, axis=0, keepdims=True)
    return rstd * (inner - hat * jnp.mean(scaled * hat, axis=1, keepdims=True))


def clear_at_start(ref):
    @pl.when(pl.program_id(0) == 0)
    def _():
        ref[...] = jnp.zeros_like(ref)


def pick_kernel(*refs):
    out = refs[-1]
    sources, cut, _ = refs[0].shape
    for n, ref in enumerate(refs[:-1]):
        which, piece = divmod(n, (len(refs) - 1) // 2)
        out[piece * sources : (piece + 1) * sources, which * cut : (which + 1) * cut] = ref[...]


def pick(arrays, cut):
    sources, wide, model = arrays[0].shape
    spec = pl.BlockSpec((sources, cut, model), lambda i: (0, wide // cut - 1, 0))
    shape = (sources * len(arrays) // 2, 2 * cut, model)
    return pl.pallas_call(
        pick_kernel,
        out_shape=jax.ShapeDtypeStruct(shape, BF),
        grid=(1,),
        in_specs=[spec] * len(arrays),
        out_specs=pl.BlockSpec(shape, lambda i: (0, 0, 0)),
        cost_estimate=cost(2),
        name="pick",
    )(*arrays)


def out_kernel(order, places, *refs, group, views):
    projected_ref, residual_ref, normed_ref, w_ref, held = refs[-5:]
    mixed, tokens, vec_ref, weights = refs[:group], refs[group : group + 2], refs[group + 2], refs[group + 3 : -5]
    step = pl.program_id(0)

    @pl.when(step == 0)
    def _():
        if not views:
            w_ref[...] = weights[0][...]
            return
        sources, cut = weights[0].shape[0], weights[0].shape[1] // 2
        halves = places.shape[0] // 2
        per = sources // halves
        for which in range(2):
            for n in range(sources):
                source = order[which, n]
                start = pl.multiple_of((source % per) * 2 * cut + which * cut, cut)
                for core in range(2):
                    block = places[core * halves + source // per]
                    w_ref[block, pl.ds(start, cut), :] = weights[core][n, which * cut : (which + 1) * cut]

    projected = dot(mixed[0][...], w_ref[0])
    for d in range(1, group):
        projected = projected + dot(mixed[d][...], w_ref[d])
    projected_ref[...] = projected
    hat, _ = spread_of(projected)
    x = take(step, tokens, held).astype(F32)
    residual = x + hat * vec_ref[2:3] + vec_ref[3:4]
    residual_ref[...] = residual
    hat, _ = spread_of(residual)
    normed_ref[...] = (hat * vec_ref[4:5] + vec_ref[5:6]).astype(BF)


def out_projection(order, places, mixed, tokens, vec, weights, views):
    group = len(mixed)
    count, width = mixed[0].shape
    rows, model = tokens[0].shape
    fixed = lambda shape: pl.BlockSpec(shape, lambda i, *t: (0,) * len(shape))
    tall = pl.BlockSpec((rows, model), lambda i, *t: (i, 0))
    specs = [fixed(x.shape) for x in weights]
    return pl.pallas_call(
        functools.partial(out_kernel, group=group, views=views),
        out_shape=[
            jax.ShapeDtypeStruct((count, model), F32),
            jax.ShapeDtypeStruct((count, model), F32),
            jax.ShapeDtypeStruct((count, model), BF),
            jax.ShapeDtypeStruct((group, width, model), BF),
        ],
        grid_spec=pltpu.PrefetchScalarGridSpec(
            num_scalar_prefetch=2,
            grid=(count // rows,),
            in_specs=[pl.BlockSpec((rows, width), lambda i, *t: (i, 0))] * group
            + [fixed((rows, model))] * 2
            + [fixed(vec.shape)]
            + specs,
            out_specs=[tall, tall, tall, fixed((group, width, model))],
            scratch_shapes=[pltpu.VMEM((rows, model), BF)],
        ),
        compiler_params=pltpu.CompilerParams(
            dimension_semantics=("arbitrary",), vmem_limit_bytes=40 << 20
        ),
        cost_estimate=cost(5),
        name="out_projection",
    )(order, places, *mixed, *tokens, vec, *weights)


def middle_kernel(own_ref, came_ref, residual_ref, g0_ref, g1_ref, vec_ref, out_ref, low_ref, sums_ref, held):
    clear_at_start(sums_ref)
    hat, rstd = spread_of(own_ref[...] + came_ref[...].astype(F32))
    out_ref[...] = (residual_ref[...] + hat * vec_ref[6:7] + vec_ref[7:8]).astype(BF)
    grad = take(pl.program_id(0), (g0_ref, g1_ref), held).astype(F32)
    low_ref[...] = norm_slope(hat, rstd, vec_ref[6:7], grad, sums_ref, 6).astype(BF)


def turn_kernel(own_ref, came_ref, residual_ref, projected_ref, g0_ref, g1_ref, vec_ref, w_ref, *refs, group):
    grad_ref, low_ref, *heads, sums_ref, held = refs
    clear_at_start(sums_ref)
    hat, rstd = spread_of(residual_ref[...])
    grad = own_ref[...] + came_ref[...].astype(F32)
    passed = take(pl.program_id(0), (g0_ref, g1_ref), held).astype(F32)
    grad = passed + norm_slope(hat, rstd, vec_ref[4:5], grad, sums_ref, 4)
    grad_ref[...] = grad
    hat, rstd = spread_of(projected_ref[...])
    low = norm_slope(hat, rstd, vec_ref[2:3], grad, sums_ref, 2).astype(BF)
    low_ref[...] = low
    for d in range(group):
        heads[d][...] = dot(low, w_ref[d], NT).astype(BF)


def last_kernel(x_ref, grad_ref, *refs):
    *parts, vec_ref, out_ref, sums_ref = refs
    clear_at_start(sums_ref)
    hat, rstd = spread_of(x_ref[...].astype(F32))
    grad = parts[0][...].astype(F32)
    for part in parts[1:]:
        grad = grad + part[...].astype(F32)
    grad = norm_slope(hat, rstd, vec_ref[0:1], grad, sums_ref, 0)
    out_ref[...] = (grad_ref[...] + grad).astype(BF)


def row_call(kernel, name, us, rows, tall, halves, fixed, outs, limit=40):
    model = tall[0].shape[1]
    count = tall[0].shape[0]
    starts = [at[1] if isinstance(at, tuple) else 0 for at in tall]
    tall = [at[0] if isinstance(at, tuple) else at for at in tall]
    whole = lambda x: pl.BlockSpec(x.shape, lambda i, n=x.ndim: (0,) * n)
    block = lambda width: pl.BlockSpec((rows, width), lambda i: (i, 0))
    return pl.pallas_call(
        kernel,
        out_shape=[jax.ShapeDtypeStruct((count, width), kind) for width, kind in outs]
        + [jax.ShapeDtypeStruct((8, model), F32)],
        grid=(count // rows,),
        in_specs=[
            pl.BlockSpec((rows, model), lambda i, start=start: (i + start, 0)) for start in starts
        ]
        + [whole(x) for x in (*halves, *fixed)],
        out_specs=[block(width) for width, _ in outs] + [pl.BlockSpec((8, model), lambda i: (0, 0))],
        scratch_shapes=[pltpu.VMEM((rows, model), BF)] if halves else [],
        compiler_params=pltpu.CompilerParams(
            dimension_semantics=("arbitrary",), vmem_limit_bytes=limit << 20
        ),
        cost_estimate=cost(us),
        name=name,
    )(*tall, *halves, *fixed)


def input_grad_kernel(table, *refs):
    w_ref, give_ref, keep_ref = refs[-3:]
    total = None
    for n, ref in enumerate(refs[:-3]):
        term = dot(ref[...], w_ref[:, n * 384 : (n + 1) * 384], NT)
        total = term if total is None else total + term
    giving = pl.program_id(0) < pl.num_programs(0) // 2

    @pl.when(giving)
    def _():
        give_ref[0] = total.astype(BF)

    @pl.when(jnp.logical_not(giving))
    def _():
        keep_ref[0] = total.astype(BF)


def input_grad(table, grads, w, rows):
    model = w.shape[0]
    blocks = grads[0].shape[0] // rows
    half = blocks // 2
    return pl.pallas_call(
        input_grad_kernel,
        out_shape=[jax.ShapeDtypeStruct((half, rows, model), BF)] * 2,
        grid_spec=pltpu.PrefetchScalarGridSpec(
            num_scalar_prefetch=1,
            grid=(blocks,),
            in_specs=[pl.BlockSpec((rows, 384), lambda i, t: (t[i], 0))] * len(grads)
            + [pl.BlockSpec(w.shape, lambda i, t: (0, 0))],
            out_specs=[
                pl.BlockSpec((1, rows, model), lambda i, t: (jnp.minimum(i, half - 1), 0, 0)),
                pl.BlockSpec((1, rows, model), lambda i, t: (jnp.maximum(i - half, 0), 0, 0)),
            ],
        ),
        compiler_params=pltpu.CompilerParams(
            dimension_semantics=("arbitrary",), vmem_limit_bytes=40 << 20
        ),
        cost_estimate=cost(6),
        name="input_grad",
    )(table, *grads, w)


def head_sum_kernel(*refs, group, spread):
    x_refs, outs = refs[:-3], refs[-3:]
    width = outs[0].shape[1] // group
    for m in range(group):
        for pair, ref in enumerate(x_refs):
            total = None
            for n in spread(m):
                term = ref[n].astype(F32)
                total = term if total is None else total + term
            at = slice(m * width + pair * 128, m * width + (pair + 1) * 128)
            for which, out in enumerate(outs):
                out[:, at] = total[:, which * 128 : (which + 1) * 128]


def head_sum(parts, group, spread):
    _, rows, wide = parts[0].shape
    return pl.pallas_call(
        functools.partial(head_sum_kernel, group=group, spread=spread),
        out_shape=[jax.ShapeDtypeStruct((rows, group * len(parts) * wide // 3), F32)] * 3,
        cost_estimate=cost(2),
        name="head_sum",
    )(*parts)


def flip(x, axis, bit):
    size = lax.axis_size(axis)
    return lax.ppermute(x, axis, [(i, i ^ bit) for i in range(size)])


def scatter_sends(x, axis, dim, bit):
    here = (lax.axis_index(axis) // bit) % 2
    shape = x.shape
    x = x.reshape(shape[:dim] + (shape[dim] // 2, 2) + shape[dim + 1 :])
    mine = lax.dynamic_index_in_dim(x, here, dim + 1, keepdims=False)
    return mine, lax.dynamic_index_in_dim(x, 1 - here, dim + 1, keepdims=False)


def join(mine, came, kind=BF):
    return (mine.astype(F32) + came.astype(F32)).astype(kind)


def scatter_axis(x, axis, dim, bit=1, kind=BF):
    size = lax.axis_size(axis)
    while bit < size:
        mine, theirs = scatter_sends(x, axis, dim, bit)
        x = join(mine, flip(theirs, axis, bit), kind)
        bit *= 2
    return x.reshape(x.shape[:dim] + x.shape[dim + 1 :])


def together(*groups):
    flat, tree = jax.tree.flatten(groups)
    return jax.tree.unflatten(tree, lax.optimization_barrier(tuple(flat)))


def place_in(order):
    index = jnp.arange(order.shape[0], dtype=jnp.int32)
    return jnp.sum(jnp.where(order[:, None] == index[None, :], index[:, None], 0), axis=0)


def gather_order(axes):
    masks = {axis: [0] for axis in AXES}
    for axis in axes:
        bit = lax.axis_size(axis) // 2
        while bit:
            for name in AXES:
                step = bit if name == axis else 0
                masks[name] = masks[name] + [m ^ step for m in masks[name]]
            bit //= 2
    return {axis: jnp.array(masks[axis], jnp.int32) for axis in AXES}


def source_of(axes, along=("j", "h", "a", "b")):
    masks, total = gather_order(axes), 0
    for axis in along:
        total = total * lax.axis_size(axis) + (lax.axis_index(axis) ^ masks[axis])
    return total


def stages_of(axes):
    stages = []
    for axis in axes:
        bit = lax.axis_size(axis) // 2
        while bit:
            stages.append((axis, bit))
            bit //= 2
    return stages


def after(x, *others):
    return lax.optimization_barrier((x,) + others)[0]


def body(
    tokens, cotangent, w_query, w_key, w_value, w_output, w_up, w_down,
    attn_in_gain, attn_in_bias, attn_out_gain, attn_out_bias,
    mlp_in_gain, mlp_in_bias, mlp_out_gain, mlp_out_bias,
):
    _, rows, model = tokens.shape
    nh, na, nb = lax.axis_size("h"), lax.axis_size("a"), lax.axis_size("b")
    jh = 2 * nh
    devices = 4 * nh * na * nb
    group = 2 * nh * nb
    half = na // 2
    length = rows * na * nb
    width = model // group
    pairs = width // 128
    part = w_query.shape[0]
    ij, ih, ic, ia, ib = (lax.axis_index(axis) for axis in AXES)
    slot, parity = ia // half, ia % 2
    member = (ih * 2 + ic) * nb + ib

    def place(j, h, c, a, b):
        return (((j * nh + h) * 2 + c) * na + a) * nb + b

    everyone = [
        (j, h, c, a, b)
        for j in range(2)
        for h in range(nh)
        for c in range(2)
        for a in range(na)
        for b in range(nb)
    ]
    moves = ([], [])
    for turn in range(2):
        for j, h, c, a, b in everyone:
            to_h, to_c = divmod(a % half, 2)
            plane = (h * 2 + c) * 2 + (turn + a // half) % 2
            target = place(j, to_h, to_c, plane, b)
            moves[turn].append((place(j, h, c, a, b), target))

    def regroup(x, turn):
        x = lax.dynamic_index_in_dim(x, (turn + slot) % 2, 0, keepdims=False)
        return lax.ppermute(x, AXES, moves[turn])

    def restore(x, turn):
        return lax.ppermute(x, AXES, [(there, here) for here, there in moves[turn]])

    def ordered(first, second):
        swap = slot == 1
        return jnp.stack([jnp.where(swap, second, first), jnp.where(swap, first, second)])

    def by_offset(x, offset):
        sends = []
        for j, h, c, a, b in everyone:
            to_hc, to_b = divmod(((h * 2 + c) * nb + b) ^ offset, nb)
            sends.append((place(j, h, c, a, b), place(j, to_hc // 2, to_hc % 2, a, to_b)))
        return lax.ppermute(x, AXES, sends)

    core_bit = nb
    far_bits = [1 << n for n in range(group.bit_length() - 1) if (1 << n) != core_bit]

    ff = w_up.shape[1]
    unit = ff // (2 * jh)
    up_split = w_up.reshape(part, jh, 2, unit)
    up_mine = lax.dynamic_index_in_dim(up_split, ic, 2, keepdims=False)
    up_other = flip(lax.dynamic_index_in_dim(up_split, 1 - ic, 2, keepdims=False), "c", 1)
    up_rows = jnp.stack(
        [jnp.where(ic == 0, up_mine, up_other), jnp.where(ic == 0, up_other, up_mine)]
    )
    n_up, n_down = 2 * part * jh * unit // model, w_down.shape[0]
    views = unit == model and part % 32 == 0 and n_up == n_down
    up_rows = up_rows.transpose(2, 0, 1, 3).reshape(n_up, model)
    cut, cut_up, cut_out = n_down // 2, n_up // 2, part // 2

    line_stages = stages_of(("a",))
    low_axes, high_axes = ("b", "h", "j"), ("h", "j", "b")

    def grow(x, came):
        return jnp.concatenate([x, came])

    def grow_all(x, stages):
        for axis, bit in stages:
            x = grow(x, flip(x, axis, bit))
        return x

    first = [up_rows[:cut_up], w_output[:cut_out], up_rows[cut_up:], w_output[cut_out:]]
    first, second = jnp.concatenate(first)[None], w_down[None]

    columns = jnp.stack(
        [w.reshape(part, group, pairs, 128) for w in (w_query, w_key, w_value)], axis=3
    ).reshape(part, group, 3 * width)
    columns = columns.transpose(1, 0, 2)
    columns = lax.all_to_all(columns, ("h", "c", "b"), 0, 0, tiled=True)
    columns = columns.reshape(1, group * part, 3 * width)

    blocks = 2 * group
    index = jnp.arange(blocks, dtype=jnp.int32)
    table = (member ^ (index % group)) * 2 + (parity ^ (index // group))
    positions_of = (parity ^ (index % 2)) * group + (member ^ (index // 2))
    lane, first = together(jnp.arange(128, dtype=jnp.int32), first)
    frequency = jnp.exp(
        (lane % (HEAD_DIM // 2)).astype(F32) * (-2.0 * math.log(10000.0) / HEAD_DIM)
    )
    angles = jnp.arange(length, dtype=jnp.int32).astype(F32)[:, None] * frequency[None, :]
    cosine = jnp.cos(angles)
    sine = jnp.sin(angles) * jnp.where((lane // (HEAD_DIM // 2)) % 2 == 0, -1.0, 1.0)[None, :]

    vectors, columns = together(
        jnp.stack(
            [attn_in_gain, attn_in_bias, attn_out_gain, attn_out_bias,
             mlp_in_gain, mlp_in_bias, mlp_out_gain, mlp_out_bias]
        ),
        columns,
    )
    vectors = jnp.broadcast_to(vectors[None], (devices,) + vectors.shape)
    vectors = lax.all_to_all(vectors, AXES, 0, 0, tiled=True)
    vectors = vectors.transpose(1, 0, 2).reshape(8, model).astype(F32)

    def columns_in_order(x):
        x = x[place_in(w_from)].reshape(2, na, nh, 2, nb, part, 3 * width)
        return x.transpose(0, 2, 3, 1, 4, 5, 6).reshape(model, 3 * width)

    own = [regroup(tokens, turn) for turn in range(2)]
    first_came = flip(first, *line_stages[0])
    w_came = flip(columns, *line_stages[0])
    own, first_came, w_came, second, cosine, sine, vectors = together(
        own, first_came, w_came, second, cosine, sine, vectors
    )
    first = grow_all(grow(first, first_came), line_stages[1:])
    wide = cut_up + cut_out
    low_stages, high_stages = stages_of(low_axes), stages_of(high_axes)
    first_low, first_high = first[:, :wide], first[:, wide:]
    columns = grow_all(grow(columns, w_came), line_stages[1:-1])
    second_came, w_came = flip(second, *line_stages[0]), flip(columns, *line_stages[-1])
    high_came = flip(first_high, *high_stages[0])
    pieces = {0: jnp.stack(own)}
    for bit in far_bits:
        for offset in list(pieces):
            pieces[offset ^ bit] = by_offset(pieces[offset], bit)
    pieces[core_bit] = by_offset(pieces[0], core_bit)
    pieces, high_came, second_came, w_came = together(pieces, high_came, second_came, w_came)
    second = grow_all(grow(second, second_came), line_stages[1:-1])
    columns = grow(columns, w_came)

    w_came = flip(columns, "j", 1)
    w_from = source_of(("a", "j"), ("j", "a"))
    low_came, second_came = flip(first_low, *low_stages[0]), flip(second, *line_stages[-1])
    for offset in range(1, group):
        if not offset & core_bit:
            pieces[offset ^ core_bit] = by_offset(pieces[offset], core_bit)
    pieces, w_came, low_came, second_came = together(pieces, w_came, low_came, second_came)
    if views:
        w_heads, w_shape = [columns, w_came], (na, nb, part)
    else:
        w_heads, w_shape = [columns_in_order(grow(columns, w_came))], None
    first_low = grow_all(grow(first_low, low_came), low_stages[1:-1])
    first_high = grow_all(grow(first_high, high_came), high_stages[1:-1])
    second = grow(second, second_came)
    pieces, first_low, first_high, second = together(pieces, first_low, first_high, second)
    low_came, high_came = flip(first_low, *low_stages[-1]), flip(first_high, *high_stages[-1])
    seconds = [second]
    if views:
        seconds += [flip(second, "b", 1), flip(second, "j", 1)]
    normed, queries, keys, values, w_heads = qkv_call(
        positions_of, w_from, [pieces[d] for d in range(group)], w_heads, vectors,
        cosine, sine, w_shape,
    )
    grad_in = [regroup(cotangent, 0)]
    attended, lse = attention_forward(table, queries, keys, values, rows)
    attended, lse, low_came, high_came, grad_in, cotangent = together(
        attended, lse, low_came, high_came, grad_in, cotangent
    )
    first_low, first_high = [first_low, low_came], [first_high, high_came]
    if views:
        near = source_of(("a",))
        over_b, over_j = (near // nb) * nb + (near % nb ^ 1), near ^ (na * nb)
        over_both = over_b ^ (na * nb)
        down_from = jnp.concatenate([near, over_b, over_j, over_both])
    else:
        seconds = [grow_all(second, stages_of(("h", "j", "b")))]
        down_from = source_of(("a", "h", "j", "b"))
    low_from, high_from = (source_of(("a",) + axes) for axes in (low_axes, high_axes))

    def exchange(x):
        return [x[0]] + [by_offset(x[d], d) for d in range(1, group)]

    order = jnp.stack([low_from, high_from, down_from])
    low_at, high_at = place_in(low_from), place_in(high_from)
    core_block = jnp.arange(2 * jh, dtype=jnp.int32)
    if views:
        mine = pick(first_low + first_high, cut_out)
        out_weights = [mine, flip(mine, "c", 1)]
    else:
        mine = jnp.concatenate(
            [jnp.concatenate([x[:, cut_up:] for x in pair]) for pair in (first_low, first_high)],
            axis=1,
        )
        mine = jnp.concatenate([mine[:, :cut_out][low_at], mine[:, cut_out:][high_at]], axis=1)
        mine = mine.reshape(jh, na * nb * part, model)
        other = flip(mine, "c", 1)
        w_out = jnp.where(
            ic == 0, jnp.stack([mine, other], axis=1), jnp.stack([other, mine], axis=1)
        ).reshape(group, width, model)
        out_weights = [w_out[member ^ jnp.arange(group)]]
    places = member ^ ((core_block % jh) * 2 + (ic ^ (core_block // jh)))
    mixed = exchange(attended.reshape(group, 2 * rows, width))
    projected, residual, mlp_mine, w_out = out_projection(
        order, places, mixed, own, vectors, out_weights, views
    )
    mlp_rows = [mlp_mine, flip(mlp_mine, "c", 1)]
    if views:
        mlp_rows, seconds = together(mlp_rows, seconds)
        seconds += [flip(seconds[1][: na // 2], "j", 1), flip(seconds[2][na // 2 :], "b", 1)]
    if views:
        tables = [order]
        up_weights = [(x, 2 * part) for x in first_low + first_high]
    else:
        tables = []
        up = [jnp.concatenate([x[:, :cut_up] for x in pair]) for pair in (first_low, first_high)]
        up = jnp.concatenate([up[0][low_at], up[1][high_at]], axis=1)
        up = up.reshape(jh, na, nb, jh, 2, part, unit)
        up_weights = [(up.transpose(0, 4, 1, 2, 5, 3, 6).reshape(model, jh * unit), model)]
    grad_in.append(regroup(cotangent, 1))
    pre_act, activated = mlp_call(
        mlp_up_kernel, "mlp_up", 11, mlp_rows, [], up_weights, tables,
        [(model, jh * unit)], 2, False,
    )
    activated, grad_in, seconds = together(activated, grad_in, seconds)
    if views:
        down_weights = [(x, n_down) for x in seconds]
    else:
        down = seconds[0][place_in(down_from)]
        down_weights = [(down.reshape(jh * unit, model), jh * unit)]
    branch, branch_other = mlp_call(
        mlp_down_kernel, "mlp_down", 9, [], [activated], down_weights, tables,
        [(jh * unit, model)], 0, True,
    )
    block_loose, branch_mine, mo_sums = row_call(
        middle_kernel, "middle", 3, rows,
        [branch, flip(branch_other, "c", 1), residual], grad_in, [vectors],
        [(model, BF), (model, BF)],
    )
    branch_rows = [branch_mine, flip(branch_mine, "c", 1)]

    def sends(x, axis, dim):
        return scatter_sends(x, axis, dim, 1) if lax.axis_size(axis) > 1 else (x, None)

    def send(pair, axis):
        return None if pair[1] is None else flip(pair[1], axis, 1)

    def added(pair, came, shape):
        return (pair[0] if came is None else join(pair[0], came)).reshape(shape)

    def sends_of(arrays, axis, dim):
        kept, given = zip(*[sends(x, axis, dim) for x in arrays])
        return list(kept), None if given[0] is None else jnp.concatenate(given, axis=-1)

    def added_of(kept, came, shape):
        out, start = [], 0
        for x in kept:
            width = x.shape[-1]
            if came is not None:
                x = join(x, came[..., start : start + width])
            out.append(x.reshape(shape + (width,)))
            start += width
        return out

    down_part = dot(activated, jnp.concatenate(branch_rows), TN).astype(BF)
    down_part = down_part.reshape(2, nh, na, nb, n_down, model)
    low_sends = sends(down_part[..., :cut, :], "b", 3)
    high_sends = sends(down_part[..., cut:, :], "j", 0)
    branch_rows, low_sends, high_sends, block_loose = together(
        branch_rows, low_sends, high_sends, block_loose
    )
    half_b, halves_b = (ib if nb > 1 else None), min(nb, 2)
    low_bit, next_bit = ia % 2, (ia // 2) % 2
    low_came, high_came = send(low_sends, "b"), send(high_sends, "j")
    block_came = [restore(block_loose[:rows], 0), restore(block_loose[rows:], 1)]
    pre_low, grad_mlp, grad_other = mlp_call(
        mlp_backward_kernel, "mlp_backward", 20, branch_rows, [pre_act],
        up_weights + down_weights, tables, [(model, jh * unit), (jh * unit, model)], 1, True,
    )
    pre_low, grad_mlp, grad_other, low_came, high_came, block_came = together(
        pre_low, grad_mlp, grad_other, low_came, high_came, block_came
    )
    grad_other = flip(grad_other, "c", 1)
    low_sends, high_sends = relay(
        [
            (ij, (1, 2, nh * na * cut), [(low_sends[0], low_came, 0)]),
            (half_b, (nh * na, halves_b, cut), [(high_sends[0], high_came, 0)]),
        ],
        views,
    )
    grad_mlp, grad_other, low_sends, high_sends = together(
        grad_mlp, grad_other, low_sends, high_sends
    )
    low_came, high_came = send(low_sends, "j"), send(high_sends, "b")
    grad_residual, projected_low, *attended_low, turn_sums = row_call(
        functools.partial(turn_kernel, group=group), "turn", 6, rows,
        [grad_mlp, grad_other, residual, projected], grad_in, [vectors, w_out],
        [(model, F32), (model, BF)] + [(width, BF)] * group, limit=60,
    )
    attended_low, projected_low, pre_low, low_came, high_came, block_came = together(
        attended_low, projected_low, pre_low, low_came, high_came, block_came
    )
    grad_heads = exchange(attended_low)
    grad_heads[1], pre_low = together(grad_heads[1], pre_low)
    grad_heads = jnp.stack(grad_heads).reshape(blocks, rows, width)
    down_pieces = [(low_sends[0][0], low_came, 0), (high_sends[0][0], high_came, 0)]
    (down_sends,) = relay([(low_bit, (na // 2, 2, cut), down_pieces)], views)
    up_part = dot(jnp.concatenate(mlp_rows), pre_low, TN).astype(BF)
    up_part = up_part.reshape(2, nh, 2, na, nb, part, jh * unit)
    grad_out = jnp.stack([dot(mixed[d], projected_low, TN).astype(BF) for d in range(group)])
    grad_out = jnp.stack(
        [lax.dynamic_index_in_dim(grad_out, member ^ m, 0, keepdims=False) for m in range(group)]
    ).reshape(2, nh, 2, na, nb, part, model)
    grad_out = scatter_axis(grad_out, "c", 2)
    low_sends = sends_of([up_part[:, :, 0], grad_out[..., : model // 2]], "j", 0)
    high_sends = sends_of([up_part[:, :, 1], grad_out[..., model // 2 :]], "b", 3)
    grad_heads, down_sends, low_sends, high_sends = together(
        grad_heads, down_sends, low_sends, high_sends
    )

    def backward(pair, grads):
        return attention_backward(
            table, pair, queries, keys, values, attended, grads, lse, cosine, sine
        )

    units = jh * unit
    low_came, high_came = send(low_sends, "j"), send(high_sends, "b")
    down_came = send(down_sends, "a")
    grad_pairs = [backward(0, grad_heads)]
    grad_pairs, down_came, low_came, high_came = together(
        grad_pairs, down_came, low_came, high_came
    )
    weight_pairs = [dot(normed, grad_pairs[0], TN).astype(BF)]
    low_pieces = [(low_sends[0][0], low_came, 0), (low_sends[0][1], low_came, units)]
    high_pieces = [(high_sends[0][0], high_came, 0), (high_sends[0][1], high_came, units)]
    down_pieces = [(down_sends[0][0], down_came, 0), (down_sends[0][1], down_came, model)]
    low_sends, high_sends, down_sends = relay(
        [
            (half_b, (na, halves_b, part), low_pieces),
            (ij, (1, 2, nh * na * part), high_pieces),
            (next_bit, (na // 4, 2, cut), down_pieces),
        ],
        views,
    )
    heads_in = [
        lax.all_to_all(weight_pairs[0].reshape(devices, part, 384), AXES, 0, 0, tiled=True)
    ]
    if pairs > 1:
        grad_heads, down_sends, low_sends, high_sends, weight_pairs = together(
            grad_heads, down_sends, low_sends, high_sends, weight_pairs
        )
    down_came, low_came = flip(down_sends[1], "a", 2), send(low_sends, "b")
    high_came = send(high_sends, "j")
    if pairs > 1:
        grad_pairs.append(backward(1, grad_heads))
    grads_give = [d for d in range(group) if d & core_bit]
    block_order = [2 * d + r for d in grads_give for r in range(2)]
    block_order += [2 * (d ^ core_bit) + r for d in grads_give for r in range(2)]
    grad_pairs, down_came, low_came, high_came, heads_in = together(
        grad_pairs, down_came, low_came, high_came, heads_in
    )
    rest_pieces = [
        (x, came, at)
        for (kept, _), came in ((low_sends, low_came), (high_sends, high_came))
        for x, at in zip(kept, (0, units))
    ]
    (rest_sends,) = relay([(low_bit, (na // 2, 2, part), rest_pieces)], views)
    grad_pairs, rest_sends = together(grad_pairs, rest_sends)
    rest_came = send(rest_sends, "a")
    grad_give, grad_keep = input_grad(
        positions_of[jnp.array(block_order, jnp.int32)], grad_pairs, w_heads, rows
    )
    grad_give, grad_keep, grad_pairs = together(grad_give, grad_keep, grad_pairs)
    give_came = by_offset(grad_give, core_bit)
    give_came, grad_keep = together(give_came, grad_keep)

    grad_keep = join(grad_keep, give_came)
    sums = {
        d ^ core_bit: [grad_keep[2 * n + r] for r in range(2)] for n, d in enumerate(grads_give)
    }
    for bit in far_bits[:-1]:
        for d in [d for d in sums if d & bit]:
            gone = sums.pop(d)
            for r in range(2):
                sums[d ^ bit][r] = join(sums[d ^ bit][r], by_offset(gone[r], bit))
    sums, grad_pairs = together(sums, grad_pairs)
    if far_bits:
        final = [by_offset(x, far_bits[-1]) for x in sums[far_bits[-1]]]
    weight_pairs = [dot(normed, x, TN).astype(BF) for x in grad_pairs[1:]]
    weight_pairs, rest_came = together(weight_pairs, rest_came)
    for x in weight_pairs:
        heads_in.append(lax.all_to_all(x.reshape(devices, part, 384), AXES, 0, 0, tiled=True))
    starts = (0, units, units + model // 2, 2 * units + model // 2)
    rest_pieces = [(x, rest_came, at) for x, at in zip(rest_sends[0], starts)]
    (rest_sends,) = relay([(next_bit, (na // 4, 2, part), rest_pieces)], views)
    rest_came = flip(rest_sends[1], "a", 2)
    if far_bits:
        final[0], down_came, block_came = together(final[0], down_came, block_came)
        final[1], rest_came = together(final[1], rest_came)
    down_parts = added_of(down_sends[0], down_came, (na // 4, cut))
    down_part = jnp.concatenate([scatter_axis(x, "a", 0, 4) for x in down_parts])
    block_out = ordered(*block_came)

    small, totals = mo_sums + turn_sums, []
    for r in range(2):
        parts = [sums[0][r]] + ([final[r]] if far_bits else [])
        total, sums_in = row_call(
            last_kernel, "last", 2, rows,
            [own[r], (grad_residual, r)] + parts, [], [vectors],
            [(model, BF)],
        )
        small = small + sums_in
        if r == 0 and far_bits:
            total, final[1] = together(total, final[1])
        totals.append(total)
    grad_tokens = [restore(total, r) for r, total in enumerate(totals)]
    rest_parts = added_of(rest_sends[0], rest_came, (na // 4, part))
    low_up, low_out, high_up, high_out = (scatter_axis(x, "a", 0, 4) for x in rest_parts)
    small = small.reshape(8, 2, nh, 2, na, nb, part).transpose(3, 5, 1, 2, 4, 0, 6)
    for axis in ("c", "b", "j", "h", "a"):
        small = scatter_axis(small, axis, 0, kind=F32)
    grad_tokens = ordered(*grad_tokens)

    def spread(m):
        hc, b = divmod(m, nb)
        return [place(j, hc // 2, hc % 2, a, b) for j in range(2) for a in range(na)]

    g_query, g_key, g_value = head_sum(heads_in, group, spread)
    g_down, g_out = down_part.astype(F32), jnp.concatenate([low_out, high_out], axis=1).astype(F32)
    up_part = jnp.stack([low_up, high_up])
    up_keep = lax.dynamic_index_in_dim(up_part, ic, 0, keepdims=False).reshape(part, jh, unit)
    up_give = lax.dynamic_index_in_dim(up_part, 1 - ic, 0, keepdims=False)
    up_come = flip(up_give, "c", 1).reshape(part, jh, unit)
    g_up = jnp.where(
        ic == 0, jnp.stack([up_keep, up_come], axis=2), jnp.stack([up_come, up_keep], axis=2)
    ).reshape(part, ff).astype(F32)

    return (
        block_out, grad_tokens, g_query, g_key, g_value, g_out, g_up, g_down,
        small[0], small[1], small[2], small[3], small[4], small[5], small[6], small[7],
    )


def solution(mesh):
    fsdp, seq = mesh.shape["fsdp"], mesh.shape["seq"]
    inner = Mesh(mesh.devices.reshape(2, fsdp // 4, 2, fsdp, seq // fsdp), AXES)
    lead, line = ("j", "h", "c"), ("a", "b")
    acts = P(lead, line, None)
    weights = P(lead + line, None)
    vector = P(lead + line)
    return jax.shard_map(
        body,
        mesh=inner,
        in_specs=(acts,) * 2 + (weights,) * 6 + (vector,) * 8,
        out_specs=(acts,) * 2 + (weights,) * 6 + (vector,) * 8,
        check_vma=False,
    )
```

```python
import functools
import math

import jax
import jax.numpy as jnp
from jax import lax
from jax.experimental import pallas as pl
from jax.experimental.pallas import tpu as pltpu
from jax.sharding import Mesh
from jax.sharding import PartitionSpec as P

HEADS = 16
HEAD_DIM = 64
EPSILON = 1e-05
NEGATIVE = -1e30
LOG2E = math.log2(math.e)
AXES = ("j", "h", "c", "a", "b")
BF = jnp.bfloat16
F32 = jnp.float32
NT = (((1,), (1,)), ((), ()))
NN = (((1,), (0,)), ((), ()))
TN = (((0,), (0,)), ((), ()))


def cost(us):
    return pl.CostEstimate(flops=int(us * 1e6), bytes_accessed=1 << 10, transcendentals=0)


def dot(left, right, dims=NN):
    return lax.dot_general(left, right, dims, preferred_element_type=F32)


def qkv_kernel(table, order, *refs, group, shape):
    x_refs, w_refs = refs[:group], refs[group:-9]
    vec_ref, cos_ref, sin_ref, n_ref, q_ref, k_ref, v_ref, w_ref, held = refs[-9:]
    step = pl.program_id(0)

    @pl.when(step == 0)
    def _():
        if shape is None:
            w_ref[...] = w_refs[0][...]
            return
        na, nb, part = shape
        sources = w_refs[0].shape[0]
        for n in range(len(w_refs) * sources):
            j, a = order[n] // na, order[n] % na
            for m in range(group):
                row = ((j * (group // nb) + m // nb) * na + a) * nb + m % nb
                start = pl.multiple_of(row * part, part)
                block = w_refs[n // sources][n % sources, m * part : (m + 1) * part, :]
                w_ref[pl.ds(start, part), :] = block

    for n in range(group):

        @pl.when(step // 2 == n)
        def _(n=n):
            held[...] = x_refs[n][step % 2]

    x = held[...].astype(F32)
    center = x - jnp.mean(x, axis=1, keepdims=True)
    rstd = lax.rsqrt(jnp.mean(center * center, axis=1, keepdims=True) + EPSILON)
    normed = (center * rstd * vec_ref[0:1] + vec_ref[1:2]).astype(BF)
    n_ref[...] = normed
    full = dot(normed, w_ref[...])
    lane = lax.broadcasted_iota(jnp.int32, (1, 128), 1)
    first = (lane % HEAD_DIM) < HEAD_DIM // 2
    cosine, sine = cos_ref[...], sin_ref[...]
    for pair in range(q_ref.shape[1] // 128):
        at = slice(pair * 128, (pair + 1) * 128)
        for which, out, scale in ((0, q_ref, LOG2E * HEAD_DIM**-0.5), (1, k_ref, 1.0)):
            t = full[:, (3 * pair + which) * 128 : (3 * pair + which + 1) * 128]
            other = jnp.where(first, pltpu.roll(t, 96, 1), pltpu.roll(t, 32, 1))
            out[:, at] = ((t * cosine + other * sine) * scale).astype(BF)
        v_ref[:, at] = full[:, (3 * pair + 2) * 128 : (3 * pair + 3) * 128].astype(BF)


def qkv_call(table, order, pieces, w, vec, cosine, sine, shape):
    group = len(pieces)
    _, rows, model = pieces[0].shape
    width = model // group
    length = 2 * group * rows
    at = lambda i, *t: (t[0][i], 0)
    fixed = lambda shape: pl.BlockSpec(
        shape, lambda i, *t: (0,) * len(shape), pipeline_mode=pl.Buffered(1)
    )
    return pl.pallas_call(
        functools.partial(qkv_kernel, group=group, shape=shape),
        out_shape=[jax.ShapeDtypeStruct((length, model), BF)]
        + [jax.ShapeDtypeStruct((length, width), BF)] * 3
        + [jax.ShapeDtypeStruct((model, 3 * width), BF)],
        grid_spec=pltpu.PrefetchScalarGridSpec(
            num_scalar_prefetch=2,
            grid=(2 * group,),
            in_specs=[fixed((2, rows, model))] * group
            + [fixed(x.shape) for x in (*w, vec)]
            + [pl.BlockSpec((rows, 128), at)] * 2,
            out_specs=[pl.BlockSpec((rows, model), at)]
            + [pl.BlockSpec((rows, width), at)] * 3
            + [fixed((model, 3 * width))],
            scratch_shapes=[pltpu.VMEM((rows, model), BF)],
        ),
        compiler_params=pltpu.CompilerParams(
            dimension_semantics=("arbitrary",), vmem_limit_bytes=60 << 20
        ),
        cost_estimate=cost(11),
        name="qkv",
    )(table, order, *pieces, *w, vec, cosine, sine)


def forward_kernel(table, q_ref, k_ref, v_ref, o_ref, lse_ref, vaug, *, bq, bk, rows):
    i = pl.program_id(1)
    lane = lax.broadcasted_iota(jnp.int32, (1, 128), 1)
    low = lane < HEAD_DIM

    @pl.when(i == 0)
    def _():
        v = v_ref[...]
        one = jnp.ones_like(v)
        vaug[0] = jnp.where(low, v, one)
        vaug[1] = jnp.where(low, one, v)

    parts = bq // bk
    heads = []
    for n in range(parts):
        q = q_ref[n * bk : (n + 1) * bk, :]
        zero = jnp.zeros_like(q)
        heads.append((jnp.where(low, q, zero), jnp.where(low, zero, q)))

    def step(kb, carry, first, masked):
        start = pl.multiple_of(kb * bk, bk)
        k_blk = k_ref[pl.ds(start, bk), :]
        out = list(carry)
        for n in range(first, parts):
            for h in range(2):
                top, acc = carry[2 * n + h]
                s = dot(heads[n][h], k_blk, NT)
                if masked and n == first:
                    row = lax.broadcasted_iota(jnp.int32, s.shape, 0)
                    col = lax.broadcasted_iota(jnp.int32, s.shape, 1)
                    s = jnp.where(col <= row, s, NEGATIVE)
                new = jnp.maximum(top, jnp.max(s, axis=1, keepdims=True))
                p = jnp.exp2(s - new)
                acc = acc * jnp.exp2(top - new) + dot(p.astype(BF), vaug[h, pl.ds(start, bk), :])
                out[2 * n + h] = (new, acc)
        return tuple(out)

    carry = tuple(
        (jnp.full((bk, 1), NEGATIVE, F32), jnp.zeros((bk, 128), F32)) for _ in range(2 * parts)
    )
    full = i * parts
    carry = lax.fori_loop(0, full, lambda kb, c: step(kb, c, 0, False), carry)
    for d in range(parts):
        carry = step(full + d, carry, d, True)
    for n in range(parts):
        (top0, acc0), (top1, acc1) = carry[2 * n : 2 * n + 2]
        total = pltpu.roll(jnp.where(low, acc1, acc0), HEAD_DIM, 1)
        o = (jnp.where(low, acc0, acc1) / total).astype(BF)
        for d in range(bk // rows):
            o_ref[table[(full + n) * (bk // rows) + d]] = o[d * rows : (d + 1) * rows]
        lse_ref[n * bk : (n + 1) * bk, :] = jnp.where(low, top0, top1) + jnp.log2(total)


def attention_forward(table, q, k, v, rows):
    length, width = q.shape
    bq, bk = min(2048, length), min(512, length)
    blocks = length // rows
    return pl.pallas_call(
        functools.partial(forward_kernel, bq=bq, bk=bk, rows=rows),
        out_shape=[
            jax.ShapeDtypeStruct((blocks, rows, width), BF),
            jax.ShapeDtypeStruct((length, width), F32),
        ],
        grid_spec=pltpu.PrefetchScalarGridSpec(
            num_scalar_prefetch=1,
            grid=(width // 128, length // bq),
            in_specs=[
                pl.BlockSpec((bq, 128), lambda p, i, t: (i, p)),
                pl.BlockSpec((length, 128), lambda p, i, t: (0, p)),
                pl.BlockSpec((length, 128), lambda p, i, t: (0, p)),
            ],
            out_specs=[
                pl.BlockSpec((blocks, rows, 128), lambda p, i, t: (0, 0, p)),
                pl.BlockSpec((bq, 128), lambda p, i, t: (i, p)),
            ],
            scratch_shapes=[pltpu.VMEM((2, length, 128), BF)],
        ),
        compiler_params=pltpu.CompilerParams(
            dimension_semantics=("arbitrary", "arbitrary"), vmem_limit_bytes=60 << 20
        ),
        cost_estimate=cost(23),
        name="attention_forward",
    )(table, q, k, v)


def split3(x):
    high = x.astype(BF)
    rest = x - high.astype(F32)
    mid = rest.astype(BF)
    return high, mid, (rest - mid.astype(F32)).astype(BF)


def backward_kernel(
    table, q_ref, k_ref, v_ref, o_ref, do_ref, lse_ref, cos_ref, sin_ref, ck_ref, sk_ref,
    d_ref, qa, da, dqt, *, bk, rows
):
    j = pl.program_id(0)
    length = q_ref.shape[0]
    lane = lax.broadcasted_iota(jnp.int32, (1, 128), 1)
    low = lane < HEAD_DIM
    first = (lane % HEAD_DIM) < HEAD_DIM // 2

    def unturn(t, cosine, sine):
        other = jnp.where(first, pltpu.roll(t, 96, 1), pltpu.roll(t, 32, 1))
        return t * cosine - other * sine

    @pl.when(j == 0)
    def _():
        dqt[...] = jnp.zeros_like(dqt)

        def prep(b, _):
            r = pl.ds(pl.multiple_of(b * rows, rows), rows)
            q, do = q_ref[r, :], do_ref[table[b]]
            product = o_ref[table[b]].astype(F32) * do.astype(F32)
            for h in range(2):
                mine = low if h == 0 else jnp.logical_not(low)
                base = HEAD_DIM if h == 0 else 0
                delta = -jnp.sum(jnp.where(mine, product, 0.0), axis=1, keepdims=True)
                lse = -lse_ref[r, HEAD_DIM * h : HEAD_DIM * h + 1]
                for source, value, target in ((q, lse, qa), (do, delta, da)):
                    x = jnp.where(mine, source, jnp.zeros_like(source))
                    for n, part in enumerate(split3(value)):
                        x = jnp.where(lane == base + n, part, x)
                    target[h, r, :] = x
            return 0

        lax.fori_loop(0, length // rows, prep, 0)

    k, v = k_ref[...], v_ref[...]
    one, zero = jnp.ones_like(k), jnp.zeros_like(k)
    ka, va, kt = [], [], []
    for h in range(2):
        mine = low if h == 0 else jnp.logical_not(low)
        base = HEAD_DIM if h == 0 else 0
        extra = jnp.where(jnp.logical_and(lane >= base, lane < base + 3), one, zero)
        ka.append(jnp.where(mine, k, extra))
        va.append(jnp.where(mine, v, extra))
        kt.append(jnp.where(mine, k, zero).T)

    def products(h, keys, r, masked):
        qh, dh = qa[h, r, :], da[h, r, :]
        st = dot(ka[h][keys], qh, NT)
        if masked:
            key = lax.broadcasted_iota(jnp.int32, st.shape, 0)
            query = lax.broadcasted_iota(jnp.int32, st.shape, 1)
            st = jnp.where(key <= query, st, NEGATIVE)
        p = jnp.exp2(st)
        ds = (p * dot(va[h][keys], dh, NT)).astype(BF)
        return dot(ds, qh), dot(p.astype(BF), dh), ds

    def step(qb, carry):
        r = pl.ds(pl.multiple_of(qb * bk, bk), bk)
        out, low_scores = [], []
        for h in range(2):
            dk, dv, ds = products(h, slice(None), r, False)
            out.append((carry[h][0] + dk, carry[h][1] + dv))
            low_scores.append(ds)
        dqt[:, r] += dot(kt[0], low_scores[0]) + dot(kt[1], low_scores[1])
        return tuple(out)

    half = bk // 2
    carry = []
    upper = pl.ds(pl.multiple_of(j * bk, bk), bk)
    lower = pl.ds(pl.multiple_of(j * bk + half, half), half)
    firsts = [products(h, slice(0, half), upper, True) for h in range(2)]
    seconds = [products(h, slice(half, bk), lower, True) for h in range(2)]
    for h in range(2):
        carry.append(
            tuple(jnp.concatenate([firsts[h][n], seconds[h][n]], axis=0) for n in range(2))
        )
    dqt[:, upper] += dot(kt[0][:, :half], firsts[0][2]) + dot(kt[1][:, :half], firsts[1][2])
    dqt[:, lower] += dot(kt[0][:, half:], seconds[0][2]) + dot(kt[1][:, half:], seconds[1][2])
    carry = lax.fori_loop(j + 1, length // bk, step, tuple(carry))
    (dk0, dv0), (dk1, dv1) = carry
    dk = unturn(jnp.where(low, dk0, dk1) * (1.0 / LOG2E), ck_ref[...], sk_ref[...])
    mine = pl.ds(pl.multiple_of(j * bk, bk), bk)
    d_ref[mine, 128:256] = dk.astype(BF)
    d_ref[mine, 256:384] = jnp.where(low, dv0, dv1).astype(BF)

    @pl.when(j == pl.num_programs(0) - 1)
    def _():
        dq = dqt[...].T * HEAD_DIM**-0.5
        d_ref[:, 0:128] = unturn(dq, cos_ref[...], sin_ref[...]).astype(BF)


def attention_backward(table, pair, q, k, v, o, do, lse, cosine, sine):
    length = q.shape[0]
    blocks, rows, _ = o.shape
    bk = min(512, length)
    full = pl.BlockSpec((length, 128), lambda j, t: (0, pair))
    block = pl.BlockSpec((bk, 128), lambda j, t: (j, pair))
    loose = pl.BlockSpec((blocks, rows, 128), lambda j, t: (0, 0, pair))
    return pl.pallas_call(
        functools.partial(backward_kernel, bk=bk, rows=rows),
        out_shape=jax.ShapeDtypeStruct((length, 384), BF),
        grid_spec=pltpu.PrefetchScalarGridSpec(
            num_scalar_prefetch=1,
            grid=(length // bk,),
            in_specs=[
                full, block, block, loose, loose, full,
                pl.BlockSpec((length, 128), lambda j, t: (0, 0)),
                pl.BlockSpec((length, 128), lambda j, t: (0, 0)),
                pl.BlockSpec((bk, 128), lambda j, t: (j, 0)),
                pl.BlockSpec((bk, 128), lambda j, t: (j, 0)),
            ],
            out_specs=pl.BlockSpec((length, 384), lambda j, t: (0, 0)),
            scratch_shapes=[
                pltpu.VMEM((2, length, 128), BF),
                pltpu.VMEM((2, length, 128), BF),
                pltpu.VMEM((128, length), F32),
            ],
        ),
        compiler_params=pltpu.CompilerParams(
            dimension_semantics=("arbitrary",), vmem_limit_bytes=28 << 20
        ),
        cost_estimate=cost(44),
        name="attention_backward",
    )(table, q, k, v, o, do, lse, cosine, sine, cosine, sine)


def gelu(v):
    return 0.5 * v * (1.0 + jnp.tanh(0.7978845608 * (v + 0.044715 * v * v * v)))


def gelu_slope(v):
    square = v * v
    t = jnp.tanh(0.7978845608 * v * (1.0 + 0.044715 * square))
    inner = 0.7978845608 * (1.0 + 3.0 * 0.044715 * square)
    return 0.5 * (1.0 + t) + 0.5 * v * (1.0 - t * t) * inner


def take(step, refs, held):
    for n, ref in enumerate(refs):

        @pl.when(step == n)
        def _(ref=ref):
            held[...] = ref[...].reshape(held.shape)

    return held[...]


def load_up(order, refs, up):
    pieces, (sources, rows, unit) = len(refs) // 2, refs[0].shape
    part, total = rows // 2, pieces * sources
    per = total // (up.shape[1] // unit)
    for which in range(2):
        for n in range(total):
            source = order[which, n]
            ref = refs[which * pieces + n // sources]
            base = (source // per) * 2 * per + source % per
            for c in range(2):
                start = pl.multiple_of((base + c * per) * part, part)
                up[pl.ds(start, part), which * unit : (which + 1) * unit] = ref[
                    n % sources, c * part : (c + 1) * part, :
                ]


def load_down(order, refs, down):
    at = 0
    for ref in refs:
        deep = ref.shape[1]
        for n in range(ref.shape[0]):
            down[pl.ds(pl.multiple_of(order[2, at] * deep, deep), deep), :] = ref[n]
            at += 1


def mlp_up_kernel(*refs, tables):
    pre_ref, act_ref, held = refs[tables + 2 :][-(3 + tables) :][:3]
    x_refs, weights = refs[tables : tables + 2], refs[tables + 2 : -(3 + tables)]
    up = weights[0]
    if tables:
        up = refs[-1]

        @pl.when(pl.program_id(0) == 0)
        def _():
            load_up(refs[0], weights, up)

    x = take(pl.program_id(0), x_refs, held)
    for n in range(up.shape[1] // x.shape[1]):
        at = slice(n * x.shape[1], (n + 1) * x.shape[1])
        pre = dot(x, up[:, at])
        pre_ref[:, at] = pre.astype(BF)
        act_ref[:, at] = gelu(pre).astype(BF)


def leave(total, own_ref, other_ref):
    @pl.when(pl.program_id(0) == 0)
    def _():
        own_ref[...] = total

    @pl.when(pl.program_id(0) == 1)
    def _():
        other_ref[...] = total.astype(BF)


def mlp_down_kernel(*refs, tables):
    act_ref, weights = refs[tables], refs[tables + 1 : -(2 + tables)]
    own_ref, other_ref = refs[tables + 1 :][-(2 + tables) :][:2]
    down = weights[0]
    if tables:
        down = refs[-1]

        @pl.when(pl.program_id(0) == 0)
        def _():
            load_down(refs[0], weights, down)

    leave(dot(act_ref[...], down[...]), own_ref, other_ref)


def mlp_backward_kernel(*refs, tables):
    g_refs, pre_ref, weights = refs[tables : tables + 2], refs[tables + 2], refs[tables + 3 : -(4 + 2 * tables)]
    low_ref, own_ref, other_ref, held = refs[tables + 3 :][-(4 + 2 * tables) :][:4]
    up, down = weights[0], weights[-1]
    if tables:
        up, down = refs[-2:]

        @pl.when(pl.program_id(0) == 0)
        def _():
            load_up(refs[0], weights[:4], up)
            load_down(refs[0], weights[4:], down)

    g = take(pl.program_id(0), g_refs, held)
    total = None
    for n in range(up.shape[1] // g.shape[1]):
        at = slice(n * g.shape[1], (n + 1) * g.shape[1])
        grad = dot(g, down[at, :], NT)
        low = (grad * gelu_slope(pre_ref[:, at].astype(F32))).astype(BF)
        low_ref[:, at] = low
        term = dot(low, up[:, at], NT)
        total = term if total is None else total + term
    leave(total, own_ref, other_ref)


def mlp_call(kernel, name, us, narrow, wide, weights, tables, scratch, wide_outs, split):
    count = (narrow or wide)[0].shape[0] if narrow else wide[0].shape[0] // 2
    model = weights[0][0].shape[-1] if tables else min(weights[0][0].shape)
    units = 2 * model if tables else max(weights[0][0].shape)
    fixed = lambda shape: pl.BlockSpec(
        shape, lambda m, *t: (0,) * len(shape), pipeline_mode=pl.Buffered(1)
    )
    wide_spec = pl.BlockSpec((count, units), lambda m, *t: (m, 0))
    return pl.pallas_call(
        functools.partial(kernel, tables=len(tables)),
        out_shape=[jax.ShapeDtypeStruct((2 * count, units), BF)] * wide_outs
        + [jax.ShapeDtypeStruct((count, model), kind) for kind in (F32, BF) if split],
        grid_spec=pltpu.PrefetchScalarGridSpec(
            num_scalar_prefetch=len(tables),
            grid=(2,),
            in_specs=[fixed((count, model))] * len(narrow)
            + [wide_spec] * len(wide)
            + [fixed(x.shape[:-2] + (rows, x.shape[-1])) for x, rows in weights],
            out_specs=[wide_spec] * wide_outs + [fixed((count, model))] * (2 * split),
            scratch_shapes=[pltpu.VMEM((count, model), BF)] * bool(narrow)
            + [pltpu.VMEM(shape, BF) for shape in scratch if tables],
        ),
        compiler_params=pltpu.CompilerParams(
            dimension_semantics=("arbitrary",), vmem_limit_bytes=56 << 20
        ),
        cost_estimate=cost(us),
        name=name,
    )(*tables, *narrow, *wide, *[x for x, _ in weights])


def relay_kernel(here, *refs, layout, arrivals):
    count = sum(len(pieces) for _, pieces in layout)
    kept, came = refs[:count], refs[count : count + arrivals]
    outs, given = refs[count + arrivals : 2 * count + arrivals], refs[2 * count + arrivals :]
    at = 0
    for g, (n, pieces) in enumerate(layout):
        mine = here[g]
        for start, source, offset in pieces:
            width = kept[at].shape[3]
            for i in range(n):
                for keep in (True, False):
                    half = mine if keep else 1 - mine
                    x = kept[at][i, half].astype(F32)
                    x = x + came[source][i, half, :, offset : offset + width].astype(F32)
                    if keep:
                        outs[at][i] = x.astype(BF)
                    else:
                        given[g][i, :, start : start + width] = x.astype(BF)
            at += 1


def relay(groups, fused):
    if not fused:
        results = []
        for here, (n, halves, m), pieces in groups:
            kept, given = [], []
            for x, came, offset in pieces:
                width = x.shape[-1]
                x = x.reshape(-1, width)
                if came is not None:
                    x = join(x, came.reshape(-1, came.shape[-1])[:, offset : offset + width])
                if x.shape[0] != n * halves * m:
                    x = scatter_axis(x.reshape(lax.axis_size("h"), -1, width), "h", 0)
                x = x.reshape(n, halves, m, width)
                mine = 0 if here is None else here
                kept.append(lax.dynamic_index_in_dim(x, mine, 1, keepdims=False))
                if here is not None:
                    given.append(lax.dynamic_index_in_dim(x, 1 - here, 1, keepdims=False))
            results.append((kept, jnp.concatenate(given, axis=-1) if given else None))
        return results
    kept, came, layout, widths = [], [], [], []
    for _, (n, halves, m), pieces in groups:
        start, entries = 0, []
        for x, arrived, offset in pieces:
            kept.append(x.reshape(n, halves, m, x.shape[-1]))
            if not any(arrived is y for y, _ in came):
                came.append((arrived, (n, halves, m, arrived.shape[-1])))
            source = [arrived is y for y, _ in came].index(True)
            entries.append((start, source, offset))
            start += x.shape[-1]
        layout.append((n, tuple(entries)))
        widths.append((n, m, start))
    came = [y.reshape(shape) for y, shape in came]
    shapes = [(x.shape[0],) + x.shape[2:] for x in kept] + widths
    fixed = lambda shape: pl.BlockSpec(
        tuple(shape), lambda i, t: (0,) * len(shape), pipeline_mode=pl.Buffered(1)
    )
    outs = pl.pallas_call(
        functools.partial(relay_kernel, layout=tuple(layout), arrivals=len(came)),
        out_shape=[jax.ShapeDtypeStruct(shape, BF) for shape in shapes],
        grid_spec=pltpu.PrefetchScalarGridSpec(
            num_scalar_prefetch=1,
            grid=(1,),
            in_specs=[fixed(x.shape) for x in kept + came],
            out_specs=[fixed(shape) for shape in shapes],
        ),
        compiler_params=pltpu.CompilerParams(
            dimension_semantics=("arbitrary",), vmem_limit_bytes=60 << 20
        ),
        cost_estimate=cost(4),
        name="relay",
    )(jnp.stack([here for here, *_ in groups]), *kept, *came)
    results, at = [], 0
    for g, (_, entries) in enumerate(layout):
        results.append((list(outs[at : at + len(entries)]), outs[len(kept) + g]))
        at += len(entries)
    return results


def spread_of(values):
    center = values - jnp.mean(values, axis=1, keepdims=True)
    rstd = lax.rsqrt(jnp.mean(center * center, axis=1, keepdims=True) + EPSILON)
    return center * rstd, rstd


def norm_slope(hat, rstd, gain, grad, sums_ref, at):
    scaled = grad * gain
    inner = scaled - jnp.mean(scaled, axis=1, keepdims=True)
    sums_ref[at : at + 1] += jnp.sum(grad * hat, axis=0, keepdims=True)
    sums_ref[at + 1 : at + 2] += jnp.sum(grad, axis=0, keepdims=True)
    return rstd * (inner - hat * jnp.mean(scaled * hat, axis=1, keepdims=True))


def clear_at_start(ref):
    @pl.when(pl.program_id(0) == 0)
    def _():
        ref[...] = jnp.zeros_like(ref)


def pick_kernel(*refs):
    out = refs[-1]
    sources, cut, _ = refs[0].shape
    for n, ref in enumerate(refs[:-1]):
        which, piece = divmod(n, (len(refs) - 1) // 2)
        out[piece * sources : (piece + 1) * sources, which * cut : (which + 1) * cut] = ref[...]


def pick(arrays, cut):
    sources, wide, model = arrays[0].shape
    spec = pl.BlockSpec((sources, cut, model), lambda i: (0, wide // cut - 1, 0))
    shape = (sources * len(arrays) // 2, 2 * cut, model)
    return pl.pallas_call(
        pick_kernel,
        out_shape=jax.ShapeDtypeStruct(shape, BF),
        grid=(1,),
        in_specs=[spec] * len(arrays),
        out_specs=pl.BlockSpec(shape, lambda i: (0, 0, 0)),
        cost_estimate=cost(2),
        name="pick",
    )(*arrays)


def out_kernel(order, places, *refs, group, views):
    projected_ref, residual_ref, normed_ref, w_ref, held = refs[-5:]
    mixed, tokens, vec_ref, weights = refs[:group], refs[group : group + 2], refs[group + 2], refs[group + 3 : -5]
    step = pl.program_id(0)

    @pl.when(step == 0)
    def _():
        if not views:
            w_ref[...] = weights[0][...]
            return
        sources, cut = weights[0].shape[0], weights[0].shape[1] // 2
        halves = places.shape[0] // 2
        per = sources // halves
        for which in range(2):
            for n in range(sources):
                source = order[which, n]
                start = pl.multiple_of((source % per) * 2 * cut + which * cut, cut)
                for core in range(2):
                    block = places[core * halves + source // per]
                    w_ref[block, pl.ds(start, cut), :] = weights[core][n, which * cut : (which + 1) * cut]

    projected = dot(mixed[0][...], w_ref[0])
    for d in range(1, group):
        projected = projected + dot(mixed[d][...], w_ref[d])
    projected_ref[...] = projected
    hat, _ = spread_of(projected)
    x = take(step, tokens, held).astype(F32)
    residual = x + hat * vec_ref[2:3] + vec_ref[3:4]
    residual_ref[...] = residual
    hat, _ = spread_of(residual)
    normed_ref[...] = (hat * vec_ref[4:5] + vec_ref[5:6]).astype(BF)


def out_projection(order, places, mixed, tokens, vec, weights, views):
    group = len(mixed)
    count, width = mixed[0].shape
    rows, model = tokens[0].shape
    fixed = lambda shape: pl.BlockSpec(shape, lambda i, *t: (0,) * len(shape))
    tall = pl.BlockSpec((rows, model), lambda i, *t: (i, 0))
    specs = [fixed(x.shape) for x in weights]
    return pl.pallas_call(
        functools.partial(out_kernel, group=group, views=views),
        out_shape=[
            jax.ShapeDtypeStruct((count, model), F32),
            jax.ShapeDtypeStruct((count, model), F32),
            jax.ShapeDtypeStruct((count, model), BF),
            jax.ShapeDtypeStruct((group, width, model), BF),
        ],
        grid_spec=pltpu.PrefetchScalarGridSpec(
            num_scalar_prefetch=2,
            grid=(count // rows,),
            in_specs=[pl.BlockSpec((rows, width), lambda i, *t: (i, 0))] * group
            + [fixed((rows, model))] * 2
            + [fixed(vec.shape)]
            + specs,
            out_specs=[tall, tall, tall, fixed((group, width, model))],
            scratch_shapes=[pltpu.VMEM((rows, model), BF)],
        ),
        compiler_params=pltpu.CompilerParams(
            dimension_semantics=("arbitrary",), vmem_limit_bytes=40 << 20
        ),
        cost_estimate=cost(5),
        name="out_projection",
    )(order, places, *mixed, *tokens, vec, *weights)


def middle_kernel(own_ref, came_ref, residual_ref, g0_ref, g1_ref, vec_ref, out_ref, low_ref, sums_ref, held):
    clear_at_start(sums_ref)
    hat, rstd = spread_of(own_ref[...] + came_ref[...].astype(F32))
    out_ref[...] = (residual_ref[...] + hat * vec_ref[6:7] + vec_ref[7:8]).astype(BF)
    grad = take(pl.program_id(0), (g0_ref, g1_ref), held).astype(F32)
    low_ref[...] = norm_slope(hat, rstd, vec_ref[6:7], grad, sums_ref, 6).astype(BF)


def turn_kernel(own_ref, came_ref, residual_ref, projected_ref, g0_ref, g1_ref, vec_ref, w_ref, *refs, group):
    grad_ref, low_ref, *heads, sums_ref, held = refs
    clear_at_start(sums_ref)
    hat, rstd = spread_of(residual_ref[...])
    grad = own_ref[...] + came_ref[...].astype(F32)
    passed = take(pl.program_id(0), (g0_ref, g1_ref), held).astype(F32)
    grad = passed + norm_slope(hat, rstd, vec_ref[4:5], grad, sums_ref, 4)
    grad_ref[...] = grad
    hat, rstd = spread_of(projected_ref[...])
    low = norm_slope(hat, rstd, vec_ref[2:3], grad, sums_ref, 2).astype(BF)
    low_ref[...] = low
    for d in range(group):
        heads[d][...] = dot(low, w_ref[d], NT).astype(BF)


def last_kernel(x_ref, grad_ref, *refs):
    *parts, vec_ref, out_ref, sums_ref = refs
    clear_at_start(sums_ref)
    hat, rstd = spread_of(x_ref[...].astype(F32))
    grad = parts[0][...].astype(F32)
    for part in parts[1:]:
        grad = grad + part[...].astype(F32)
    grad = norm_slope(hat, rstd, vec_ref[0:1], grad, sums_ref, 0)
    out_ref[...] = (grad_ref[...] + grad).astype(BF)


def row_call(kernel, name, us, rows, tall, halves, fixed, outs, limit=40):
    model = tall[0].shape[1]
    count = tall[0].shape[0]
    starts = [at[1] if isinstance(at, tuple) else 0 for at in tall]
    tall = [at[0] if isinstance(at, tuple) else at for at in tall]
    whole = lambda x: pl.BlockSpec(x.shape, lambda i, n=x.ndim: (0,) * n)
    block = lambda width: pl.BlockSpec((rows, width), lambda i: (i, 0))
    return pl.pallas_call(
        kernel,
        out_shape=[jax.ShapeDtypeStruct((count, width), kind) for width, kind in outs]
        + [jax.ShapeDtypeStruct((8, model), F32)],
        grid=(count // rows,),
        in_specs=[
            pl.BlockSpec((rows, model), lambda i, start=start: (i + start, 0)) for start in starts
        ]
        + [whole(x) for x in (*halves, *fixed)],
        out_specs=[block(width) for width, _ in outs] + [pl.BlockSpec((8, model), lambda i: (0, 0))],
        scratch_shapes=[pltpu.VMEM((rows, model), BF)] if halves else [],
        compiler_params=pltpu.CompilerParams(
            dimension_semantics=("arbitrary",), vmem_limit_bytes=limit << 20
        ),
        cost_estimate=cost(us),
        name=name,
    )(*tall, *halves, *fixed)


def input_grad_kernel(table, *refs):
    w_ref, give_ref, keep_ref = refs[-3:]
    total = None
    for n, ref in enumerate(refs[:-3]):
        term = dot(ref[...], w_ref[:, n * 384 : (n + 1) * 384], NT)
        total = term if total is None else total + term
    giving = pl.program_id(0) < pl.num_programs(0) // 2

    @pl.when(giving)
    def _():
        give_ref[0] = total.astype(BF)

    @pl.when(jnp.logical_not(giving))
    def _():
        keep_ref[0] = total.astype(BF)


def input_grad(table, grads, w, rows):
    model = w.shape[0]
    blocks = grads[0].shape[0] // rows
    half = blocks // 2
    return pl.pallas_call(
        input_grad_kernel,
        out_shape=[jax.ShapeDtypeStruct((half, rows, model), BF)] * 2,
        grid_spec=pltpu.PrefetchScalarGridSpec(
            num_scalar_prefetch=1,
            grid=(blocks,),
            in_specs=[pl.BlockSpec((rows, 384), lambda i, t: (t[i], 0))] * len(grads)
            + [pl.BlockSpec(w.shape, lambda i, t: (0, 0))],
            out_specs=[
                pl.BlockSpec((1, rows, model), lambda i, t: (jnp.minimum(i, half - 1), 0, 0)),
                pl.BlockSpec((1, rows, model), lambda i, t: (jnp.maximum(i - half, 0), 0, 0)),
            ],
        ),
        compiler_params=pltpu.CompilerParams(
            dimension_semantics=("arbitrary",), vmem_limit_bytes=40 << 20
        ),
        cost_estimate=cost(6),
        name="input_grad",
    )(table, *grads, w)


def head_sum_kernel(*refs, group, spread):
    x_refs, outs = refs[:-3], refs[-3:]
    width = outs[0].shape[1] // group
    for m in range(group):
        for pair, ref in enumerate(x_refs):
            total = None
            for n in spread(m):
                term = ref[n].astype(F32)
                total = term if total is None else total + term
            at = slice(m * width + pair * 128, m * width + (pair + 1) * 128)
            for which, out in enumerate(outs):
                out[:, at] = total[:, which * 128 : (which + 1) * 128]


def head_sum(parts, group, spread):
    _, rows, wide = parts[0].shape
    return pl.pallas_call(
        functools.partial(head_sum_kernel, group=group, spread=spread),
        out_shape=[jax.ShapeDtypeStruct((rows, group * len(parts) * wide // 3), F32)] * 3,
        cost_estimate=cost(2),
        name="head_sum",
    )(*parts)


def flip(x, axis, bit):
    size = lax.axis_size(axis)
    return lax.ppermute(x, axis, [(i, i ^ bit) for i in range(size)])


def scatter_sends(x, axis, dim, bit):
    here = (lax.axis_index(axis) // bit) % 2
    shape = x.shape
    x = x.reshape(shape[:dim] + (shape[dim] // 2, 2) + shape[dim + 1 :])
    mine = lax.dynamic_index_in_dim(x, here, dim + 1, keepdims=False)
    return mine, lax.dynamic_index_in_dim(x, 1 - here, dim + 1, keepdims=False)


def join(mine, came, kind=BF):
    return (mine.astype(F32) + came.astype(F32)).astype(kind)


def scatter_axis(x, axis, dim, bit=1, kind=BF):
    size = lax.axis_size(axis)
    while bit < size:
        mine, theirs = scatter_sends(x, axis, dim, bit)
        x = join(mine, flip(theirs, axis, bit), kind)
        bit *= 2
    return x.reshape(x.shape[:dim] + x.shape[dim + 1 :])


def together(*groups):
    flat, tree = jax.tree.flatten(groups)
    return jax.tree.unflatten(tree, lax.optimization_barrier(tuple(flat)))


def place_in(order):
    index = jnp.arange(order.shape[0], dtype=jnp.int32)
    return jnp.sum(jnp.where(order[:, None] == index[None, :], index[:, None], 0), axis=0)


def gather_order(axes):
    masks = {axis: [0] for axis in AXES}
    for axis in axes:
        bit = lax.axis_size(axis) // 2
        while bit:
            for name in AXES:
                step = bit if name == axis else 0
                masks[name] = masks[name] + [m ^ step for m in masks[name]]
            bit //= 2
    return {axis: jnp.array(masks[axis], jnp.int32) for axis in AXES}


def source_of(axes, along=("j", "h", "a", "b")):
    masks, total = gather_order(axes), 0
    for axis in along:
        total = total * lax.axis_size(axis) + (lax.axis_index(axis) ^ masks[axis])
    return total


def stages_of(axes):
    stages = []
    for axis in axes:
        bit = lax.axis_size(axis) // 2
        while bit:
            stages.append((axis, bit))
            bit //= 2
    return stages


def after(x, *others):
    return lax.optimization_barrier((x,) + others)[0]


def body(
    tokens, cotangent, w_query, w_key, w_value, w_output, w_up, w_down,
    attn_in_gain, attn_in_bias, attn_out_gain, attn_out_bias,
    mlp_in_gain, mlp_in_bias, mlp_out_gain, mlp_out_bias,
):
    _, rows, model = tokens.shape
    nh, na, nb = lax.axis_size("h"), lax.axis_size("a"), lax.axis_size("b")
    jh = 2 * nh
    devices = 4 * nh * na * nb
    group = 2 * nh * nb
    half = na // 2
    length = rows * na * nb
    width = model // group
    pairs = width // 128
    part = w_query.shape[0]
    ij, ih, ic, ia, ib = (lax.axis_index(axis) for axis in AXES)
    slot, parity = ia // half, ia % 2
    member = (ih * 2 + ic) * nb + ib

    def place(j, h, c, a, b):
        return (((j * nh + h) * 2 + c) * na + a) * nb + b

    everyone = [
        (j, h, c, a, b)
        for j in range(2)
        for h in range(nh)
        for c in range(2)
        for a in range(na)
        for b in range(nb)
    ]
    moves = ([], [])
    for turn in range(2):
        for j, h, c, a, b in everyone:
            to_h, to_c = divmod(a % half, 2)
            plane = (h * 2 + c) * 2 + (turn + a // half) % 2
            target = place(j, to_h, to_c, plane, b)
            moves[turn].append((place(j, h, c, a, b), target))

    def regroup(x, turn):
        x = lax.dynamic_index_in_dim(x, (turn + slot) % 2, 0, keepdims=False)
        return lax.ppermute(x, AXES, moves[turn])

    def restore(x, turn):
        return lax.ppermute(x, AXES, [(there, here) for here, there in moves[turn]])

    def ordered(first, second):
        swap = slot == 1
        return jnp.stack([jnp.where(swap, second, first), jnp.where(swap, first, second)])

    def by_offset(x, offset):
        sends = []
        for j, h, c, a, b in everyone:
            to_hc, to_b = divmod(((h * 2 + c) * nb + b) ^ offset, nb)
            sends.append((place(j, h, c, a, b), place(j, to_hc // 2, to_hc % 2, a, to_b)))
        return lax.ppermute(x, AXES, sends)

    core_bit = nb
    far_bits = [1 << n for n in range(group.bit_length() - 1) if (1 << n) != core_bit]

    ff = w_up.shape[1]
    unit = ff // (2 * jh)
    up_split = w_up.reshape(part, jh, 2, unit)
    up_mine = lax.dynamic_index_in_dim(up_split, ic, 2, keepdims=False)
    up_other = flip(lax.dynamic_index_in_dim(up_split, 1 - ic, 2, keepdims=False), "c", 1)
    up_rows = jnp.stack(
        [jnp.where(ic == 0, up_mine, up_other), jnp.where(ic == 0, up_other, up_mine)]
    )
    n_up, n_down = 2 * part * jh * unit // model, w_down.shape[0]
    views = unit == model and part % 32 == 0 and n_up == n_down
    up_rows = up_rows.transpose(2, 0, 1, 3).reshape(n_up, model)
    cut, cut_up, cut_out = n_down // 2, n_up // 2, part // 2

    line_stages = stages_of(("a",))
    low_axes, high_axes = ("b", "h", "j"), ("h", "j", "b")

    def grow(x, came):
        return jnp.concatenate([x, came])

    def grow_all(x, stages):
        for axis, bit in stages:
            x = grow(x, flip(x, axis, bit))
        return x

    first = [up_rows[:cut_up], w_output[:cut_out], up_rows[cut_up:], w_output[cut_out:]]
    first, second = jnp.concatenate(first)[None], w_down[None]

    columns = jnp.stack(
        [w.reshape(part, group, pairs, 128) for w in (w_query, w_key, w_value)], axis=3
    ).reshape(part, group, 3 * width)
    columns = columns.transpose(1, 0, 2)
    columns = lax.all_to_all(columns, ("h", "c", "b"), 0, 0, tiled=True)
    columns = columns.reshape(1, group * part, 3 * width)

    blocks = 2 * group
    index = jnp.arange(blocks, dtype=jnp.int32)
    table = (member ^ (index % group)) * 2 + (parity ^ (index // group))
    positions_of = (parity ^ (index % 2)) * group + (member ^ (index // 2))
    lane, first = together(jnp.arange(128, dtype=jnp.int32), first)
    frequency = jnp.exp(
        (lane % (HEAD_DIM // 2)).astype(F32) * (-2.0 * math.log(10000.0) / HEAD_DIM)
    )
    angles = jnp.arange(length, dtype=jnp.int32).astype(F32)[:, None] * frequency[None, :]
    cosine = jnp.cos(angles)
    sine = jnp.sin(angles) * jnp.where((lane // (HEAD_DIM // 2)) % 2 == 0, -1.0, 1.0)[None, :]

    vectors, columns = together(
        jnp.stack(
            [attn_in_gain, attn_in_bias, attn_out_gain, attn_out_bias,
             mlp_in_gain, mlp_in_bias, mlp_out_gain, mlp_out_bias]
        ),
        columns,
    )
    vectors = jnp.broadcast_to(vectors[None], (devices,) + vectors.shape)
    vectors = lax.all_to_all(vectors, AXES, 0, 0, tiled=True)
    vectors = vectors.transpose(1, 0, 2).reshape(8, model).astype(F32)

    def columns_in_order(x):
        x = x[place_in(w_from)].reshape(2, na, nh, 2, nb, part, 3 * width)
        return x.transpose(0, 2, 3, 1, 4, 5, 6).reshape(model, 3 * width)

    own = [regroup(tokens, turn) for turn in range(2)]
    first_came = flip(first, *line_stages[0])
    w_came = flip(columns, *line_stages[0])
    own, first_came, w_came, second, cosine, sine, vectors = together(
        own, first_came, w_came, second, cosine, sine, vectors
    )
    first = grow_all(grow(first, first_came), line_stages[1:])
    wide = cut_up + cut_out
    low_stages, high_stages = stages_of(low_axes), stages_of(high_axes)
    first_low, first_high = first[:, :wide], first[:, wide:]
    columns = grow_all(grow(columns, w_came), line_stages[1:-1])
    second_came, w_came = flip(second, *line_stages[0]), flip(columns, *line_stages[-1])
    high_came = flip(first_high, *high_stages[0])
    pieces = {0: jnp.stack(own)}
    for bit in far_bits:
        for offset in list(pieces):
            pieces[offset ^ bit] = by_offset(pieces[offset], bit)
    pieces[core_bit] = by_offset(pieces[0], core_bit)
    pieces, high_came, second_came, w_came = together(pieces, high_came, second_came, w_came)
    second = grow_all(grow(second, second_came), line_stages[1:-1])
    columns = grow(columns, w_came)

    w_came = flip(columns, "j", 1)
    w_from = source_of(("a", "j"), ("j", "a"))
    low_came, second_came = flip(first_low, *low_stages[0]), flip(second, *line_stages[-1])
    for offset in range(1, group):
        if not offset & core_bit:
            pieces[offset ^ core_bit] = by_offset(pieces[offset], core_bit)
    pieces, w_came, low_came, second_came = together(pieces, w_came, low_came, second_came)
    if views:
        w_heads, w_shape = [columns, w_came], (na, nb, part)
    else:
        w_heads, w_shape = [columns_in_order(grow(columns, w_came))], None
    first_low = grow_all(grow(first_low, low_came), low_stages[1:-1])
    first_high = grow_all(grow(first_high, high_came), high_stages[1:-1])
    second = grow(second, second_came)
    pieces, first_low, first_high, second = together(pieces, first_low, first_high, second)
    low_came, high_came = flip(first_low, *low_stages[-1]), flip(first_high, *high_stages[-1])
    seconds = [second]
    if views:
        seconds += [flip(second, "b", 1), flip(second, "j", 1)]
    normed, queries, keys, values, w_heads = qkv_call(
        positions_of, w_from, [pieces[d] for d in range(group)], w_heads, vectors,
        cosine, sine, w_shape,
    )
    grad_in = [regroup(cotangent, 0)]
    attended, lse = attention_forward(table, queries, keys, values, rows)
    attended, lse, low_came, high_came, grad_in, cotangent = together(
        attended, lse, low_came, high_came, grad_in, cotangent
    )
    first_low, first_high = [first_low, low_came], [first_high, high_came]
    if views:
        near = source_of(("a",))
        over_b, over_j = (near // nb) * nb + (near % nb ^ 1), near ^ (na * nb)
        over_both = over_b ^ (na * nb)
        down_from = jnp.concatenate([near, over_b, over_j, over_both])
    else:
        seconds = [grow_all(second, stages_of(("h", "j", "b")))]
        down_from = source_of(("a", "h", "j", "b"))
    low_from, high_from = (source_of(("a",) + axes) for axes in (low_axes, high_axes))

    def exchange(x):
        return [x[0]] + [by_offset(x[d], d) for d in range(1, group)]

    order = jnp.stack([low_from, high_from, down_from])
    low_at, high_at = place_in(low_from), place_in(high_from)
    core_block = jnp.arange(2 * jh, dtype=jnp.int32)
    if views:
        mine = pick(first_low + first_high, cut_out)
        out_weights = [mine, flip(mine, "c", 1)]
    else:
        mine = jnp.concatenate(
            [jnp.concatenate([x[:, cut_up:] for x in pair]) for pair in (first_low, first_high)],
            axis=1,
        )
        mine = jnp.concatenate([mine[:, :cut_out][low_at], mine[:, cut_out:][high_at]], axis=1)
        mine = mine.reshape(jh, na * nb * part, model)
        other = flip(mine, "c", 1)
        w_out = jnp.where(
            ic == 0, jnp.stack([mine, other], axis=1), jnp.stack([other, mine], axis=1)
        ).reshape(group, width, model)
        out_weights = [w_out[member ^ jnp.arange(group)]]
    places = member ^ ((core_block % jh) * 2 + (ic ^ (core_block // jh)))
    mixed = exchange(attended.reshape(group, 2 * rows, width))
    projected, residual, mlp_mine, w_out = out_projection(
        order, places, mixed, own, vectors, out_weights, views
    )
    mlp_rows = [mlp_mine, flip(mlp_mine, "c", 1)]
    if views:
        mlp_rows, seconds = together(mlp_rows, seconds)
        seconds += [flip(seconds[1][: na // 2], "j", 1), flip(seconds[2][na // 2 :], "b", 1)]
    if views:
        tables = [order]
        up_weights = [(x, 2 * part) for x in first_low + first_high]
    else:
        tables = []
        up = [jnp.concatenate([x[:, :cut_up] for x in pair]) for pair in (first_low, first_high)]
        up = jnp.concatenate([up[0][low_at], up[1][high_at]], axis=1)
        up = up.reshape(jh, na, nb, jh, 2, part, unit)
        up_weights = [(up.transpose(0, 4, 1, 2, 5, 3, 6).reshape(model, jh * unit), model)]
    grad_in.append(regroup(cotangent, 1))
    pre_act, activated = mlp_call(
        mlp_up_kernel, "mlp_up", 11, mlp_rows, [], up_weights, tables,
        [(model, jh * unit)], 2, False,
    )
    activated, grad_in, seconds = together(activated, grad_in, seconds)
    if views:
        down_weights = [(x, n_down) for x in seconds]
    else:
        down = seconds[0][place_in(down_from)]
        down_weights = [(down.reshape(jh * unit, model), jh * unit)]
    branch, branch_other = mlp_call(
        mlp_down_kernel, "mlp_down", 9, [], [activated], down_weights, tables,
        [(jh * unit, model)], 0, True,
    )
    block_loose, branch_mine, mo_sums = row_call(
        middle_kernel, "middle", 3, rows,
        [branch, flip(branch_other, "c", 1), residual], grad_in, [vectors],
        [(model, BF), (model, BF)],
    )
    branch_rows = [branch_mine, flip(branch_mine, "c", 1)]

    def sends(x, axis, dim):
        return scatter_sends(x, axis, dim, 1) if lax.axis_size(axis) > 1 else (x, None)

    def send(pair, axis):
        return None if pair[1] is None else flip(pair[1], axis, 1)

    def added(pair, came, shape):
        return (pair[0] if came is None else join(pair[0], came)).reshape(shape)

    def sends_of(arrays, axis, dim):
        kept, given = zip(*[sends(x, axis, dim) for x in arrays])
        return list(kept), None if given[0] is None else jnp.concatenate(given, axis=-1)

    def added_of(kept, came, shape):
        out, start = [], 0
        for x in kept:
            width = x.shape[-1]
            if came is not None:
                x = join(x, came[..., start : start + width])
            out.append(x.reshape(shape + (width,)))
            start += width
        return out

    down_part = dot(activated, jnp.concatenate(branch_rows), TN).astype(BF)
    down_part = down_part.reshape(2, nh, na, nb, n_down, model)
    low_sends = sends(down_part[..., :cut, :], "b", 3)
    high_sends = sends(down_part[..., cut:, :], "j", 0)
    branch_rows, low_sends, high_sends, block_loose = together(
        branch_rows, low_sends, high_sends, block_loose
    )
    half_b, halves_b = (ib if nb > 1 else None), min(nb, 2)
    low_bit, next_bit = ia % 2, (ia // 2) % 2
    low_came, high_came = send(low_sends, "b"), send(high_sends, "j")
    block_came = [restore(block_loose[:rows], 0), restore(block_loose[rows:], 1)]
    pre_low, grad_mlp, grad_other = mlp_call(
        mlp_backward_kernel, "mlp_backward", 20, branch_rows, [pre_act],
        up_weights + down_weights, tables, [(model, jh * unit), (jh * unit, model)], 1, True,
    )
    pre_low, grad_mlp, grad_other, low_came, high_came, block_came = together(
        pre_low, grad_mlp, grad_other, low_came, high_came, block_came
    )
    grad_other = flip(grad_other, "c", 1)
    low_sends, high_sends = relay(
        [
            (ij, (1, 2, nh * na * cut), [(low_sends[0], low_came, 0)]),
            (half_b, (nh * na, halves_b, cut), [(high_sends[0], high_came, 0)]),
        ],
        views,
    )
    grad_mlp, grad_other, low_sends, high_sends = together(
        grad_mlp, grad_other, low_sends, high_sends
    )
    low_came, high_came = send(low_sends, "j"), send(high_sends, "b")
    grad_residual, projected_low, *attended_low, turn_sums = row_call(
        functools.partial(turn_kernel, group=group), "turn", 6, rows,
        [grad_mlp, grad_other, residual, projected], grad_in, [vectors, w_out],
        [(model, F32), (model, BF)] + [(width, BF)] * group, limit=60,
    )
    attended_low, projected_low, pre_low, low_came, high_came, block_came = together(
        attended_low, projected_low, pre_low, low_came, high_came, block_came
    )
    grad_heads = exchange(attended_low)
    grad_heads[1], pre_low = together(grad_heads[1], pre_low)
    grad_heads = jnp.stack(grad_heads).reshape(blocks, rows, width)
    down_pieces = [(low_sends[0][0], low_came, 0), (high_sends[0][0], high_came, 0)]
    (down_sends,) = relay([(low_bit, (na // 2, 2, cut), down_pieces)], views)
    up_part = dot(jnp.concatenate(mlp_rows), pre_low, TN).astype(BF)
    up_part = up_part.reshape(2, nh, 2, na, nb, part, jh * unit)
    grad_out = jnp.stack([dot(mixed[d], projected_low, TN).astype(BF) for d in range(group)])
    grad_out = jnp.stack(
        [lax.dynamic_index_in_dim(grad_out, member ^ m, 0, keepdims=False) for m in range(group)]
    ).reshape(2, nh, 2, na, nb, part, model)
    grad_out = scatter_axis(grad_out, "c", 2)
    low_sends = sends_of([up_part[:, :, 0], grad_out[..., : model // 2]], "j", 0)
    high_sends = sends_of([up_part[:, :, 1], grad_out[..., model // 2 :]], "b", 3)
    grad_heads, down_sends, low_sends, high_sends = together(
        grad_heads, down_sends, low_sends, high_sends
    )

    def backward(pair, grads):
        return attention_backward(
            table, pair, queries, keys, values, attended, grads, lse, cosine, sine
        )

    units = jh * unit
    low_came, high_came = send(low_sends, "j"), send(high_sends, "b")
    down_came = send(down_sends, "a")
    grad_pairs = [backward(0, grad_heads)]
    weight_pairs = [dot(normed, grad_pairs[0], TN).astype(BF)]
    weight_pairs, down_came, low_came, high_came = together(
        weight_pairs, down_came, low_came, high_came
    )
    low_pieces = [(low_sends[0][0], low_came, 0), (low_sends[0][1], low_came, units)]
    high_pieces = [(high_sends[0][0], high_came, 0), (high_sends[0][1], high_came, units)]
    down_pieces = [(down_sends[0][0], down_came, 0), (down_sends[0][1], down_came, model)]
    low_sends, high_sends, down_sends = relay(
        [
            (half_b, (na, halves_b, part), low_pieces),
            (ij, (1, 2, nh * na * part), high_pieces),
            (next_bit, (na // 4, 2, cut), down_pieces),
        ],
        views,
    )
    heads_in = [
        lax.all_to_all(weight_pairs[0].reshape(devices, part, 384), AXES, 0, 0, tiled=True)
    ]
    if pairs > 1:
        grad_heads, down_sends, low_sends, high_sends, weight_pairs = together(
            grad_heads, down_sends, low_sends, high_sends, weight_pairs
        )
    down_came, low_came = flip(down_sends[1], "a", 2), send(low_sends, "b")
    high_came = send(high_sends, "j")
    if pairs > 1:
        grad_pairs.append(backward(1, grad_heads))
    grads_give = [d for d in range(group) if d & core_bit]
    block_order = [2 * d + r for d in grads_give for r in range(2)]
    block_order += [2 * (d ^ core_bit) + r for d in grads_give for r in range(2)]
    grad_pairs, down_came, low_came, high_came, heads_in = together(
        grad_pairs, down_came, low_came, high_came, heads_in
    )
    rest_pieces = [
        (x, came, at)
        for (kept, _), came in ((low_sends, low_came), (high_sends, high_came))
        for x, at in zip(kept, (0, units))
    ]
    (rest_sends,) = relay([(low_bit, (na // 2, 2, part), rest_pieces)], views)
    grad_pairs, rest_sends = together(grad_pairs, rest_sends)
    rest_came = send(rest_sends, "a")
    grad_give, grad_keep = input_grad(
        positions_of[jnp.array(block_order, jnp.int32)], grad_pairs, w_heads, rows
    )
    grad_give, grad_keep, grad_pairs = together(grad_give, grad_keep, grad_pairs)
    give_came = by_offset(grad_give, core_bit)
    give_came, grad_keep = together(give_came, grad_keep)

    grad_keep = join(grad_keep, give_came)
    sums = {
        d ^ core_bit: [grad_keep[2 * n + r] for r in range(2)] for n, d in enumerate(grads_give)
    }
    for bit in far_bits[:-1]:
        for d in [d for d in sums if d & bit]:
            gone = sums.pop(d)
            for r in range(2):
                sums[d ^ bit][r] = join(sums[d ^ bit][r], by_offset(gone[r], bit))
    sums, grad_pairs = together(sums, grad_pairs)
    if far_bits:
        final = [by_offset(x, far_bits[-1]) for x in sums[far_bits[-1]]]
    weight_pairs = [dot(normed, x, TN).astype(BF) for x in grad_pairs[1:]]
    weight_pairs, rest_came = together(weight_pairs, rest_came)
    for x in weight_pairs:
        heads_in.append(lax.all_to_all(x.reshape(devices, part, 384), AXES, 0, 0, tiled=True))
    starts = (0, units, units + model // 2, 2 * units + model // 2)
    rest_pieces = [(x, rest_came, at) for x, at in zip(rest_sends[0], starts)]
    (rest_sends,) = relay([(next_bit, (na // 4, 2, part), rest_pieces)], views)
    rest_came = flip(rest_sends[1], "a", 2)
    if far_bits:
        final[0], down_came, block_came = together(final[0], down_came, block_came)
        final[1], rest_came = together(final[1], rest_came)
    down_parts = added_of(down_sends[0], down_came, (na // 4, cut))
    down_part = jnp.concatenate([scatter_axis(x, "a", 0, 4) for x in down_parts])
    block_out = ordered(*block_came)

    small, totals = mo_sums + turn_sums, []
    for r in range(2):
        parts = [sums[0][r]] + ([final[r]] if far_bits else [])
        total, sums_in = row_call(
            last_kernel, "last", 2, rows,
            [own[r], (grad_residual, r)] + parts, [], [vectors],
            [(model, BF)],
        )
        small = small + sums_in
        if r == 0 and far_bits:
            total, final[1] = together(total, final[1])
        totals.append(total)
    grad_tokens = [restore(total, r) for r, total in enumerate(totals)]
    rest_parts = added_of(rest_sends[0], rest_came, (na // 4, part))
    low_up, low_out, high_up, high_out = (scatter_axis(x, "a", 0, 4) for x in rest_parts)
    small = small.reshape(8, 2, nh, 2, na, nb, part).transpose(3, 5, 1, 2, 4, 0, 6)
    for axis in ("c", "b", "j", "h", "a"):
        small = scatter_axis(small, axis, 0, kind=F32)
    grad_tokens = ordered(*grad_tokens)

    def spread(m):
        hc, b = divmod(m, nb)
        return [place(j, hc // 2, hc % 2, a, b) for j in range(2) for a in range(na)]

    g_query, g_key, g_value = head_sum(heads_in, group, spread)
    g_down, g_out = down_part.astype(F32), jnp.concatenate([low_out, high_out], axis=1).astype(F32)
    up_part = jnp.stack([low_up, high_up])
    up_keep = lax.dynamic_index_in_dim(up_part, ic, 0, keepdims=False).reshape(part, jh, unit)
    up_give = lax.dynamic_index_in_dim(up_part, 1 - ic, 0, keepdims=False)
    up_come = flip(up_give, "c", 1).reshape(part, jh, unit)
    g_up = jnp.where(
        ic == 0, jnp.stack([up_keep, up_come], axis=2), jnp.stack([up_come, up_keep], axis=2)
    ).reshape(part, ff).astype(F32)

    return (
        block_out, grad_tokens, g_query, g_key, g_value, g_out, g_up, g_down,
        small[0], small[1], small[2], small[3], small[4], small[5], small[6], small[7],
    )


def solution(mesh):
    fsdp, seq = mesh.shape["fsdp"], mesh.shape["seq"]
    inner = Mesh(mesh.devices.reshape(2, fsdp // 4, 2, fsdp, seq // fsdp), AXES)
    lead, line = ("j", "h", "c"), ("a", "b")
    acts = P(lead, line, None)
    weights = P(lead + line, None)
    vector = P(lead + line)
    return jax.shard_map(
        body,
        mesh=inner,
        in_specs=(acts,) * 2 + (weights,) * 6 + (vector,) * 8,
        out_specs=(acts,) * 2 + (weights,) * 6 + (vector,) * 8,
        check_vma=False,
    )
```

```python
import functools
import math

import jax
import jax.numpy as jnp
from jax import lax
from jax.experimental import pallas as pl
from jax.experimental.pallas import tpu as pltpu
from jax.sharding import Mesh
from jax.sharding import PartitionSpec as P

HEADS = 16
HEAD_DIM = 64
EPSILON = 1e-05
NEGATIVE = -1e30
LOG2E = math.log2(math.e)
AXES = ("j", "h", "c", "a", "b")
BF = jnp.bfloat16
F32 = jnp.float32
NT = (((1,), (1,)), ((), ()))
NN = (((1,), (0,)), ((), ()))
TN = (((0,), (0,)), ((), ()))


def cost(us):
    return pl.CostEstimate(flops=int(us * 1e6), bytes_accessed=1 << 10, transcendentals=0)


def dot(left, right, dims=NN):
    return lax.dot_general(left, right, dims, preferred_element_type=F32)


def qkv_kernel(table, order, *refs, group, shape):
    x_refs, w_refs = refs[:group], refs[group:-9]
    vec_ref, cos_ref, sin_ref, n_ref, q_ref, k_ref, v_ref, w_ref, held = refs[-9:]
    step = pl.program_id(0)

    @pl.when(step == 0)
    def _():
        if shape is None:
            w_ref[...] = w_refs[0][...]
            return
        na, nb, part = shape
        sources = w_refs[0].shape[0]
        for n in range(len(w_refs) * sources):
            j, a = order[n] // na, order[n] % na
            for m in range(group):
                row = ((j * (group // nb) + m // nb) * na + a) * nb + m % nb
                start = pl.multiple_of(row * part, part)
                block = w_refs[n // sources][n % sources, m * part : (m + 1) * part, :]
                w_ref[pl.ds(start, part), :] = block

    for n in range(group):

        @pl.when(step // 2 == n)
        def _(n=n):
            held[...] = x_refs[n][step % 2]

    x = held[...].astype(F32)
    center = x - jnp.mean(x, axis=1, keepdims=True)
    rstd = lax.rsqrt(jnp.mean(center * center, axis=1, keepdims=True) + EPSILON)
    normed = (center * rstd * vec_ref[0:1] + vec_ref[1:2]).astype(BF)
    n_ref[...] = normed
    full = dot(normed, w_ref[...])
    lane = lax.broadcasted_iota(jnp.int32, (1, 128), 1)
    first = (lane % HEAD_DIM) < HEAD_DIM // 2
    cosine, sine = cos_ref[...], sin_ref[...]
    for pair in range(q_ref.shape[1] // 128):
        at = slice(pair * 128, (pair + 1) * 128)
        for which, out, scale in ((0, q_ref, LOG2E * HEAD_DIM**-0.5), (1, k_ref, 1.0)):
            t = full[:, (3 * pair + which) * 128 : (3 * pair + which + 1) * 128]
            other = jnp.where(first, pltpu.roll(t, 96, 1), pltpu.roll(t, 32, 1))
            out[:, at] = ((t * cosine + other * sine) * scale).astype(BF)
        v_ref[:, at] = full[:, (3 * pair + 2) * 128 : (3 * pair + 3) * 128].astype(BF)


def qkv_call(table, order, pieces, w, vec, cosine, sine, shape):
    group = len(pieces)
    _, rows, model = pieces[0].shape
    width = model // group
    length = 2 * group * rows
    at = lambda i, *t: (t[0][i], 0)
    fixed = lambda shape: pl.BlockSpec(
        shape, lambda i, *t: (0,) * len(shape), pipeline_mode=pl.Buffered(1)
    )
    return pl.pallas_call(
        functools.partial(qkv_kernel, group=group, shape=shape),
        out_shape=[jax.ShapeDtypeStruct((length, model), BF)]
        + [jax.ShapeDtypeStruct((length, width), BF)] * 3
        + [jax.ShapeDtypeStruct((model, 3 * width), BF)],
        grid_spec=pltpu.PrefetchScalarGridSpec(
            num_scalar_prefetch=2,
            grid=(2 * group,),
            in_specs=[fixed((2, rows, model))] * group
            + [fixed(x.shape) for x in (*w, vec)]
            + [pl.BlockSpec((rows, 128), at)] * 2,
            out_specs=[pl.BlockSpec((rows, model), at)]
            + [pl.BlockSpec((rows, width), at)] * 3
            + [fixed((model, 3 * width))],
            scratch_shapes=[pltpu.VMEM((rows, model), BF)],
        ),
        compiler_params=pltpu.CompilerParams(
            dimension_semantics=("arbitrary",), vmem_limit_bytes=60 << 20
        ),
        cost_estimate=cost(11),
        name="qkv",
    )(table, order, *pieces, *w, vec, cosine, sine)


def forward_kernel(table, q_ref, k_ref, v_ref, o_ref, lse_ref, vaug, *, bq, bk, rows):
    i = pl.program_id(1)
    lane = lax.broadcasted_iota(jnp.int32, (1, 128), 1)
    low = lane < HEAD_DIM

    @pl.when(i == 0)
    def _():
        v = v_ref[...]
        one = jnp.ones_like(v)
        vaug[0] = jnp.where(low, v, one)
        vaug[1] = jnp.where(low, one, v)

    parts = bq // bk
    heads = []
    for n in range(parts):
        q = q_ref[n * bk : (n + 1) * bk, :]
        zero = jnp.zeros_like(q)
        heads.append((jnp.where(low, q, zero), jnp.where(low, zero, q)))

    def step(kb, carry, first, masked):
        start = pl.multiple_of(kb * bk, bk)
        k_blk = k_ref[pl.ds(start, bk), :]
        out = list(carry)
        for n in range(first, parts):
            for h in range(2):
                top, acc = carry[2 * n + h]
                s = dot(heads[n][h], k_blk, NT)
                if masked and n == first:
                    row = lax.broadcasted_iota(jnp.int32, s.shape, 0)
                    col = lax.broadcasted_iota(jnp.int32, s.shape, 1)
                    s = jnp.where(col <= row, s, NEGATIVE)
                new = jnp.maximum(top, jnp.max(s, axis=1, keepdims=True))
                p = jnp.exp2(s - new)
                acc = acc * jnp.exp2(top - new) + dot(p.astype(BF), vaug[h, pl.ds(start, bk), :])
                out[2 * n + h] = (new, acc)
        return tuple(out)

    carry = tuple(
        (jnp.full((bk, 1), NEGATIVE, F32), jnp.zeros((bk, 128), F32)) for _ in range(2 * parts)
    )
    full = i * parts
    carry = lax.fori_loop(0, full, lambda kb, c: step(kb, c, 0, False), carry)
    for d in range(parts):
        carry = step(full + d, carry, d, True)
    for n in range(parts):
        (top0, acc0), (top1, acc1) = carry[2 * n : 2 * n + 2]
        total = pltpu.roll(jnp.where(low, acc1, acc0), HEAD_DIM, 1)
        o = (jnp.where(low, acc0, acc1) / total).astype(BF)
        for d in range(bk // rows):
            o_ref[table[(full + n) * (bk // rows) + d]] = o[d * rows : (d + 1) * rows]
        lse_ref[n * bk : (n + 1) * bk, :] = jnp.where(low, top0, top1) + jnp.log2(total)


def attention_forward(table, q, k, v, rows):
    length, width = q.shape
    bq, bk = min(2048, length), min(512, length)
    blocks = length // rows
    return pl.pallas_call(
        functools.partial(forward_kernel, bq=bq, bk=bk, rows=rows),
        out_shape=[
            jax.ShapeDtypeStruct((blocks, rows, width), BF),
            jax.ShapeDtypeStruct((length, width), F32),
        ],
        grid_spec=pltpu.PrefetchScalarGridSpec(
            num_scalar_prefetch=1,
            grid=(width // 128, length // bq),
            in_specs=[
                pl.BlockSpec((bq, 128), lambda p, i, t: (i, p)),
                pl.BlockSpec((length, 128), lambda p, i, t: (0, p)),
                pl.BlockSpec((length, 128), lambda p, i, t: (0, p)),
            ],
            out_specs=[
                pl.BlockSpec((blocks, rows, 128), lambda p, i, t: (0, 0, p)),
                pl.BlockSpec((bq, 128), lambda p, i, t: (i, p)),
            ],
            scratch_shapes=[pltpu.VMEM((2, length, 128), BF)],
        ),
        compiler_params=pltpu.CompilerParams(
            dimension_semantics=("arbitrary", "arbitrary"), vmem_limit_bytes=60 << 20
        ),
        cost_estimate=cost(23),
        name="attention_forward",
    )(table, q, k, v)


def split3(x):
    high = x.astype(BF)
    rest = x - high.astype(F32)
    mid = rest.astype(BF)
    return high, mid, (rest - mid.astype(F32)).astype(BF)


def backward_kernel(
    table, q_ref, k_ref, v_ref, o_ref, do_ref, lse_ref, cos_ref, sin_ref, ck_ref, sk_ref,
    d_ref, qa, da, dqt, *, bk, rows
):
    j = pl.program_id(0)
    length = q_ref.shape[0]
    lane = lax.broadcasted_iota(jnp.int32, (1, 128), 1)
    low = lane < HEAD_DIM
    first = (lane % HEAD_DIM) < HEAD_DIM // 2

    def unturn(t, cosine, sine):
        other = jnp.where(first, pltpu.roll(t, 96, 1), pltpu.roll(t, 32, 1))
        return t * cosine - other * sine

    @pl.when(j == 0)
    def _():
        dqt[...] = jnp.zeros_like(dqt)

        def prep(b, _):
            r = pl.ds(pl.multiple_of(b * rows, rows), rows)
            q, do = q_ref[r, :], do_ref[table[b]]
            product = o_ref[table[b]].astype(F32) * do.astype(F32)
            for h in range(2):
                mine = low if h == 0 else jnp.logical_not(low)
                base = HEAD_DIM if h == 0 else 0
                delta = -jnp.sum(jnp.where(mine, product, 0.0), axis=1, keepdims=True)
                lse = -lse_ref[r, HEAD_DIM * h : HEAD_DIM * h + 1]
                for source, value, target in ((q, lse, qa), (do, delta, da)):
                    x = jnp.where(mine, source, jnp.zeros_like(source))
                    for n, part in enumerate(split3(value)):
                        x = jnp.where(lane == base + n, part, x)
                    target[h, r, :] = x
            return 0

        lax.fori_loop(0, length // rows, prep, 0)

    k, v = k_ref[...], v_ref[...]
    one, zero = jnp.ones_like(k), jnp.zeros_like(k)
    ka, va, kt = [], [], []
    for h in range(2):
        mine = low if h == 0 else jnp.logical_not(low)
        base = HEAD_DIM if h == 0 else 0
        extra = jnp.where(jnp.logical_and(lane >= base, lane < base + 3), one, zero)
        ka.append(jnp.where(mine, k, extra))
        va.append(jnp.where(mine, v, extra))
        kt.append(jnp.where(mine, k, zero).T)

    def products(h, keys, r, masked):
        qh, dh = qa[h, r, :], da[h, r, :]
        st = dot(ka[h][keys], qh, NT)
        if masked:
            key = lax.broadcasted_iota(jnp.int32, st.shape, 0)
            query = lax.broadcasted_iota(jnp.int32, st.shape, 1)
            st = jnp.where(key <= query, st, NEGATIVE)
        p = jnp.exp2(st)
        ds = (p * dot(va[h][keys], dh, NT)).astype(BF)
        return dot(ds, qh), dot(p.astype(BF), dh), ds

    def step(qb, carry):
        r = pl.ds(pl.multiple_of(qb * bk, bk), bk)
        out, low_scores = [], []
        for h in range(2):
            dk, dv, ds = products(h, slice(None), r, False)
            out.append((carry[h][0] + dk, carry[h][1] + dv))
            low_scores.append(ds)
        dqt[:, r] += dot(kt[0], low_scores[0]) + dot(kt[1], low_scores[1])
        return tuple(out)

    half = bk // 2
    carry = []
    upper = pl.ds(pl.multiple_of(j * bk, bk), bk)
    lower = pl.ds(pl.multiple_of(j * bk + half, half), half)
    firsts = [products(h, slice(0, half), upper, True) for h in range(2)]
    seconds = [products(h, slice(half, bk), lower, True) for h in range(2)]
    for h in range(2):
        carry.append(
            tuple(jnp.concatenate([firsts[h][n], seconds[h][n]], axis=0) for n in range(2))
        )
    dqt[:, upper] += dot(kt[0][:, :half], firsts[0][2]) + dot(kt[1][:, :half], firsts[1][2])
    dqt[:, lower] += dot(kt[0][:, half:], seconds[0][2]) + dot(kt[1][:, half:], seconds[1][2])
    carry = lax.fori_loop(j + 1, length // bk, step, tuple(carry))
    (dk0, dv0), (dk1, dv1) = carry
    dk = unturn(jnp.where(low, dk0, dk1) * (1.0 / LOG2E), ck_ref[...], sk_ref[...])
    mine = pl.ds(pl.multiple_of(j * bk, bk), bk)
    d_ref[mine, 128:256] = dk.astype(BF)
    d_ref[mine, 256:384] = jnp.where(low, dv0, dv1).astype(BF)

    @pl.when(j == pl.num_programs(0) - 1)
    def _():
        dq = dqt[...].T * HEAD_DIM**-0.5
        d_ref[:, 0:128] = unturn(dq, cos_ref[...], sin_ref[...]).astype(BF)


def attention_backward(table, pair, q, k, v, o, do, lse, cosine, sine):
    length = q.shape[0]
    blocks, rows, _ = o.shape
    bk = min(512, length)
    full = pl.BlockSpec((length, 128), lambda j, t: (0, pair))
    block = pl.BlockSpec((bk, 128), lambda j, t: (j, pair))
    loose = pl.BlockSpec((blocks, rows, 128), lambda j, t: (0, 0, pair))
    return pl.pallas_call(
        functools.partial(backward_kernel, bk=bk, rows=rows),
        out_shape=jax.ShapeDtypeStruct((length, 384), BF),
        grid_spec=pltpu.PrefetchScalarGridSpec(
            num_scalar_prefetch=1,
            grid=(length // bk,),
            in_specs=[
                full, block, block, loose, loose, full,
                pl.BlockSpec((length, 128), lambda j, t: (0, 0)),
                pl.BlockSpec((length, 128), lambda j, t: (0, 0)),
                pl.BlockSpec((bk, 128), lambda j, t: (j, 0)),
                pl.BlockSpec((bk, 128), lambda j, t: (j, 0)),
            ],
            out_specs=pl.BlockSpec((length, 384), lambda j, t: (0, 0)),
            scratch_shapes=[
                pltpu.VMEM((2, length, 128), BF),
                pltpu.VMEM((2, length, 128), BF),
                pltpu.VMEM((128, length), F32),
            ],
        ),
        compiler_params=pltpu.CompilerParams(
            dimension_semantics=("arbitrary",), vmem_limit_bytes=(56 if pair else 28) << 20
        ),
        cost_estimate=cost(44),
        name="attention_backward",
    )(table, q, k, v, o, do, lse, cosine, sine, cosine, sine)


def gelu(v):
    return 0.5 * v * (1.0 + jnp.tanh(0.7978845608 * (v + 0.044715 * v * v * v)))


def gelu_slope(v):
    square = v * v
    t = jnp.tanh(0.7978845608 * v * (1.0 + 0.044715 * square))
    inner = 0.7978845608 * (1.0 + 3.0 * 0.044715 * square)
    return 0.5 * (1.0 + t) + 0.5 * v * (1.0 - t * t) * inner


def take(step, refs, held):
    for n, ref in enumerate(refs):

        @pl.when(step == n)
        def _(ref=ref):
            held[...] = ref[...].reshape(held.shape)

    return held[...]


def load_up(order, refs, up):
    pieces, (sources, rows, unit) = len(refs) // 2, refs[0].shape
    part, total = rows // 2, pieces * sources
    per = total // (up.shape[1] // unit)
    for which in range(2):
        for n in range(total):
            source = order[which, n]
            ref = refs[which * pieces + n // sources]
            base = (source // per) * 2 * per + source % per
            for c in range(2):
                start = pl.multiple_of((base + c * per) * part, part)
                up[pl.ds(start, part), which * unit : (which + 1) * unit] = ref[
                    n % sources, c * part : (c + 1) * part, :
                ]


def load_down(order, refs, down):
    at = 0
    for ref in refs:
        deep = ref.shape[1]
        for n in range(ref.shape[0]):
            down[pl.ds(pl.multiple_of(order[2, at] * deep, deep), deep), :] = ref[n]
            at += 1


def mlp_up_kernel(*refs, tables):
    pre_ref, act_ref, held = refs[tables + 2 :][-(3 + tables) :][:3]
    x_refs, weights = refs[tables : tables + 2], refs[tables + 2 : -(3 + tables)]
    up = weights[0]
    if tables:
        up = refs[-1]

        @pl.when(pl.program_id(0) == 0)
        def _():
            load_up(refs[0], weights, up)

    x = take(pl.program_id(0), x_refs, held)
    for n in range(up.shape[1] // x.shape[1]):
        at = slice(n * x.shape[1], (n + 1) * x.shape[1])
        pre = dot(x, up[:, at])
        pre_ref[:, at] = pre.astype(BF)
        act_ref[:, at] = gelu(pre).astype(BF)


def leave(total, own_ref, other_ref):
    @pl.when(pl.program_id(0) == 0)
    def _():
        own_ref[...] = total

    @pl.when(pl.program_id(0) == 1)
    def _():
        other_ref[...] = total.astype(BF)


def mlp_down_kernel(*refs, tables):
    act_ref, weights = refs[tables], refs[tables + 1 : -(2 + tables)]
    own_ref, other_ref = refs[tables + 1 :][-(2 + tables) :][:2]
    down = weights[0]
    if tables:
        down = refs[-1]

        @pl.when(pl.program_id(0) == 0)
        def _():
            load_down(refs[0], weights, down)

    leave(dot(act_ref[...], down[...]), own_ref, other_ref)


def mlp_backward_kernel(*refs, tables):
    g_refs, pre_ref, weights = refs[tables : tables + 2], refs[tables + 2], refs[tables + 3 : -(4 + 2 * tables)]
    low_ref, own_ref, other_ref, held = refs[tables + 3 :][-(4 + 2 * tables) :][:4]
    up, down = weights[0], weights[-1]
    if tables:
        up, down = refs[-2:]

        @pl.when(pl.program_id(0) == 0)
        def _():
            load_up(refs[0], weights[:4], up)
            load_down(refs[0], weights[4:], down)

    g = take(pl.program_id(0), g_refs, held)
    total = None
    for n in range(up.shape[1] // g.shape[1]):
        at = slice(n * g.shape[1], (n + 1) * g.shape[1])
        grad = dot(g, down[at, :], NT)
        low = (grad * gelu_slope(pre_ref[:, at].astype(F32))).astype(BF)
        low_ref[:, at] = low
        term = dot(low, up[:, at], NT)
        total = term if total is None else total + term
    leave(total, own_ref, other_ref)


def mlp_call(kernel, name, us, narrow, wide, weights, tables, scratch, wide_outs, split):
    count = (narrow or wide)[0].shape[0] if narrow else wide[0].shape[0] // 2
    model = weights[0][0].shape[-1] if tables else min(weights[0][0].shape)
    units = 2 * model if tables else max(weights[0][0].shape)
    fixed = lambda shape: pl.BlockSpec(
        shape, lambda m, *t: (0,) * len(shape), pipeline_mode=pl.Buffered(1)
    )
    wide_spec = pl.BlockSpec((count, units), lambda m, *t: (m, 0))
    return pl.pallas_call(
        functools.partial(kernel, tables=len(tables)),
        out_shape=[jax.ShapeDtypeStruct((2 * count, units), BF)] * wide_outs
        + [jax.ShapeDtypeStruct((count, model), kind) for kind in (F32, BF) if split],
        grid_spec=pltpu.PrefetchScalarGridSpec(
            num_scalar_prefetch=len(tables),
            grid=(2,),
            in_specs=[fixed((count, model))] * len(narrow)
            + [wide_spec] * len(wide)
            + [fixed(x.shape[:-2] + (rows, x.shape[-1])) for x, rows in weights],
            out_specs=[wide_spec] * wide_outs + [fixed((count, model))] * (2 * split),
            scratch_shapes=[pltpu.VMEM((count, model), BF)] * bool(narrow)
            + [pltpu.VMEM(shape, BF) for shape in scratch if tables],
        ),
        compiler_params=pltpu.CompilerParams(
            dimension_semantics=("arbitrary",), vmem_limit_bytes=56 << 20
        ),
        cost_estimate=cost(us),
        name=name,
    )(*tables, *narrow, *wide, *[x for x, _ in weights])


def relay_kernel(here, *refs, layout, arrivals):
    count = sum(len(pieces) for _, pieces in layout)
    kept, came = refs[:count], refs[count : count + arrivals]
    outs, given = refs[count + arrivals : 2 * count + arrivals], refs[2 * count + arrivals :]
    at = 0
    for g, (n, pieces) in enumerate(layout):
        mine = here[g]
        for start, source, offset in pieces:
            width = kept[at].shape[3]
            for i in range(n):
                for keep in (True, False):
                    half = mine if keep else 1 - mine
                    x = kept[at][i, half].astype(F32)
                    x = x + came[source][i, half, :, offset : offset + width].astype(F32)
                    if keep:
                        outs[at][i] = x.astype(BF)
                    else:
                        given[g][i, :, start : start + width] = x.astype(BF)
            at += 1


def relay(groups, fused):
    if not fused:
        results = []
        for here, (n, halves, m), pieces in groups:
            kept, given = [], []
            for x, came, offset in pieces:
                width = x.shape[-1]
                x = x.reshape(-1, width)
                if came is not None:
                    x = join(x, came.reshape(-1, came.shape[-1])[:, offset : offset + width])
                if x.shape[0] != n * halves * m:
                    x = scatter_axis(x.reshape(lax.axis_size("h"), -1, width), "h", 0)
                x = x.reshape(n, halves, m, width)
                mine = 0 if here is None else here
                kept.append(lax.dynamic_index_in_dim(x, mine, 1, keepdims=False))
                if here is not None:
                    given.append(lax.dynamic_index_in_dim(x, 1 - here, 1, keepdims=False))
            results.append((kept, jnp.concatenate(given, axis=-1) if given else None))
        return results
    kept, came, layout, widths = [], [], [], []
    for _, (n, halves, m), pieces in groups:
        start, entries = 0, []
        for x, arrived, offset in pieces:
            kept.append(x.reshape(n, halves, m, x.shape[-1]))
            if not any(arrived is y for y, _ in came):
                came.append((arrived, (n, halves, m, arrived.shape[-1])))
            source = [arrived is y for y, _ in came].index(True)
            entries.append((start, source, offset))
            start += x.shape[-1]
        layout.append((n, tuple(entries)))
        widths.append((n, m, start))
    came = [y.reshape(shape) for y, shape in came]
    shapes = [(x.shape[0],) + x.shape[2:] for x in kept] + widths
    fixed = lambda shape: pl.BlockSpec(
        tuple(shape), lambda i, t: (0,) * len(shape), pipeline_mode=pl.Buffered(1)
    )
    outs = pl.pallas_call(
        functools.partial(relay_kernel, layout=tuple(layout), arrivals=len(came)),
        out_shape=[jax.ShapeDtypeStruct(shape, BF) for shape in shapes],
        grid_spec=pltpu.PrefetchScalarGridSpec(
            num_scalar_prefetch=1,
            grid=(1,),
            in_specs=[fixed(x.shape) for x in kept + came],
            out_specs=[fixed(shape) for shape in shapes],
        ),
        compiler_params=pltpu.CompilerParams(
            dimension_semantics=("arbitrary",), vmem_limit_bytes=60 << 20
        ),
        cost_estimate=cost(4),
        name="relay",
    )(jnp.stack([here for here, *_ in groups]), *kept, *came)
    results, at = [], 0
    for g, (_, entries) in enumerate(layout):
        results.append((list(outs[at : at + len(entries)]), outs[len(kept) + g]))
        at += len(entries)
    return results


def spread_of(values):
    center = values - jnp.mean(values, axis=1, keepdims=True)
    rstd = lax.rsqrt(jnp.mean(center * center, axis=1, keepdims=True) + EPSILON)
    return center * rstd, rstd


def norm_slope(hat, rstd, gain, grad, sums_ref, at):
    scaled = grad * gain
    inner = scaled - jnp.mean(scaled, axis=1, keepdims=True)
    sums_ref[at : at + 1] += jnp.sum(grad * hat, axis=0, keepdims=True)
    sums_ref[at + 1 : at + 2] += jnp.sum(grad, axis=0, keepdims=True)
    return rstd * (inner - hat * jnp.mean(scaled * hat, axis=1, keepdims=True))


def clear_at_start(ref):
    @pl.when(pl.program_id(0) == 0)
    def _():
        ref[...] = jnp.zeros_like(ref)


def pick_kernel(*refs):
    out = refs[-1]
    sources, cut, _ = refs[0].shape
    for n, ref in enumerate(refs[:-1]):
        which, piece = divmod(n, (len(refs) - 1) // 2)
        out[piece * sources : (piece + 1) * sources, which * cut : (which + 1) * cut] = ref[...]


def pick(arrays, cut):
    sources, wide, model = arrays[0].shape
    spec = pl.BlockSpec((sources, cut, model), lambda i: (0, wide // cut - 1, 0))
    shape = (sources * len(arrays) // 2, 2 * cut, model)
    return pl.pallas_call(
        pick_kernel,
        out_shape=jax.ShapeDtypeStruct(shape, BF),
        grid=(1,),
        in_specs=[spec] * len(arrays),
        out_specs=pl.BlockSpec(shape, lambda i: (0, 0, 0)),
        cost_estimate=cost(2),
        name="pick",
    )(*arrays)


def out_kernel(order, places, *refs, group, views):
    projected_ref, residual_ref, normed_ref, w_ref, held = refs[-5:]
    mixed, tokens, vec_ref, weights = refs[:group], refs[group : group + 2], refs[group + 2], refs[group + 3 : -5]
    step = pl.program_id(0)

    @pl.when(step == 0)
    def _():
        if not views:
            w_ref[...] = weights[0][...]
            return
        sources, cut = weights[0].shape[0], weights[0].shape[1] // 2
        halves = places.shape[0] // 2
        per = sources // halves
        for which in range(2):
            for n in range(sources):
                source = order[which, n]
                start = pl.multiple_of((source % per) * 2 * cut + which * cut, cut)
                for core in range(2):
                    block = places[core * halves + source // per]
                    w_ref[block, pl.ds(start, cut), :] = weights[core][n, which * cut : (which + 1) * cut]

    projected = dot(mixed[0][...], w_ref[0])
    for d in range(1, group):
        projected = projected + dot(mixed[d][...], w_ref[d])
    projected_ref[...] = projected
    hat, _ = spread_of(projected)
    x = take(step, tokens, held).astype(F32)
    residual = x + hat * vec_ref[2:3] + vec_ref[3:4]
    residual_ref[...] = residual
    hat, _ = spread_of(residual)
    normed_ref[...] = (hat * vec_ref[4:5] + vec_ref[5:6]).astype(BF)


def out_projection(order, places, mixed, tokens, vec, weights, views):
    group = len(mixed)
    count, width = mixed[0].shape
    rows, model = tokens[0].shape
    fixed = lambda shape: pl.BlockSpec(shape, lambda i, *t: (0,) * len(shape))
    tall = pl.BlockSpec((rows, model), lambda i, *t: (i, 0))
    specs = [fixed(x.shape) for x in weights]
    return pl.pallas_call(
        functools.partial(out_kernel, group=group, views=views),
        out_shape=[
            jax.ShapeDtypeStruct((count, model), F32),
            jax.ShapeDtypeStruct((count, model), F32),
            jax.ShapeDtypeStruct((count, model), BF),
            jax.ShapeDtypeStruct((group, width, model), BF),
        ],
        grid_spec=pltpu.PrefetchScalarGridSpec(
            num_scalar_prefetch=2,
            grid=(count // rows,),
            in_specs=[pl.BlockSpec((rows, width), lambda i, *t: (i, 0))] * group
            + [fixed((rows, model))] * 2
            + [fixed(vec.shape)]
            + specs,
            out_specs=[tall, tall, tall, fixed((group, width, model))],
            scratch_shapes=[pltpu.VMEM((rows, model), BF)],
        ),
        compiler_params=pltpu.CompilerParams(
            dimension_semantics=("arbitrary",), vmem_limit_bytes=40 << 20
        ),
        cost_estimate=cost(5),
        name="out_projection",
    )(order, places, *mixed, *tokens, vec, *weights)


def middle_kernel(own_ref, came_ref, residual_ref, g0_ref, g1_ref, vec_ref, out_ref, low_ref, sums_ref, held):
    clear_at_start(sums_ref)
    hat, rstd = spread_of(own_ref[...] + came_ref[...].astype(F32))
    out_ref[...] = (residual_ref[...] + hat * vec_ref[6:7] + vec_ref[7:8]).astype(BF)
    grad = take(pl.program_id(0), (g0_ref, g1_ref), held).astype(F32)
    low_ref[...] = norm_slope(hat, rstd, vec_ref[6:7], grad, sums_ref, 6).astype(BF)


def turn_kernel(own_ref, came_ref, residual_ref, projected_ref, g0_ref, g1_ref, vec_ref, w_ref, *refs, group):
    grad_ref, low_ref, *heads, sums_ref, held = refs
    clear_at_start(sums_ref)
    hat, rstd = spread_of(residual_ref[...])
    grad = own_ref[...] + came_ref[...].astype(F32)
    passed = take(pl.program_id(0), (g0_ref, g1_ref), held).astype(F32)
    grad = passed + norm_slope(hat, rstd, vec_ref[4:5], grad, sums_ref, 4)
    grad_ref[...] = grad
    hat, rstd = spread_of(projected_ref[...])
    low = norm_slope(hat, rstd, vec_ref[2:3], grad, sums_ref, 2).astype(BF)
    low_ref[...] = low
    for d in range(group):
        heads[d][...] = dot(low, w_ref[d], NT).astype(BF)


def last_kernel(x_ref, grad_ref, *refs):
    *parts, vec_ref, out_ref, sums_ref = refs
    clear_at_start(sums_ref)
    hat, rstd = spread_of(x_ref[...].astype(F32))
    grad = parts[0][...].astype(F32)
    for part in parts[1:]:
        grad = grad + part[...].astype(F32)
    grad = norm_slope(hat, rstd, vec_ref[0:1], grad, sums_ref, 0)
    out_ref[...] = (grad_ref[...] + grad).astype(BF)


def row_call(kernel, name, us, rows, tall, halves, fixed, outs, limit=40):
    model = tall[0].shape[1]
    count = tall[0].shape[0]
    starts = [at[1] if isinstance(at, tuple) else 0 for at in tall]
    tall = [at[0] if isinstance(at, tuple) else at for at in tall]
    whole = lambda x: pl.BlockSpec(x.shape, lambda i, n=x.ndim: (0,) * n)
    block = lambda width: pl.BlockSpec((rows, width), lambda i: (i, 0))
    return pl.pallas_call(
        kernel,
        out_shape=[jax.ShapeDtypeStruct((count, width), kind) for width, kind in outs]
        + [jax.ShapeDtypeStruct((8, model), F32)],
        grid=(count // rows,),
        in_specs=[
            pl.BlockSpec((rows, model), lambda i, start=start: (i + start, 0)) for start in starts
        ]
        + [whole(x) for x in (*halves, *fixed)],
        out_specs=[block(width) for width, _ in outs] + [pl.BlockSpec((8, model), lambda i: (0, 0))],
        scratch_shapes=[pltpu.VMEM((rows, model), BF)] if halves else [],
        compiler_params=pltpu.CompilerParams(
            dimension_semantics=("arbitrary",), vmem_limit_bytes=limit << 20
        ),
        cost_estimate=cost(us),
        name=name,
    )(*tall, *halves, *fixed)


def input_grad_kernel(table, *refs):
    w_ref, give_ref, keep_ref = refs[-3:]
    total = None
    for n, ref in enumerate(refs[:-3]):
        term = dot(ref[...], w_ref[:, n * 384 : (n + 1) * 384], NT)
        total = term if total is None else total + term
    giving = pl.program_id(0) < pl.num_programs(0) // 2

    @pl.when(giving)
    def _():
        give_ref[0] = total.astype(BF)

    @pl.when(jnp.logical_not(giving))
    def _():
        keep_ref[0] = total.astype(BF)


def input_grad(table, grads, w, rows):
    model = w.shape[0]
    blocks = grads[0].shape[0] // rows
    half = blocks // 2
    return pl.pallas_call(
        input_grad_kernel,
        out_shape=[jax.ShapeDtypeStruct((half, rows, model), BF)] * 2,
        grid_spec=pltpu.PrefetchScalarGridSpec(
            num_scalar_prefetch=1,
            grid=(blocks,),
            in_specs=[pl.BlockSpec((rows, 384), lambda i, t: (t[i], 0))] * len(grads)
            + [pl.BlockSpec(w.shape, lambda i, t: (0, 0))],
            out_specs=[
                pl.BlockSpec((1, rows, model), lambda i, t: (jnp.minimum(i, half - 1), 0, 0)),
                pl.BlockSpec((1, rows, model), lambda i, t: (jnp.maximum(i - half, 0), 0, 0)),
            ],
        ),
        compiler_params=pltpu.CompilerParams(
            dimension_semantics=("arbitrary",), vmem_limit_bytes=40 << 20
        ),
        cost_estimate=cost(6),
        name="input_grad",
    )(table, *grads, w)


def head_sum_kernel(*refs, group, spread):
    x_refs, outs = refs[:-3], refs[-3:]
    width = outs[0].shape[1] // group
    for m in range(group):
        for pair, ref in enumerate(x_refs):
            total = None
            for n in spread(m):
                term = ref[n].astype(F32)
                total = term if total is None else total + term
            at = slice(m * width + pair * 128, m * width + (pair + 1) * 128)
            for which, out in enumerate(outs):
                out[:, at] = total[:, which * 128 : (which + 1) * 128]


def head_sum(parts, group, spread):
    _, rows, wide = parts[0].shape
    return pl.pallas_call(
        functools.partial(head_sum_kernel, group=group, spread=spread),
        out_shape=[jax.ShapeDtypeStruct((rows, group * len(parts) * wide // 3), F32)] * 3,
        cost_estimate=cost(2),
        name="head_sum",
    )(*parts)


def flip(x, axis, bit):
    size = lax.axis_size(axis)
    return lax.ppermute(x, axis, [(i, i ^ bit) for i in range(size)])


def scatter_sends(x, axis, dim, bit):
    here = (lax.axis_index(axis) // bit) % 2
    shape = x.shape
    x = x.reshape(shape[:dim] + (shape[dim] // 2, 2) + shape[dim + 1 :])
    mine = lax.dynamic_index_in_dim(x, here, dim + 1, keepdims=False)
    return mine, lax.dynamic_index_in_dim(x, 1 - here, dim + 1, keepdims=False)


def join(mine, came, kind=BF):
    return (mine.astype(F32) + came.astype(F32)).astype(kind)


def scatter_axis(x, axis, dim, bit=1, kind=BF):
    size = lax.axis_size(axis)
    while bit < size:
        mine, theirs = scatter_sends(x, axis, dim, bit)
        x = join(mine, flip(theirs, axis, bit), kind)
        bit *= 2
    return x.reshape(x.shape[:dim] + x.shape[dim + 1 :])


def together(*groups):
    flat, tree = jax.tree.flatten(groups)
    return jax.tree.unflatten(tree, lax.optimization_barrier(tuple(flat)))


def place_in(order):
    index = jnp.arange(order.shape[0], dtype=jnp.int32)
    return jnp.sum(jnp.where(order[:, None] == index[None, :], index[:, None], 0), axis=0)


def gather_order(axes):
    masks = {axis: [0] for axis in AXES}
    for axis in axes:
        bit = lax.axis_size(axis) // 2
        while bit:
            for name in AXES:
                step = bit if name == axis else 0
                masks[name] = masks[name] + [m ^ step for m in masks[name]]
            bit //= 2
    return {axis: jnp.array(masks[axis], jnp.int32) for axis in AXES}


def source_of(axes, along=("j", "h", "a", "b")):
    masks, total = gather_order(axes), 0
    for axis in along:
        total = total * lax.axis_size(axis) + (lax.axis_index(axis) ^ masks[axis])
    return total


def stages_of(axes):
    stages = []
    for axis in axes:
        bit = lax.axis_size(axis) // 2
        while bit:
            stages.append((axis, bit))
            bit //= 2
    return stages


def after(x, *others):
    return lax.optimization_barrier((x,) + others)[0]


def body(
    tokens, cotangent, w_query, w_key, w_value, w_output, w_up, w_down,
    attn_in_gain, attn_in_bias, attn_out_gain, attn_out_bias,
    mlp_in_gain, mlp_in_bias, mlp_out_gain, mlp_out_bias,
):
    _, rows, model = tokens.shape
    nh, na, nb = lax.axis_size("h"), lax.axis_size("a"), lax.axis_size("b")
    jh = 2 * nh
    devices = 4 * nh * na * nb
    group = 2 * nh * nb
    half = na // 2
    length = rows * na * nb
    width = model // group
    pairs = width // 128
    part = w_query.shape[0]
    ij, ih, ic, ia, ib = (lax.axis_index(axis) for axis in AXES)
    slot, parity = ia // half, ia % 2
    member = (ih * 2 + ic) * nb + ib

    def place(j, h, c, a, b):
        return (((j * nh + h) * 2 + c) * na + a) * nb + b

    everyone = [
        (j, h, c, a, b)
        for j in range(2)
        for h in range(nh)
        for c in range(2)
        for a in range(na)
        for b in range(nb)
    ]
    moves = ([], [])
    for turn in range(2):
        for j, h, c, a, b in everyone:
            to_h, to_c = divmod(a % half, 2)
            plane = (h * 2 + c) * 2 + (turn + a // half) % 2
            target = place(j, to_h, to_c, plane, b)
            moves[turn].append((place(j, h, c, a, b), target))

    def regroup(x, turn):
        x = lax.dynamic_index_in_dim(x, (turn + slot) % 2, 0, keepdims=False)
        return lax.ppermute(x, AXES, moves[turn])

    def restore(x, turn):
        return lax.ppermute(x, AXES, [(there, here) for here, there in moves[turn]])

    def ordered(first, second):
        swap = slot == 1
        return jnp.stack([jnp.where(swap, second, first), jnp.where(swap, first, second)])

    def by_offset(x, offset):
        sends = []
        for j, h, c, a, b in everyone:
            to_hc, to_b = divmod(((h * 2 + c) * nb + b) ^ offset, nb)
            sends.append((place(j, h, c, a, b), place(j, to_hc // 2, to_hc % 2, a, to_b)))
        return lax.ppermute(x, AXES, sends)

    core_bit = nb
    far_bits = [1 << n for n in range(group.bit_length() - 1) if (1 << n) != core_bit]

    ff = w_up.shape[1]
    unit = ff // (2 * jh)
    up_split = w_up.reshape(part, jh, 2, unit)
    up_mine = lax.dynamic_index_in_dim(up_split, ic, 2, keepdims=False)
    up_other = flip(lax.dynamic_index_in_dim(up_split, 1 - ic, 2, keepdims=False), "c", 1)
    up_rows = jnp.stack(
        [jnp.where(ic == 0, up_mine, up_other), jnp.where(ic == 0, up_other, up_mine)]
    )
    n_up, n_down = 2 * part * jh * unit // model, w_down.shape[0]
    views = unit == model and part % 32 == 0 and n_up == n_down
    up_rows = up_rows.transpose(2, 0, 1, 3).reshape(n_up, model)
    cut, cut_up, cut_out = n_down // 2, n_up // 2, part // 2

    line_stages = stages_of(("a",))
    low_axes, high_axes = ("b", "h", "j"), ("h", "j", "b")

    def grow(x, came):
        return jnp.concatenate([x, came])

    def grow_all(x, stages):
        for axis, bit in stages:
            x = grow(x, flip(x, axis, bit))
        return x

    first = [up_rows[:cut_up], w_output[:cut_out], up_rows[cut_up:], w_output[cut_out:]]
    first, second = jnp.concatenate(first)[None], w_down[None]

    columns = jnp.stack(
        [w.reshape(part, group, pairs, 128) for w in (w_query, w_key, w_value)], axis=3
    ).reshape(part, group, 3 * width)
    columns = columns.transpose(1, 0, 2)
    columns = lax.all_to_all(columns, ("h", "c", "b"), 0, 0, tiled=True)
    columns = columns.reshape(1, group * part, 3 * width)

    blocks = 2 * group
    index = jnp.arange(blocks, dtype=jnp.int32)
    table = (member ^ (index % group)) * 2 + (parity ^ (index // group))
    positions_of = (parity ^ (index % 2)) * group + (member ^ (index // 2))
    lane, first = together(jnp.arange(128, dtype=jnp.int32), first)
    frequency = jnp.exp(
        (lane % (HEAD_DIM // 2)).astype(F32) * (-2.0 * math.log(10000.0) / HEAD_DIM)
    )
    angles = jnp.arange(length, dtype=jnp.int32).astype(F32)[:, None] * frequency[None, :]
    cosine = jnp.cos(angles)
    sine = jnp.sin(angles) * jnp.where((lane // (HEAD_DIM // 2)) % 2 == 0, -1.0, 1.0)[None, :]

    vectors, columns = together(
        jnp.stack(
            [attn_in_gain, attn_in_bias, attn_out_gain, attn_out_bias,
             mlp_in_gain, mlp_in_bias, mlp_out_gain, mlp_out_bias]
        ),
        columns,
    )
    vectors = jnp.broadcast_to(vectors[None], (devices,) + vectors.shape)
    vectors = lax.all_to_all(vectors, AXES, 0, 0, tiled=True)
    vectors = vectors.transpose(1, 0, 2).reshape(8, model).astype(F32)

    def columns_in_order(x):
        x = x[place_in(w_from)].reshape(2, na, nh, 2, nb, part, 3 * width)
        return x.transpose(0, 2, 3, 1, 4, 5, 6).reshape(model, 3 * width)

    own = [regroup(tokens, turn) for turn in range(2)]
    first_came = flip(first, *line_stages[0])
    w_came = flip(columns, *line_stages[0])
    own, first_came, w_came, second, cosine, sine, vectors = together(
        own, first_came, w_came, second, cosine, sine, vectors
    )
    first = grow_all(grow(first, first_came), line_stages[1:])
    wide = cut_up + cut_out
    low_stages, high_stages = stages_of(low_axes), stages_of(high_axes)
    first_low, first_high = first[:, :wide], first[:, wide:]
    columns = grow_all(grow(columns, w_came), line_stages[1:-1])
    second_came, w_came = flip(second, *line_stages[0]), flip(columns, *line_stages[-1])
    high_came = flip(first_high, *high_stages[0])
    pieces = {0: jnp.stack(own)}
    for bit in far_bits:
        for offset in list(pieces):
            pieces[offset ^ bit] = by_offset(pieces[offset], bit)
    pieces[core_bit] = by_offset(pieces[0], core_bit)
    pieces, high_came, second_came, w_came = together(pieces, high_came, second_came, w_came)
    second = grow_all(grow(second, second_came), line_stages[1:-1])
    columns = grow(columns, w_came)

    w_came = flip(columns, "j", 1)
    w_from = source_of(("a", "j"), ("j", "a"))
    low_came, second_came = flip(first_low, *low_stages[0]), flip(second, *line_stages[-1])
    for offset in range(1, group):
        if not offset & core_bit:
            pieces[offset ^ core_bit] = by_offset(pieces[offset], core_bit)
    pieces, w_came, low_came, second_came = together(pieces, w_came, low_came, second_came)
    if views:
        w_heads, w_shape = [columns, w_came], (na, nb, part)
    else:
        w_heads, w_shape = [columns_in_order(grow(columns, w_came))], None
    first_low = grow_all(grow(first_low, low_came), low_stages[1:-1])
    first_high = grow_all(grow(first_high, high_came), high_stages[1:-1])
    second = grow(second, second_came)
    pieces, first_low, first_high, second = together(pieces, first_low, first_high, second)
    low_came, high_came = flip(first_low, *low_stages[-1]), flip(first_high, *high_stages[-1])
    seconds = [second]
    if views:
        seconds += [flip(second, "b", 1), flip(second, "j", 1)]
    normed, queries, keys, values, w_heads = qkv_call(
        positions_of, w_from, [pieces[d] for d in range(group)], w_heads, vectors,
        cosine, sine, w_shape,
    )
    grad_in = [regroup(cotangent, 0)]
    attended, lse = attention_forward(table, queries, keys, values, rows)
    attended, lse, low_came, high_came, grad_in, cotangent = together(
        attended, lse, low_came, high_came, grad_in, cotangent
    )
    first_low, first_high = [first_low, low_came], [first_high, high_came]
    if views:
        near = source_of(("a",))
        over_b, over_j = (near // nb) * nb + (near % nb ^ 1), near ^ (na * nb)
        over_both = over_b ^ (na * nb)
        down_from = jnp.concatenate([near, over_b, over_j, over_both])
    else:
        seconds = [grow_all(second, stages_of(("h", "j", "b")))]
        down_from = source_of(("a", "h", "j", "b"))
    low_from, high_from = (source_of(("a",) + axes) for axes in (low_axes, high_axes))

    def exchange(x):
        return [x[0]] + [by_offset(x[d], d) for d in range(1, group)]

    order = jnp.stack([low_from, high_from, down_from])
    low_at, high_at = place_in(low_from), place_in(high_from)
    core_block = jnp.arange(2 * jh, dtype=jnp.int32)
    if views:
        mine = pick(first_low + first_high, cut_out)
        out_weights = [mine, flip(mine, "c", 1)]
    else:
        mine = jnp.concatenate(
            [jnp.concatenate([x[:, cut_up:] for x in pair]) for pair in (first_low, first_high)],
            axis=1,
        )
        mine = jnp.concatenate([mine[:, :cut_out][low_at], mine[:, cut_out:][high_at]], axis=1)
        mine = mine.reshape(jh, na * nb * part, model)
        other = flip(mine, "c", 1)
        w_out = jnp.where(
            ic == 0, jnp.stack([mine, other], axis=1), jnp.stack([other, mine], axis=1)
        ).reshape(group, width, model)
        out_weights = [w_out[member ^ jnp.arange(group)]]
    places = member ^ ((core_block % jh) * 2 + (ic ^ (core_block // jh)))
    mixed = exchange(attended.reshape(group, 2 * rows, width))
    projected, residual, mlp_mine, w_out = out_projection(
        order, places, mixed, own, vectors, out_weights, views
    )
    mlp_rows = [mlp_mine, flip(mlp_mine, "c", 1)]
    if views:
        mlp_rows, seconds = together(mlp_rows, seconds)
        seconds += [flip(seconds[1][: na // 2], "j", 1), flip(seconds[2][na // 2 :], "b", 1)]
    if views:
        tables = [order]
        up_weights = [(x, 2 * part) for x in first_low + first_high]
    else:
        tables = []
        up = [jnp.concatenate([x[:, :cut_up] for x in pair]) for pair in (first_low, first_high)]
        up = jnp.concatenate([up[0][low_at], up[1][high_at]], axis=1)
        up = up.reshape(jh, na, nb, jh, 2, part, unit)
        up_weights = [(up.transpose(0, 4, 1, 2, 5, 3, 6).reshape(model, jh * unit), model)]
    grad_in.append(regroup(cotangent, 1))
    pre_act, activated = mlp_call(
        mlp_up_kernel, "mlp_up", 11, mlp_rows, [], up_weights, tables,
        [(model, jh * unit)], 2, False,
    )
    activated, grad_in, seconds = together(activated, grad_in, seconds)
    if views:
        down_weights = [(x, n_down) for x in seconds]
    else:
        down = seconds[0][place_in(down_from)]
        down_weights = [(down.reshape(jh * unit, model), jh * unit)]
    branch, branch_other = mlp_call(
        mlp_down_kernel, "mlp_down", 9, [], [activated], down_weights, tables,
        [(jh * unit, model)], 0, True,
    )
    block_loose, branch_mine, mo_sums = row_call(
        middle_kernel, "middle", 3, rows,
        [branch, flip(branch_other, "c", 1), residual], grad_in, [vectors],
        [(model, BF), (model, BF)],
    )
    branch_rows = [branch_mine, flip(branch_mine, "c", 1)]

    def sends(x, axis, dim):
        return scatter_sends(x, axis, dim, 1) if lax.axis_size(axis) > 1 else (x, None)

    def send(pair, axis):
        return None if pair[1] is None else flip(pair[1], axis, 1)

    def added(pair, came, shape):
        return (pair[0] if came is None else join(pair[0], came)).reshape(shape)

    def sends_of(arrays, axis, dim):
        kept, given = zip(*[sends(x, axis, dim) for x in arrays])
        return list(kept), None if given[0] is None else jnp.concatenate(given, axis=-1)

    def added_of(kept, came, shape):
        out, start = [], 0
        for x in kept:
            width = x.shape[-1]
            if came is not None:
                x = join(x, came[..., start : start + width])
            out.append(x.reshape(shape + (width,)))
            start += width
        return out

    down_part = dot(activated, jnp.concatenate(branch_rows), TN).astype(BF)
    down_part = down_part.reshape(2, nh, na, nb, n_down, model)
    low_sends = sends(down_part[..., :cut, :], "b", 3)
    high_sends = sends(down_part[..., cut:, :], "j", 0)
    branch_rows, low_sends, high_sends, block_loose = together(
        branch_rows, low_sends, high_sends, block_loose
    )
    half_b, halves_b = (ib if nb > 1 else None), min(nb, 2)
    low_bit, next_bit = ia % 2, (ia // 2) % 2
    low_came, high_came = send(low_sends, "b"), send(high_sends, "j")
    block_came = [restore(block_loose[:rows], 0), restore(block_loose[rows:], 1)]
    pre_low, grad_mlp, grad_other = mlp_call(
        mlp_backward_kernel, "mlp_backward", 20, branch_rows, [pre_act],
        up_weights + down_weights, tables, [(model, jh * unit), (jh * unit, model)], 1, True,
    )
    pre_low, grad_mlp, grad_other, low_came, high_came, block_came = together(
        pre_low, grad_mlp, grad_other, low_came, high_came, block_came
    )
    grad_other = flip(grad_other, "c", 1)
    low_sends, high_sends = relay(
        [
            (ij, (1, 2, nh * na * cut), [(low_sends[0], low_came, 0)]),
            (half_b, (nh * na, halves_b, cut), [(high_sends[0], high_came, 0)]),
        ],
        views,
    )
    grad_mlp, grad_other, low_sends, high_sends = together(
        grad_mlp, grad_other, low_sends, high_sends
    )
    low_came, high_came = send(low_sends, "j"), send(high_sends, "b")
    grad_residual, projected_low, *attended_low, turn_sums = row_call(
        functools.partial(turn_kernel, group=group), "turn", 6, rows,
        [grad_mlp, grad_other, residual, projected], grad_in, [vectors, w_out],
        [(model, F32), (model, BF)] + [(width, BF)] * group, limit=60,
    )
    attended_low, projected_low, pre_low, low_came, high_came, block_came = together(
        attended_low, projected_low, pre_low, low_came, high_came, block_came
    )
    grad_heads = exchange(attended_low)
    grad_heads[1], pre_low = together(grad_heads[1], pre_low)
    grad_heads = jnp.stack(grad_heads).reshape(blocks, rows, width)
    down_pieces = [(low_sends[0][0], low_came, 0), (high_sends[0][0], high_came, 0)]
    (down_sends,) = relay([(low_bit, (na // 2, 2, cut), down_pieces)], views)
    up_part = dot(jnp.concatenate(mlp_rows), pre_low, TN).astype(BF)
    up_part = up_part.reshape(2, nh, 2, na, nb, part, jh * unit)
    grad_out = jnp.stack([dot(mixed[d], projected_low, TN).astype(BF) for d in range(group)])
    grad_out = jnp.stack(
        [lax.dynamic_index_in_dim(grad_out, member ^ m, 0, keepdims=False) for m in range(group)]
    ).reshape(2, nh, 2, na, nb, part, model)
    grad_out = scatter_axis(grad_out, "c", 2)
    low_sends = sends_of([up_part[:, :, 0], grad_out[..., : model // 2]], "j", 0)
    high_sends = sends_of([up_part[:, :, 1], grad_out[..., model // 2 :]], "b", 3)
    grad_heads, down_sends, low_sends, high_sends = together(
        grad_heads, down_sends, low_sends, high_sends
    )

    def backward(pair, grads):
        return attention_backward(
            table, pair, queries, keys, values, attended, grads, lse, cosine, sine
        )

    units = jh * unit
    low_came, high_came = send(low_sends, "j"), send(high_sends, "b")
    down_came = send(down_sends, "a")
    grad_pairs = [backward(0, grad_heads)]
    weight_pairs = [dot(normed, grad_pairs[0], TN).astype(BF)]
    weight_pairs, down_came, low_came, high_came = together(
        weight_pairs, down_came, low_came, high_came
    )
    low_pieces = [(low_sends[0][0], low_came, 0), (low_sends[0][1], low_came, units)]
    high_pieces = [(high_sends[0][0], high_came, 0), (high_sends[0][1], high_came, units)]
    down_pieces = [(down_sends[0][0], down_came, 0), (down_sends[0][1], down_came, model)]
    low_sends, high_sends, down_sends = relay(
        [
            (half_b, (na, halves_b, part), low_pieces),
            (ij, (1, 2, nh * na * part), high_pieces),
            (next_bit, (na // 4, 2, cut), down_pieces),
        ],
        views,
    )
    heads_in = [
        lax.all_to_all(weight_pairs[0].reshape(devices, part, 384), AXES, 0, 0, tiled=True)
    ]
    if pairs > 1:
        grad_heads, down_sends, low_sends, high_sends, weight_pairs = together(
            grad_heads, down_sends, low_sends, high_sends, weight_pairs
        )
    down_came, low_came = flip(down_sends[1], "a", 2), send(low_sends, "b")
    high_came = send(high_sends, "j")
    if pairs > 1:
        grad_pairs.append(backward(1, grad_heads))
    grads_give = [d for d in range(group) if d & core_bit]
    block_order = [2 * d + r for d in grads_give for r in range(2)]
    block_order += [2 * (d ^ core_bit) + r for d in grads_give for r in range(2)]
    grad_pairs, down_came, low_came, high_came, heads_in = together(
        grad_pairs, down_came, low_came, high_came, heads_in
    )
    rest_pieces = [
        (x, came, at)
        for (kept, _), came in ((low_sends, low_came), (high_sends, high_came))
        for x, at in zip(kept, (0, units))
    ]
    (rest_sends,) = relay([(low_bit, (na // 2, 2, part), rest_pieces)], views)
    grad_pairs, rest_sends = together(grad_pairs, rest_sends)
    rest_came = send(rest_sends, "a")
    grad_give, grad_keep = input_grad(
        positions_of[jnp.array(block_order, jnp.int32)], grad_pairs, w_heads, rows
    )
    grad_give, grad_keep, grad_pairs = together(grad_give, grad_keep, grad_pairs)
    give_came = by_offset(grad_give, core_bit)
    give_came, grad_keep = together(give_came, grad_keep)

    grad_keep = join(grad_keep, give_came)
    sums = {
        d ^ core_bit: [grad_keep[2 * n + r] for r in range(2)] for n, d in enumerate(grads_give)
    }
    for bit in far_bits[:-1]:
        for d in [d for d in sums if d & bit]:
            gone = sums.pop(d)
            for r in range(2):
                sums[d ^ bit][r] = join(sums[d ^ bit][r], by_offset(gone[r], bit))
    sums, grad_pairs = together(sums, grad_pairs)
    if far_bits:
        final = [by_offset(x, far_bits[-1]) for x in sums[far_bits[-1]]]
    weight_pairs = [dot(normed, x, TN).astype(BF) for x in grad_pairs[1:]]
    weight_pairs, rest_came = together(weight_pairs, rest_came)
    for x in weight_pairs:
        heads_in.append(lax.all_to_all(x.reshape(devices, part, 384), AXES, 0, 0, tiled=True))
    starts = (0, units, units + model // 2, 2 * units + model // 2)
    rest_pieces = [(x, rest_came, at) for x, at in zip(rest_sends[0], starts)]
    (rest_sends,) = relay([(next_bit, (na // 4, 2, part), rest_pieces)], views)
    rest_came = flip(rest_sends[1], "a", 2)
    if far_bits:
        final[0], down_came, block_came = together(final[0], down_came, block_came)
        final[1], rest_came = together(final[1], rest_came)
    down_parts = added_of(down_sends[0], down_came, (na // 4, cut))
    down_part = jnp.concatenate([scatter_axis(x, "a", 0, 4) for x in down_parts])
    block_out = ordered(*block_came)

    small, totals = mo_sums + turn_sums, []
    for r in range(2):
        parts = [sums[0][r]] + ([final[r]] if far_bits else [])
        total, sums_in = row_call(
            last_kernel, "last", 2, rows,
            [own[r], (grad_residual, r)] + parts, [], [vectors],
            [(model, BF)],
        )
        small = small + sums_in
        if r == 0 and far_bits:
            total, final[1] = together(total, final[1])
        totals.append(total)
    grad_tokens = [restore(total, r) for r, total in enumerate(totals)]
    rest_parts = added_of(rest_sends[0], rest_came, (na // 4, part))
    low_up, low_out, high_up, high_out = (scatter_axis(x, "a", 0, 4) for x in rest_parts)
    small = small.reshape(8, 2, nh, 2, na, nb, part).transpose(3, 5, 1, 2, 4, 0, 6)
    for axis in ("c", "b", "j", "h", "a"):
        small = scatter_axis(small, axis, 0, kind=F32)
    grad_tokens = ordered(*grad_tokens)

    def spread(m):
        hc, b = divmod(m, nb)
        return [place(j, hc // 2, hc % 2, a, b) for j in range(2) for a in range(na)]

    g_query, g_key, g_value = head_sum(heads_in, group, spread)
    g_down, g_out = down_part.astype(F32), jnp.concatenate([low_out, high_out], axis=1).astype(F32)
    up_part = jnp.stack([low_up, high_up])
    up_keep = lax.dynamic_index_in_dim(up_part, ic, 0, keepdims=False).reshape(part, jh, unit)
    up_give = lax.dynamic_index_in_dim(up_part, 1 - ic, 0, keepdims=False)
    up_come = flip(up_give, "c", 1).reshape(part, jh, unit)
    g_up = jnp.where(
        ic == 0, jnp.stack([up_keep, up_come], axis=2), jnp.stack([up_come, up_keep], axis=2)
    ).reshape(part, ff).astype(F32)

    return (
        block_out, grad_tokens, g_query, g_key, g_value, g_out, g_up, g_down,
        small[0], small[1], small[2], small[3], small[4], small[5], small[6], small[7],
    )


def solution(mesh):
    fsdp, seq = mesh.shape["fsdp"], mesh.shape["seq"]
    inner = Mesh(mesh.devices.reshape(2, fsdp // 4, 2, fsdp, seq // fsdp), AXES)
    lead, line = ("j", "h", "c"), ("a", "b")
    acts = P(lead, line, None)
    weights = P(lead + line, None)
    vector = P(lead + line)
    return jax.shard_map(
        body,
        mesh=inner,
        in_specs=(acts,) * 2 + (weights,) * 6 + (vector,) * 8,
        out_specs=(acts,) * 2 + (weights,) * 6 + (vector,) * 8,
        check_vma=False,
    )
```
